32 devices in a mesh: dp: 8 (over z, core), row: 2 (over x), col: 2 (over y).
Axes of the slice: x: 2, y: 2, z: 4, core: 2. Of those that a mesh axis runs over, the one named last changes fastest.
Arguments:
- tokens: bfloat16 [40960, 1024], P(('dp', 'row'), 'col'), may hold values from -8 to 8
- key_mask: int32 [128, 256], P(('dp', 'col')), may hold values from 0 to 1, as said below
- first_gain: float32 [1024], P('col'), may hold values from 0.5 to 1.5
- first_shift: float32 [1024], P('col'), may hold values from -1 to 1
- qkv_weight: float32 [3, 16, 64, 1024], P(None, 'row', 'dp', 'col'), may hold values from -0.1875 to 0.1875
- qkv_bias: float32 [2, 16, 64], P(None, 'row', 'dp'), may hold values from -1 to 1
- out_weight: float32 [16, 64, 1024], P('row', 'dp', 'col'), may hold values from -0.75 to 0.75
- out_bias: float32 [1024], P('col'), may hold values from -1 to 1
- second_gain: float32 [1024], P('col'), may hold values from 0.5 to 1.5
- second_shift: float32 [1024], P('col'), may hold values from -1 to 1
- up_weight: float32 [4096, 1024], P(('dp', 'row'), 'col')
- up_bias: float32 [4096], P(('dp', 'row')), may hold values from -1 to 1
- down_weight: float32 [4096, 1024], P(('dp', 'row'), 'col'), may hold values from -0.09375 to 0.09375
- down_bias: float32 [1024], P('col'), may hold values from -1 to 1
- cotangent: bfloat16 [40960, 1024], P(('dp', 'row'), 'col'), may hold values from -6 to 6
Outputs:
- activations: bfloat16 [40960, 1024], P(('dp', 'row'), 'col')
- token_grad: float32 [40960, 1024], P(('dp', 'row'), 'col')
- first_gain_grad: float32 [1024], P('col')
- first_shift_grad: float32 [1024], P('col')
- qkv_weight_grad: float32 [3, 16, 64, 1024], P(None, 'row', 'dp', 'col')
- qkv_bias_grad: float32 [2, 16, 64], P(None, 'row', 'dp')
- out_weight_grad: float32 [16, 64, 1024], P('row', 'dp', 'col')
- out_bias_grad: float32 [1024], P('col')
- second_gain_grad: float32 [1024], P('col')
- second_shift_grad: float32 [1024], P('col')
- up_weight_grad: float32 [4096, 1024], P(('dp', 'row'), 'col')
- up_bias_grad: float32 [4096], P(('dp', 'row'))
- down_weight_grad: float32 [4096, 1024], P(('dp', 'row'), 'col')
- down_bias_grad: float32 [1024], P('col')
The draws below stay inside these ranges and needn't reach their ends.
Inputs may be any that keep to these rules, and one draw needn't show every extreme that they name: `key_mask`: 1 marks a visible image token and 0 a masked one; every sequence masks some of its 256 image tokens and shows most of them; buffer tokens are always visible.
All inputs are finite; a program needn't handle non-finite values.
Results may differ from the reference program's by a relative error of at most 0.025.
Values may be sent and summed in bfloat16 or wider, within the bound.
No kernel may reach another device: no remote copies, remote signals or barrier semaphores. Data moves between devices by JAX's collectives and lax.ppermute only.
A program may use at most 320 MiB of HBM per device.

```python
import jax
import jax.numpy as jnp
from jax import lax

D = 1024
H = 16
HD = 64
F = 4096
BUF = 64
IMG = 256
LEN = 320
SEQ_DEV = 8
SEQS = 128
TOKENS = 40960


def draw_tokens(key, part):
    first = jax.random.fold_in(key, 0)
    slope = jnp.exp(jnp.linspace(-0.55, 0.55, D)).astype(jnp.float32)
    values = jax.random.normal(first, (TOKENS, D), jnp.float32) * slope[None, :]
    return jnp.clip(values, -8.0, 8.0).astype(jnp.bfloat16)


def draw_key_mask(key, part):
    first, second = jax.random.split(key, 2)
    masked_count = jax.random.randint(first, (SEQS, 1), IMG // 10, 2 * IMG // 5 + 1)
    streams = jax.random.split(second, SEQS)
    orders = jax.vmap(lambda stream: jax.random.permutation(stream, IMG))(streams)
    return jnp.where(orders < masked_count, 0, 1).astype(jnp.int32)


def draw_up_weight(key, part):
    first, second = jax.random.split(jax.random.fold_in(key, 71), 2)
    scale = jnp.float32(D) ** (-0.5)
    profile = jnp.exp(jnp.linspace(-0.55, 0.55, D)).astype(jnp.float32)
    base = jax.random.normal(first, (F, D), jnp.float32)
    factor = jax.random.normal(second, (F, 1), jnp.float32)
    return (base + 0.7 * factor * profile[None, :]) * scale


def levels(stream_key, dims, cuts, low, top_value):
    level = 1.0
    for dim, blocks in cuts:
        steps = jax.random.uniform(jax.random.fold_in(jax.random.fold_in(stream_key, 6), dim), (blocks,), jnp.float32, low / len(cuts), top_value / len(cuts))
        level = level * jnp.repeat(jnp.exp(steps), dims[dim] // blocks).reshape((-1,) + (1,) * (len(dims) - 1 - dim))
    return level


def bell_draw(key, shape, scale, reach, shards=(), held_as=jnp.bfloat16):
    drawn = scale * jax.random.normal(key, shape, jnp.float32)
    if shards:
        drawn = drawn * levels(key, shape, shards, -0.22, 0.18)
    return jnp.clip(drawn, -reach, reach).astype(held_as)


def setup_inputs(seed: int = 0) -> dict:
    key_of = jax.random.split(jax.random.key(seed), 16)
    tokens = draw_tokens(jax.random.fold_in(key_of[15], 71), 0)
    key_mask = draw_key_mask(jax.random.fold_in(key_of[15], 71), 0)
    first_gain = jnp.clip(1.0 + 0.1 * jax.random.normal(key_of[2], (D,), jnp.float32), 0.5, 1.5)
    first_shift = bell_draw(key_of[3], (D,), 0.2, 1.0, ((0, 2),), jnp.float32)
    qkv_weight = bell_draw(key_of[4], (3, H, HD, D), D ** -0.5, 0.1875, ((1, 2), (2, 8), (3, 2)), jnp.float32)
    qkv_bias = bell_draw(key_of[5], (2, H, HD), 0.2, 1.0, ((1, 2), (2, 8)), jnp.float32)
    out_weight = bell_draw(key_of[6], (H, HD, D), (D // 16) ** -0.5, 0.75, ((0, 2), (1, 8), (2, 2)), jnp.float32)
    out_bias = bell_draw(key_of[7], (D,), 0.2, 1.0, ((0, 2),), jnp.float32)
    second_gain = jnp.clip(1.0 + 0.1 * jax.random.normal(key_of[8], (D,), jnp.float32), 0.5, 1.5)
    second_shift = bell_draw(key_of[9], (D,), 0.2, 1.0, ((0, 2),), jnp.float32)
    up_weight = draw_up_weight(jax.random.fold_in(key_of[15], 71), 0)
    up_bias = bell_draw(key_of[11], (F,), 0.2, 1.0, ((0, 16),), jnp.float32)
    down_weight = bell_draw(key_of[12], (F, D), F ** -0.5, 0.09375, ((0, 16), (1, 2)), jnp.float32)
    down_bias = bell_draw(key_of[13], (D,), 0.2, 1.0, ((0, 2),), jnp.float32)
    cotangent = bell_draw(key_of[14], (TOKENS, D), 1.0, 6.0, ((0, 16), (1, 2)))
    return dict(tokens=tokens, key_mask=key_mask, first_gain=first_gain, first_shift=first_shift, qkv_weight=qkv_weight, qkv_bias=qkv_bias, out_weight=out_weight, out_bias=out_bias, second_gain=second_gain, second_shift=second_shift, up_weight=up_weight, up_bias=up_bias, down_weight=down_weight, down_bias=down_bias, cotangent=cotangent)


@jax.custom_vjp
def low(v):
    return lax.optimization_barrier(v.astype(jnp.bfloat16)).astype(jnp.float32)

@jax.custom_vjp
def low_back(v):
    return v

def low_keep(v):
    return (low(v), None)

def low_pass(kept, grad):
    return (grad,)

def back_keep(v):
    return (v, None)

def back_low(kept, grad):
    return (low(grad),)
low.defvjp(low_keep, low_pass)
low_back.defvjp(back_keep, back_low)
highest = lax.Precision.HIGHEST

def layer_norm(values, gain, shift):
    center = lax.optimization_barrier(jnp.mean(values, axis=-1, keepdims=True))
    centered = values - center
    spread = lax.optimization_barrier(jnp.mean(centered * centered, axis=-1, keepdims=True))
    return centered * lax.rsqrt(spread + 1e-06) * gain + shift

def forward(inputs, visible, params):
    first_gain, first_shift, qkv_weight, qkv_bias, out_weight, out_bias, second_gain, second_shift, up_weight, up_bias, down_weight, down_bias = params
    groups = visible.shape[0]
    normed = low(layer_norm(inputs, first_gain, first_shift))
    weights = low(qkv_weight)
    biases = low(qkv_bias)
    projected = jnp.einsum('td,ihed->ithe', normed, weights, precision=highest)
    query = low(low_back(projected[0] + biases[0])).reshape(groups, LEN, H, HD)
    keyset = low(low_back(projected[1])).reshape(groups, LEN, H, HD)
    valset = low(low_back(projected[2] + biases[1])).reshape(groups, LEN, H, HD)
    scores = low_back(jnp.einsum('sqhe,skhe->shqk', query, keyset, precision=highest) * 0.125)
    allowed = visible[:, None, None, :] > 0
    scores = jnp.where(allowed, scores, -1000000000.0)
    top = lax.optimization_barrier(jnp.max(scores, axis=-1, keepdims=True))
    expanded = jnp.exp(scores - top)
    probs = expanded / lax.optimization_barrier(jnp.sum(expanded, axis=-1, keepdims=True))
    attended = jnp.einsum('shqk,skhe->sqhe', low(probs), valset, precision=highest)
    attended = low(low_back(attended)).reshape(groups * LEN, H, HD)
    branch = low_back(jnp.einsum('the,hed->td', attended, low(out_weight), precision=highest) + out_bias)
    middle = inputs + branch
    normed_two = low(layer_norm(middle, second_gain, second_shift))
    upward = low_back(jnp.dot(normed_two, low(up_weight).T, precision=highest) + low(up_bias))
    hidden = low(jax.nn.gelu(upward, approximate=False))
    branch_two = low_back(jnp.dot(hidden, low(down_weight), precision=highest) + down_bias)
    return middle + branch_two

def reference(tokens, key_mask, first_gain, first_shift, qkv_weight, qkv_bias, out_weight, out_bias, second_gain, second_shift, up_weight, up_bias, down_weight, down_bias, cotangent):
    params = (first_gain.astype(jnp.float32), first_shift.astype(jnp.float32), qkv_weight.astype(jnp.float32), qkv_bias.astype(jnp.float32), out_weight.astype(jnp.float32), out_bias.astype(jnp.float32), second_gain.astype(jnp.float32), second_shift.astype(jnp.float32), up_weight.astype(jnp.float32), up_bias.astype(jnp.float32), down_weight.astype(jnp.float32), down_bias.astype(jnp.float32))
    seq_count = key_mask.shape[0]
    groups = seq_count // SEQ_DEV
    buffer_on = jnp.ones((seq_count, BUF), jnp.int32)
    visible = jnp.concatenate([buffer_on, key_mask.astype(jnp.int32)], axis=1).reshape(groups, SEQ_DEV, LEN)
    inputs = tokens.astype(jnp.float32).reshape(groups, SEQ_DEV * LEN, D)
    pulled = cotangent.astype(jnp.float32).reshape(groups, SEQ_DEV * LEN, D)

    def step(totals, item):
        group_in, group_vis, group_cot = item
        outputs, pull = jax.vjp(lambda values, weights: forward(values, group_vis, weights), group_in, params)
        input_grad, param_grads = pull(group_cot)
        totals = jax.tree.map(lambda first, second: first + second, totals, param_grads)
        return (totals, (outputs.astype(jnp.bfloat16), input_grad))
    zeros = jax.tree.map(jnp.zeros_like, params)
    totals, (outputs, grads) = lax.scan(step, zeros, (inputs, visible, pulled))
    return (outputs.reshape(-1, D), grads.reshape(-1, D), totals[0], totals[1], totals[2], totals[3], totals[4], totals[5], totals[6], totals[7], totals[8], totals[9], totals[10], totals[11])
```

```python
import jax
import jax.numpy as jnp
from jax import lax
from jax.sharding import Mesh, PartitionSpec as P

HD = 64
BUF = 64
LEN = 320
attn_scale = 0.125
masked_fill = -1000000000.0
norm_epsilon = 1e-06
bf16 = jnp.bfloat16
f32 = jnp.float32


def shift(values, axis, size, step):
    return lax.ppermute(values, axis, [(i, (i + step) % size) for i in range(size)])


def contract_last(left, right):
    return lax.dot_general(left, right, (((1,), (1,)), ((), ())), preferred_element_type=f32)


def contract_first(left, right):
    return lax.dot_general(left, right, (((0,), (0,)), ((), ())), preferred_element_type=f32)


def make_local(nz, ncore, nrow, ncol):
    def axis_in(values, axis, size):
        return [values] + [shift(values, axis, size, k) for k in range(1, size)]

    def gather(shard):
        along_z = jnp.stack(axis_in(shard, "z", nz))
        along_col = jnp.stack(axis_in(along_z, "col", ncol))
        along_row = jnp.stack(axis_in(along_col, "row", nrow))
        return jnp.stack(axis_in(along_row, "core", ncore))

    def axis_out(parts, axis, size):
        total = parts[0].astype(f32)
        for k in range(1, size):
            total = total + shift(parts[k].astype(bf16), axis, size, -k).astype(f32)
        return total

    def scatter(grads):
        one = axis_out(grads, "core", ncore).astype(bf16)
        two = axis_out(one, "row", nrow).astype(bf16)
        three = axis_out(two, "col", ncol).astype(bf16)
        return axis_out(three, "z", nz)

    def tokens_in(values):
        rows = values.shape[0] // ncol
        here = lax.axis_index("col")
        parts = [lax.dynamic_slice_in_dim(values, here * rows, rows, 0)]
        for k in range(1, ncol):
            block = lax.dynamic_slice_in_dim(values, ((here + k) % ncol) * rows, rows, 0)
            parts.append(shift(block, "col", ncol, k))
        return jnp.concatenate(parts, axis=1)

    def tokens_out(values, dtype):
        rows = values.shape[0]
        width = values.shape[1] // ncol
        here = lax.axis_index("col")
        result = jnp.zeros((rows * ncol, width), dtype)
        result = lax.dynamic_update_slice_in_dim(result, values[:, :width].astype(dtype), here * rows, 0)
        for k in range(1, ncol):
            block = shift(values[:, k * width : (k + 1) * width].astype(bf16), "col", ncol, -k)
            result = lax.dynamic_update_slice_in_dim(
                result, block.astype(dtype), ((here + k) % ncol) * rows, 0
            )
        return result

    def features(vector):
        return jnp.concatenate(axis_in(vector, "col", ncol))

    def norm_forward(values, gain, first_shift):
        center = jnp.mean(values, axis=1, keepdims=True)
        centered = values - center
        spread = jnp.mean(centered * centered, axis=1, keepdims=True)
        inverse = lax.rsqrt(spread + norm_epsilon)
        unit = centered * inverse
        return unit * gain + first_shift, unit, inverse

    def norm_backward(grad, gain, unit, inverse):
        scaled = grad * gain
        total = jnp.mean(scaled, axis=1, keepdims=True)
        paired = jnp.mean(scaled * unit, axis=1, keepdims=True)
        return inverse * (scaled - total - unit * paired)

    def local(
        tokens,
        key_mask,
        first_gain,
        first_shift,
        qkv_weight,
        qkv_bias,
        out_weight,
        out_bias,
        second_gain,
        second_shift,
        up_weight,
        up_bias,
        down_weight,
        down_bias,
        cotangent,
    ):
        count = tokens.shape[0] // ncol
        seqs = count // LEN
        heads_part, hd_part, width = out_weight.shape
        heads = heads_part * nrow
        hidden_part = up_weight.shape[0]
        dim = width * ncol
        hidden_units = hidden_part * nrow * nz * ncore

        inputs = tokens_in(tokens).astype(f32)
        qkv_all = gather(qkv_weight.astype(bf16))
        small = jnp.concatenate([qkv_bias.reshape(-1), up_bias]).astype(bf16)
        vectors = jnp.stack([first_gain, first_shift, second_gain, second_shift, out_bias, down_bias])
        vectors = jnp.concatenate(axis_in(vectors, "col", ncol), axis=1)
        gain_one, shift_one, gain_two, shift_two, out_offset, down_offset = [vectors[i : i + 1] for i in range(6)]
        small_z = jnp.stack(axis_in(small, "z", nz))
        small_row = jnp.stack(axis_in(small_z, "row", nrow))
        small_all = jnp.stack(axis_in(small_row, "core", ncore)).astype(f32)
        qkv_count = qkv_bias.size
        qkv_offset = small_all[..., :qkv_count].reshape(ncore, nrow, nz, 2, heads_part, hd_part)
        qkv_offset = jnp.transpose(qkv_offset, (3, 1, 4, 0, 2, 5)).reshape(2, 1, heads * HD)
        up_offset = small_all[..., qkv_count:].reshape(1, hidden_units)
        masks = jnp.zeros((ncol,) + key_mask.shape, key_mask.dtype)
        here = lax.axis_index("col")
        for k, part in enumerate(axis_in(key_mask, "col", ncol)):
            masks = lax.dynamic_update_slice_in_dim(masks, part[None], (here - k + ncol) % ncol, 0)
        masks = masks.reshape(-1, key_mask.shape[1])
        first_seq = (lax.axis_index("row") * ncol + here) * seqs
        masks = lax.dynamic_slice_in_dim(masks, first_seq, seqs, 0)
        visible = jnp.concatenate([jnp.ones((seqs, BUF), jnp.int32), masks], axis=1) > 0

        qkv_matrix = jnp.transpose(qkv_all, (4, 1, 5, 0, 3, 6, 2, 7)).reshape(3 * heads * HD, dim)
        out_all = gather(out_weight.astype(bf16))
        out_matrix = jnp.transpose(out_all, (1, 4, 0, 3, 5, 2, 6)).reshape(heads * HD, dim)
        up_all = gather(up_weight.astype(bf16))
        up_matrix = jnp.transpose(up_all, (0, 1, 3, 4, 2, 5)).reshape(hidden_units, dim)
        down_all = gather(down_weight.astype(bf16))
        down_matrix = jnp.transpose(down_all, (0, 1, 3, 4, 2, 5)).reshape(hidden_units, dim)
        grad_low = tokens_in(cotangent)

        normed, unit_one, inverse_one = norm_forward(inputs, gain_one, shift_one)
        normed = normed.astype(bf16)
        projected = contract_last(normed, qkv_matrix).reshape(count, 3, heads * HD)
        shape = (seqs, LEN, heads, HD)
        query = (projected[:, 0] + qkv_offset[0]).astype(bf16).reshape(shape)
        keyset = projected[:, 1].astype(bf16).reshape(shape)
        valset = (projected[:, 2] + qkv_offset[1]).astype(bf16).reshape(shape)

        def attend_scores():
            scores = (
                jnp.einsum("sqhe,skhe->shqk", query, keyset, preferred_element_type=f32) * attn_scale
            )
            return jnp.where(visible[:, None, None, :], scores, masked_fill)

        scores = attend_scores()
        top = jnp.max(scores, axis=-1, keepdims=True)
        expanded = jnp.exp(scores - top)
        denominator = jnp.sum(expanded, axis=-1, keepdims=True)
        probs = expanded / denominator
        logsum = top + jnp.log(denominator)
        attended = jnp.einsum(
            "shqk,skhe->sqhe", probs.astype(bf16), valset, preferred_element_type=f32
        ).astype(bf16).reshape(count, heads * HD)
        branch = jnp.dot(attended, out_matrix, preferred_element_type=f32)
        middle = inputs + (branch + out_offset)
        normed_two, unit_two, inverse_two = norm_forward(middle, gain_two, shift_two)
        normed_two = normed_two.astype(bf16)
        upward = contract_last(normed_two, up_matrix) + up_offset
        gelu_value, gelu_pull = jax.vjp(lambda value: jax.nn.gelu(value, approximate=False), upward)
        hidden = gelu_value.astype(bf16)
        branch_two = jnp.dot(hidden, down_matrix, preferred_element_type=f32) + down_offset
        activations = tokens_out(middle + branch_two, bf16)

        grad_out = grad_low.astype(f32)
        down_bias_sum = jnp.sum(grad_out, axis=0)
        hidden_shape = (ncore, nrow, nz, hidden_part, ncol, width)

        def ffn_scatter(grad):
            return scatter(jnp.transpose(grad.reshape(hidden_shape), (0, 1, 4, 2, 3, 5)))

        hidden_grad = contract_last(grad_low, down_matrix)
        down_grad = ffn_scatter(contract_first(hidden, grad_low).astype(bf16))
        upward_grad = gelu_pull(hidden_grad)[0].astype(bf16)
        up_grad = ffn_scatter(contract_first(upward_grad, normed_two).astype(bf16))
        up_bias_sum = jnp.sum(upward_grad, axis=0, dtype=f32)
        normed_two_grad = jnp.dot(upward_grad, up_matrix, preferred_element_type=f32)
        second_gain_sum = jnp.sum(normed_two_grad * unit_two, axis=0)
        second_shift_sum = jnp.sum(normed_two_grad, axis=0)
        middle_grad = grad_out + norm_backward(normed_two_grad, gain_two, unit_two, inverse_two)
        branch_low = middle_grad.astype(bf16)
        out_bias_sum = jnp.sum(branch_low, axis=0, dtype=f32)
        out_grad = contract_first(attended, branch_low).astype(bf16)
        out_grad = out_grad.reshape(nrow, heads_part, ncore, nz, hd_part, ncol, width)
        out_grad = scatter(jnp.transpose(out_grad, (2, 0, 5, 3, 1, 4, 6)))
        attended_grad = contract_last(branch_low, out_matrix).astype(bf16).reshape(shape)
        again = jnp.exp(attend_scores() - logsum)
        value_grad = jnp.einsum(
            "shqk,sqhe->skhe", again.astype(bf16), attended_grad, preferred_element_type=f32
        ).astype(bf16)
        prob_grad = jnp.einsum("sqhe,skhe->shqk", attended_grad, valset, preferred_element_type=f32)
        score_grad = (
            again * (prob_grad - jnp.sum(prob_grad * again, axis=-1, keepdims=True))
        ).astype(bf16)
        query_grad = (
            jnp.einsum("shqk,skhe->sqhe", score_grad, keyset, preferred_element_type=f32) * attn_scale
        ).astype(bf16)
        key_grad = (
            jnp.einsum("shqk,sqhe->skhe", score_grad, query, preferred_element_type=f32) * attn_scale
        ).astype(bf16)
        flat = (count, heads * HD)
        stacked = jnp.concatenate(
            [query_grad.reshape(flat), key_grad.reshape(flat), value_grad.reshape(flat)], axis=1
        )
        qkv_grad = contract_first(stacked, normed).astype(bf16)
        qkv_grad = qkv_grad.reshape(3, nrow, heads_part, ncore, nz, hd_part, ncol, width)
        qkv_grad = scatter(jnp.transpose(qkv_grad, (3, 1, 6, 4, 0, 2, 5, 7)))
        bias_sum = jnp.sum(stacked, axis=0, dtype=f32).reshape(3, nrow, heads_part, ncore, nz, hd_part)
        bias_sum = jnp.stack([bias_sum[0], bias_sum[2]])
        bias_sum = jnp.transpose(bias_sum, (3, 1, 4, 0, 2, 5)).reshape(ncore, nrow, nz, qkv_count)
        normed_grad = jnp.dot(stacked, qkv_matrix, preferred_element_type=f32)
        first_gain_sum = jnp.sum(normed_grad * unit_one, axis=0)
        first_shift_sum = jnp.sum(normed_grad, axis=0)
        token_grad = tokens_out(
            middle_grad + norm_backward(normed_grad, gain_one, unit_one, inverse_one), f32
        )

        def wide_out(parts, axis, size):
            total = parts[0]
            for k in range(1, size):
                total = total + shift(parts[k], axis, size, -k)
            return total

        def wide_all(values, axis, size):
            total = values
            for k in range(1, size):
                total = total + shift(values, axis, size, k)
            return total

        bias_all = jnp.concatenate(
            [bias_sum, up_bias_sum.reshape(ncore, nrow, nz, hidden_part)], axis=-1
        )
        bias_all = wide_out(bias_all, "core", ncore)
        bias_all = wide_out(bias_all, "row", nrow)
        bias_all = wide_all(bias_all, "col", ncol)
        bias_all = wide_out(bias_all, "z", nz)
        qkv_bias_grad = bias_all[:qkv_count].reshape(qkv_bias.shape)
        up_bias_grad = bias_all[qkv_count:]
        sums = jnp.stack(
            [
                first_gain_sum,
                first_shift_sum,
                out_bias_sum,
                second_gain_sum,
                second_shift_sum,
                down_bias_sum,
            ]
        )
        sums = [sums[:, k * width : (k + 1) * width] for k in range(ncol)]
        sums = wide_out(sums, "col", ncol)
        sums = wide_all(sums, "core", ncore)
        sums = wide_all(sums, "row", nrow)
        sums = wide_all(sums, "z", nz)
        return (
            activations,
            token_grad,
            sums[0],
            sums[1],
            qkv_grad,
            qkv_bias_grad,
            out_grad,
            sums[2],
            sums[3],
            sums[4],
            up_grad,
            up_bias_grad,
            down_grad,
            sums[5],
        )

    return local


def solution(mesh):
    devices = mesh.devices
    nz, ncore = devices.shape[0] // 2, 2
    nrow, ncol = devices.shape[1], devices.shape[2]
    fine = Mesh(devices.reshape(nz, ncore, nrow, ncol), ("z", "core", "row", "col"))
    dp = ("z", "core")
    in_specs = (
        P(("z", "core", "row"), "col"),
        P(("z", "core", "col"), None),
        P("col"),
        P("col"),
        P(None, "row", dp, "col"),
        P(None, "row", dp),
        P("row", dp, "col"),
        P("col"),
        P("col"),
        P("col"),
        P(("z", "core", "row"), "col"),
        P(("z", "core", "row")),
        P(("z", "core", "row"), "col"),
        P("col"),
        P(("z", "core", "row"), "col"),
    )
    out_specs = (
        P(("z", "core", "row"), "col"),
        P(("z", "core", "row"), "col"),
        P("col"),
        P("col"),
        P(None, "row", dp, "col"),
        P(None, "row", dp),
        P("row", dp, "col"),
        P("col"),
        P("col"),
        P("col"),
        P(("z", "core", "row"), "col"),
        P(("z", "core", "row")),
        P(("z", "core", "row"), "col"),
        P("col"),
    )
    return jax.shard_map(
        make_local(nz, ncore, nrow, ncol),
        mesh=fine,
        in_specs=in_specs,
        out_specs=out_specs,
        check_vma=False,
    )
```

```python
import functools

import jax
import jax.numpy as jnp
from jax import lax
from jax.experimental import pallas as pl
from jax.experimental.pallas import tpu as pltpu
from jax.sharding import Mesh, PartitionSpec as P

HD = 64
PAIR = 2 * HD
BUF = 64
LEN = 320
masked_fill = -1000000000.0
norm_epsilon = 1e-06
attn_scale = 0.125
exp2_scale = attn_scale * 1.4426950408889634
root_half = 0.7071067811865476
density = 0.3989422804014327
bf16 = jnp.bfloat16
f32 = jnp.float32
MIB = 1 << 20


def shift(values, axis, size, step):
    return lax.ppermute(values, axis, [(i, (i + step) % size) for i in range(size)])


def contract_last(left, right):
    return lax.dot_general(left, right, (((1,), (1,)), ((), ())), preferred_element_type=f32)


def contract_first(left, right):
    return lax.dot_general(left, right, (((0,), (0,)), ((), ())), preferred_element_type=f32)


def matmul(left, right):
    return lax.dot_general(left, right, (((1,), (0,)), ((), ())), preferred_element_type=f32)


def whole(shape):
    return pl.BlockSpec(shape, lambda *_: (0,) * len(shape), pipeline_mode=pl.Buffered(1))


def summed(shape):
    return pl.BlockSpec(shape, lambda *_: (0,) * len(shape))


def call(kernel, grid, in_specs, out_specs, out_shape, flops, moved, name, vmem=48, scratch=()):
    return pl.pallas_call(
        kernel,
        grid=grid,
        in_specs=in_specs,
        out_specs=out_specs,
        out_shape=out_shape,
        scratch_shapes=scratch,
        name=name,
        compiler_params=pltpu.CompilerParams(vmem_limit_bytes=vmem * MIB),
        cost_estimate=pl.CostEstimate(flops=flops, bytes_accessed=moved, transcendentals=0),
    )


def unit_norm(values):
    center = jnp.mean(values, axis=1, keepdims=True)
    centered = values - center
    spread = jnp.mean(centered * centered, axis=1, keepdims=True)
    inverse = lax.rsqrt(spread + norm_epsilon)
    return centered * inverse, inverse


def norm_pull(grad, gain, unit, inverse):
    scaled = grad * gain
    total = jnp.mean(scaled, axis=1, keepdims=True)
    paired = jnp.mean(scaled * unit, axis=1, keepdims=True)
    return inverse * (scaled - total - unit * paired)


def qkv_kernel(x_ref, gain_ref, shift_ref, w_ref, bias_ref, a_ref, out_ref):
    unit, _ = unit_norm(x_ref[...].astype(f32))
    a = (unit * gain_ref[...] + shift_ref[...]).astype(bf16)
    a_ref[...] = a
    for i in range(3):
        value = contract_last(a, w_ref[i])
        if i != 1:
            value = value + bias_ref[i // 2 : i // 2 + 1]
        out_ref[i] = value.astype(bf16)


def split_heads(pair):
    first = lax.broadcasted_iota(jnp.int32, pair.shape, 1) < HD
    zero = jnp.zeros_like(pair)
    return jnp.concatenate([jnp.where(first, pair, zero), jnp.where(first, zero, pair)], axis=0)


def join_heads(both):
    rows = both.shape[0] // 2
    first = lax.broadcasted_iota(jnp.int32, (rows, both.shape[1]), 1) < HD
    return jnp.where(first, both[:rows], both[rows:])


def attend_kernel(qkv_ref, mask_ref, out_ref):
    seen = mask_ref[0] > 0
    scores = contract_last(split_heads(qkv_ref[0]), qkv_ref[1])
    scores = jnp.where(seen, scores, masked_fill / attn_scale)
    top = jnp.max(scores, axis=1, keepdims=True)
    grown = jnp.exp2((scores - top) * exp2_scale)
    total = jnp.sum(grown, axis=1, keepdims=True)
    mixed = matmul(grown.astype(bf16), qkv_ref[2]) / total
    out_ref[...] = join_heads(mixed).astype(bf16)


def attend_pull_kernel(qkv_ref, mask_ref, do_ref, out_ref):
    seen = mask_ref[0] > 0
    both = split_heads(qkv_ref[0])
    keys = qkv_ref[1]
    vals = qkv_ref[2]
    pulled = split_heads(do_ref[...])
    scores = contract_last(keys, both)
    scores = jnp.where(seen, scores, masked_fill / attn_scale)
    top = jnp.max(scores, axis=0, keepdims=True)
    grown = jnp.exp2((scores - top) * exp2_scale)
    probs = grown * (1.0 / jnp.sum(grown, axis=0, keepdims=True))
    prob_grad = contract_last(vals, pulled)
    out_ref[2] = matmul(probs.astype(bf16), pulled).astype(bf16)
    inner = jnp.sum(prob_grad * probs, axis=0, keepdims=True)
    score_grad = (probs * (prob_grad - inner)).astype(bf16)
    out_ref[1] = (matmul(score_grad, both) * attn_scale).astype(bf16)
    query_grad = contract_first(score_grad, keys) * attn_scale
    out_ref[0] = join_heads(query_grad).astype(bf16)


def out_kernel(x_ref, o_ref, w_ref, bias_ref, gain_ref, shift_ref, middle_ref, a_ref):
    middle = x_ref[...].astype(f32) + (matmul(o_ref[...], w_ref[...]) + bias_ref[...])
    middle_ref[...] = middle
    unit, _ = unit_norm(middle)
    a_ref[...] = (unit * gain_ref[...] + shift_ref[...]).astype(bf16)


def up_kernel(ncol, blocks, a_ref, bias_ref, *refs):
    w_refs, (hid_ref, slope_ref) = refs[: blocks * ncol], refs[blocks * ncol :]
    width = a_ref.shape[1] // ncol
    step = w_refs[0].shape[0]
    for b in range(blocks):
        value = bias_ref[:, b * step : (b + 1) * step]
        for c in range(ncol):
            value = value + contract_last(a_ref[:, c * width : (c + 1) * width], w_refs[b * ncol + c][...])
        cdf = 0.5 + 0.5 * lax.erf(value * root_half)
        pdf = jnp.exp(-0.5 * value * value) * density
        hid_ref[:, b * step : (b + 1) * step] = (value * cdf).astype(bf16)
        slope_ref[:, b * step : (b + 1) * step] = (cdf + value * pdf).astype(bf16)


def down_kernel(ncol, blocks, hid_ref, middle_ref, bias_ref, *refs):
    w_refs, (own_ref, other_ref) = refs[: blocks * ncol], refs[blocks * ncol :]
    step, width = w_refs[0].shape
    for c in range(ncol):
        lanes = slice(c * width, (c + 1) * width)
        value = middle_ref[:, lanes] + bias_ref[:, lanes]
        for b in range(blocks):
            value = value + matmul(hid_ref[:, b * step : (b + 1) * step], w_refs[b * ncol + c][...])
        if c == 0:
            own_ref[...] = value.astype(bf16)
        else:
            other_ref[c - 1] = value.astype(bf16)


def hidden_pull_kernel(ncol, blocks, g_ref, slope_ref, *refs):
    w_refs, (du_ref, sum_ref) = refs[: blocks * ncol], refs[blocks * ncol :]
    step, width = w_refs[0].shape

    @pl.when(pl.program_id(0) == 0)
    def _():
        sum_ref[...] = jnp.zeros_like(sum_ref)

    for b in range(blocks):
        rows = slice(b * step, (b + 1) * step)
        value = contract_last(g_ref[:, :width], w_refs[b * ncol][...])
        for c in range(1, ncol):
            value = value + contract_last(g_ref[:, c * width : (c + 1) * width], w_refs[b * ncol + c][...])
        low = (value * slope_ref[:, rows].astype(f32)).astype(bf16)
        du_ref[:, rows] = low
        sum_ref[:, rows] += jnp.sum(low.astype(f32), axis=0, keepdims=True)


def middle_pull_kernel(ncol, blocks, du_ref, middle_ref, g_ref, gain_ref, wo_ref, *refs):
    w_refs, (grad_ref, low_ref, do_ref, sum_ref) = refs[: blocks * ncol], refs[blocks * ncol :]
    step, width = w_refs[0].shape

    @pl.when(pl.program_id(0) == 0)
    def _():
        sum_ref[...] = jnp.zeros_like(sum_ref)

    parts = []
    for c in range(ncol):
        value = matmul(du_ref[:, :step], w_refs[c][...])
        for b in range(1, blocks):
            value = value + matmul(du_ref[:, b * step : (b + 1) * step], w_refs[b * ncol + c][...])
        parts.append(value)
    grad = jnp.concatenate(parts, axis=1)
    unit, inverse = unit_norm(middle_ref[...])
    out_grad = g_ref[...].astype(f32)
    total = out_grad + norm_pull(grad, gain_ref[...], unit, inverse)
    grad_ref[...] = total
    low = total.astype(bf16)
    low_ref[...] = low
    do_ref[...] = contract_last(low, wo_ref[...]).astype(bf16)
    sum_ref[0:1] += jnp.sum(low.astype(f32), axis=0, keepdims=True)
    sum_ref[1:2] += jnp.sum(grad * unit, axis=0, keepdims=True)
    sum_ref[2:3] += jnp.sum(grad, axis=0, keepdims=True)
    sum_ref[3:4] += jnp.sum(out_grad, axis=0, keepdims=True)


def token_pull_kernel(ncol, dqkv_ref, x_ref, grad_ref, gain_ref, w_ref, own_ref, other_ref, sum_ref):
    @pl.when(pl.program_id(0) == 0)
    def _():
        sum_ref[...] = jnp.zeros_like(sum_ref)

    grad = matmul(dqkv_ref[0], w_ref[0])
    for i in range(1, 3):
        grad = grad + matmul(dqkv_ref[i], w_ref[i])
    unit, inverse = unit_norm(x_ref[...].astype(f32))
    total = grad_ref[...] + norm_pull(grad, gain_ref[...], unit, inverse)
    width = total.shape[1] // ncol
    own_ref[...] = total[:, :width]
    for c in range(1, ncol):
        other_ref[c - 1] = total[:, c * width : (c + 1) * width].astype(bf16)
    sum_ref[0:1] += jnp.sum(grad * unit, axis=0, keepdims=True)
    sum_ref[1:2] += jnp.sum(grad, axis=0, keepdims=True)


def ffn_grad_kernel(ncol, l_ref, r_ref, out_ref):
    width = r_ref.shape[1] // ncol
    left = l_ref[...]
    for c in range(ncol):
        out_ref[0, c] = contract_first(left, r_ref[:, c * width : (c + 1) * width]).astype(bf16)


def head_grad_kernel(dims, l_ref, r_ref, out_ref, *sums):
    ncore, ncol, nz, part, piece = dims
    width = r_ref.shape[1] // ncol
    left = l_ref[0]
    for c in range(ncol):
        value = contract_first(left, r_ref[:, c * width : (c + 1) * width]).astype(bf16)
        value = value.reshape(part, ncore, nz, piece, width)
        for core in range(ncore):
            for z in range(nz):
                out_ref[core, 0, c, z, 0] = value[:, core, z]
    if sums:
        sums[0][0] = jnp.sum(left.astype(f32), axis=0, keepdims=True)


def make_local(nz, ncore, nrow, ncol):
    blocks = ncore * nrow

    def axis_in(values, axis, size):
        return [values] + [shift(values, axis, size, k) for k in range(1, size)]

    def gather(shard):
        along_z = jnp.stack(axis_in(shard, "z", nz))
        along_col = axis_in(along_z, "col", ncol)
        by_col = [axis_in(piece, "row", nrow) for piece in along_col]
        by_row = [by_col[c][r] for r in range(nrow) for c in range(ncol)]
        by_core = [axis_in(piece, "core", ncore) for piece in by_row]
        return [by_core[i][k] for k in range(ncore) for i in range(len(by_row))]

    def scatter(mine, sent):
        held = [mine] + [shift(part, "core", ncore, -(k + 1)) for k, part in enumerate(sent)]

        def total(parts, index):
            value = parts[0][index].astype(f32)
            for part in parts[1:]:
                value = value + part[index].astype(f32)
            return value

        got = [
            shift(total(held, (k,)).astype(bf16), "row", nrow, -k) for k in range(1, nrow)
        ]
        held = [part[0] for part in held] + got
        got = [
            shift(total(held, (k,)).astype(bf16), "col", ncol, -k) for k in range(1, ncol)
        ]
        held = [part[0] for part in held] + got
        got = [shift(total(held, (k,)).astype(bf16), "z", nz, -k) for k in range(1, nz)]
        value = total(held, (0,))
        for part in got:
            value = value + part.astype(f32)
        return value

    def tokens_in(values):
        rows = values.shape[0] // ncol
        here = lax.axis_index("col")
        parts = [lax.dynamic_slice_in_dim(values, here * rows, rows, 0)]
        for k in range(1, ncol):
            block = lax.dynamic_slice_in_dim(values, ((here + k) % ncol) * rows, rows, 0)
            parts.append(shift(block, "col", ncol, k))
        return jnp.concatenate(parts, axis=1)

    def tokens_out(own, other):
        rows = own.shape[0]
        here = lax.axis_index("col")
        result = jnp.zeros((rows * ncol, own.shape[1]), own.dtype)
        result = lax.dynamic_update_slice_in_dim(result, own, here * rows, 0)
        for k in range(1, ncol):
            block = shift(other[k - 1], "col", ncol, -k).astype(own.dtype)
            result = lax.dynamic_update_slice_in_dim(result, block, ((here + k) % ncol) * rows, 0)
        return result

    def local(
        tokens,
        key_mask,
        first_gain,
        first_shift,
        qkv_weight,
        qkv_bias,
        out_weight,
        out_bias,
        second_gain,
        second_shift,
        up_weight,
        up_bias,
        down_weight,
        down_bias,
        cotangent,
    ):
        count = tokens.shape[0] // ncol
        seqs = count // LEN
        part, piece, width = out_weight.shape
        heads = part * nrow
        flat = heads * HD
        hidden_part = up_weight.shape[0]
        step = nz * hidden_part
        dim = width * ncol
        hidden = step * blocks
        pairs = heads // 2
        moved = count * dim

        def tile(shape, index=None):
            return pl.BlockSpec(shape, index or (lambda t: (t,) + (0,) * (len(shape) - 1)))

        inputs = tokens_in(tokens)
        qkv_pieces = gather(qkv_weight.astype(bf16))
        small = jnp.concatenate([qkv_bias.reshape(-1), up_bias]).astype(bf16)
        vectors = jnp.stack([first_gain, first_shift, second_gain, second_shift, out_bias, down_bias])
        vectors = jnp.concatenate(axis_in(vectors, "col", ncol), axis=1)
        gain_one, shift_one, gain_two, shift_two, out_offset, down_offset = [vectors[i : i + 1] for i in range(6)]
        small_z = jnp.stack(axis_in(small, "z", nz))
        small_row = jnp.stack(axis_in(small_z, "row", nrow))
        small_all = jnp.stack(axis_in(small_row, "core", ncore)).astype(f32)
        qkv_count = qkv_bias.size
        qkv_offset = small_all[..., :qkv_count].reshape(ncore, nrow, nz, 2, part, piece)
        qkv_offset = jnp.transpose(qkv_offset, (3, 1, 4, 0, 2, 5)).reshape(2, flat)
        up_offset = small_all[..., qkv_count:].reshape(1, hidden)
        masks = jnp.zeros((ncol,) + key_mask.shape, key_mask.dtype)
        here = lax.axis_index("col")
        for k, mask in enumerate(axis_in(key_mask, "col", ncol)):
            masks = lax.dynamic_update_slice_in_dim(masks, mask[None], (here - k + ncol) % ncol, 0)
        masks = masks.reshape(-1, key_mask.shape[1])
        first_seq = (lax.axis_index("row") * ncol + here) * seqs
        masks = lax.dynamic_slice_in_dim(masks, first_seq, seqs, 0)
        visible = jnp.concatenate([jnp.ones((seqs, BUF), jnp.int32), masks], axis=1)

        grid_shape = (ncore, nrow, ncol, nz)
        qkv_all = jnp.stack(qkv_pieces).reshape(grid_shape + qkv_weight.shape)
        qkv_matrix = jnp.transpose(qkv_all, (4, 1, 5, 0, 3, 6, 2, 7)).reshape(3, flat, dim)
        out_all = jnp.stack(gather(out_weight.astype(bf16))).reshape(grid_shape + out_weight.shape)
        out_matrix = jnp.transpose(out_all, (1, 4, 0, 3, 5, 2, 6)).reshape(flat, dim)
        up_pieces = [w.reshape(step, width) for w in gather(up_weight.astype(bf16))]
        down_pieces = [w.reshape(step, width) for w in gather(down_weight.astype(bf16))]
        grad_low = tokens_in(cotangent)

        tokens_spec = tile((LEN, dim))
        hidden_spec = tile((LEN, hidden))
        piece_specs = [whole((step, width))] * (blocks * ncol)
        vector_spec = whole((1, dim))
        three = pl.BlockSpec((3, LEN, flat), lambda t: (0, t, 0))
        pair_spec = pl.BlockSpec((3, LEN, PAIR), lambda s, p: (0, s, p))
        one_pair = pl.BlockSpec((LEN, PAIR), lambda s, p: (s, p))
        own_spec = tile((LEN, width))
        other_spec = pl.BlockSpec((ncol - 1, LEN, width), lambda t: (0, t, 0))

        def out_of(*shape, dtype=bf16):
            return jax.ShapeDtypeStruct(shape, dtype)

        normed, qkv = call(
            qkv_kernel,
            (seqs,),
            [tokens_spec, vector_spec, vector_spec, whole((3, flat, dim)), whole((2, flat))],
            [tokens_spec, three],
            [out_of(count, dim), out_of(3, count, flat)],
            6 * moved * flat,
            6 * flat * dim + 10 * moved,
            "qkv",
        )(inputs, gain_one, shift_one, qkv_matrix, qkv_offset)
        attended = call(
            attend_kernel,
            (seqs, pairs),
            [pair_spec, pl.BlockSpec((1, 1, LEN), lambda s, p: (s, 0, 0))],
            one_pair,
            out_of(count, flat),
            16 * count * LEN * flat,
            8 * moved,
            "attend",
        )(qkv, visible[:, None, :])
        middle, normed_two = call(
            out_kernel,
            (seqs,),
            [tokens_spec, tile((LEN, flat)), whole((flat, dim)), vector_spec, vector_spec, vector_spec],
            [tokens_spec, tokens_spec],
            [out_of(count, dim, dtype=f32), out_of(count, dim)],
            2 * moved * flat,
            2 * flat * dim + 10 * moved,
            "out",
        )(inputs, attended, out_matrix, out_offset, gain_two, shift_two)
        hid, slope = call(
            functools.partial(up_kernel, ncol, blocks),
            (seqs,),
            [tokens_spec, whole((1, hidden))] + piece_specs,
            [hidden_spec, hidden_spec],
            [out_of(count, hidden), out_of(count, hidden)],
            8 * moved * hidden,
            2 * hidden * dim + 4 * count * hidden,
            "up",
        )(normed_two, up_offset, *up_pieces)

        def ffn_grad(left, right, core, name):
            halves = 2
            rows = step // halves
            return call(
                functools.partial(ffn_grad_kernel, ncol),
                (nrow, halves),
                [
                    pl.BlockSpec((count, rows), lambda r, h: (0, (core * nrow + r) * halves + h)),
                    whole((count, dim)),
                ],
                pl.BlockSpec((1, ncol, rows, width), lambda r, h: (r, 0, h, 0)),
                out_of(nrow, ncol, step, width),
                2 * moved * hidden // ncore,
                2 * (hidden * dim + count * hidden) // ncore + 2 * moved,
                name,
            )(left, right).reshape(nrow, ncol, nz, hidden_part, width)

        def ffn_scatter(left, right, name):
            sent = [ffn_grad(left, right, core, name) for core in range(1, ncore)]
            return scatter(ffn_grad(left, right, 0, name), sent)

        def head_grad(left, right, kinds, name, sums=False):
            dims = (ncore, ncol, nz, part, piece)
            out = call(
                functools.partial(head_grad_kernel, dims),
                (kinds, nrow),
                [
                    pl.BlockSpec((1, count, part * HD), lambda i, r: (i, 0, r)),
                    whole((count, dim)),
                ],
                [
                    pl.BlockSpec(
                        (ncore, 1, ncol, nz, 1, part, piece, width), lambda i, r: (0, r, 0, 0, i, 0, 0, 0)
                    )
                ]
                + [pl.BlockSpec((1, 1, part * HD), lambda i, r: (i, 0, r))] * sums,
                [out_of(ncore, nrow, ncol, nz, kinds, part, piece, width)]
                + [out_of(kinds, 1, flat, dtype=f32)] * sums,
                2 * moved * flat * kinds,
                2 * kinds * (flat * dim + moved) + 2 * moved,
                name,
            )(left, right)
            grads = out[0]
            return scatter(grads[0], [grads[k] for k in range(1, ncore)]), out[1:]

        down_grad = ffn_scatter(hid, grad_low, "down_grad")
        own, other = call(
            functools.partial(down_kernel, ncol, blocks),
            (seqs,),
            [hidden_spec, tokens_spec, vector_spec] + piece_specs,
            [own_spec, other_spec],
            [out_of(count, width), out_of(ncol - 1, count, width)],
            2 * moved * hidden,
            2 * hidden * dim + 2 * count * hidden + 6 * moved,
            "down",
        )(hid, middle, down_offset, *down_pieces)
        activations = tokens_out(own, other)
        upward_grad, up_bias_sum = call(
            functools.partial(hidden_pull_kernel, ncol, blocks),
            (seqs,),
            [tokens_spec, hidden_spec] + piece_specs,
            [hidden_spec, summed((1, hidden))],
            [out_of(count, hidden), out_of(1, hidden, dtype=f32)],
            2 * moved * hidden,
            2 * hidden * dim + 4 * count * hidden,
            "hidden_pull",
        )(grad_low, slope, *down_pieces)
        up_grad = ffn_scatter(upward_grad, normed_two, "up_grad")
        middle_grad, branch_low, attended_grad, sums_two = call(
            functools.partial(middle_pull_kernel, ncol, blocks),
            (seqs,),
            [hidden_spec, tokens_spec, tokens_spec, vector_spec, whole((flat, dim))] + piece_specs,
            [tokens_spec, tokens_spec, tile((LEN, flat)), summed((4, dim))],
            [
                out_of(count, dim, dtype=f32),
                out_of(count, dim),
                out_of(count, flat),
                out_of(4, dim, dtype=f32),
            ],
            2 * moved * (hidden + flat),
            2 * hidden * dim + 2 * count * hidden + 14 * moved,
            "middle_pull",
        )(upward_grad, middle, grad_low, gain_two, out_matrix, *up_pieces)
        out_grad, _ = head_grad(attended[None], branch_low, 1, "out_grad")
        stacked = call(
            attend_pull_kernel,
            (seqs, pairs),
            [pair_spec, pl.BlockSpec((1, LEN, 1), lambda s, p: (s, 0, 0)), one_pair],
            pair_spec,
            out_of(3, count, flat),
            30 * count * LEN * flat,
            14 * moved,
            "attend_pull",
        )(qkv, visible[:, :, None], attended_grad)
        qkv_grad, (head_sums,) = head_grad(stacked, normed, 3, "qkv_grad", True)
        own, other, sums_one = call(
            functools.partial(token_pull_kernel, ncol),
            (seqs,),
            [three, tokens_spec, tokens_spec, vector_spec, whole((3, flat, dim))],
            [own_spec, other_spec, summed((2, dim))],
            [
                out_of(count, width, dtype=f32),
                out_of(ncol - 1, count, width),
                out_of(2, dim, dtype=f32),
            ],
            6 * moved * flat,
            6 * flat * dim + 14 * moved,
            "token_pull",
        )(stacked, inputs, middle_grad, gain_one, qkv_matrix)
        token_grad = tokens_out(own, other)

        bias_sum = jnp.stack([head_sums[0, 0], head_sums[2, 0]]).reshape(2, nrow, part, ncore, nz, piece)
        bias_sum = jnp.transpose(bias_sum, (3, 1, 4, 0, 2, 5)).reshape(ncore, nrow, nz, qkv_count)
        bias_sum = jnp.concatenate([bias_sum, up_bias_sum.reshape(ncore, nrow, nz, hidden_part)], axis=-1)
        sums = jnp.concatenate([sums_one, sums_two])
        own_sums = sums[:, :width].reshape(-1)
        size = own_sums.size
        flat_bias = bias_sum.reshape(-1)
        pack = jnp.concatenate([own_sums, flat_bias])
        for k in range(1, ncol):
            sent = jnp.concatenate([sums[:, k * width : (k + 1) * width].reshape(-1), flat_bias])
            pack = pack + shift(sent, "col", ncol, -k)
        for axis, count_along in (("core", ncore), ("row", nrow), ("z", nz)):
            both = pack[:size]
            rest = pack[size:].reshape(count_along, -1)
            pack = jnp.concatenate([both, rest[0]])
            for k in range(1, count_along):
                pack = pack + shift(jnp.concatenate([both, rest[k]]), axis, count_along, -k)
        sums = pack[:size].reshape(-1, width)
        bias_sum = pack[size:]
        return (
            activations,
            token_grad,
            sums[0],
            sums[1],
            qkv_grad,
            bias_sum[:qkv_count].reshape(qkv_bias.shape),
            out_grad[0],
            sums[2],
            sums[3],
            sums[4],
            up_grad,
            bias_sum[qkv_count:],
            down_grad,
            sums[5],
        )

    return local


def solution(mesh):
    devices = mesh.devices
    nz, ncore = devices.shape[0] // 2, 2
    nrow, ncol = devices.shape[1], devices.shape[2]
    fine = Mesh(devices.reshape(nz, ncore, nrow, ncol), ("z", "core", "row", "col"))
    dp = ("z", "core")
    rows = P(("z", "core", "row"), "col")
    qkv_weight = P(None, "row", dp, "col")
    qkv_bias = P(None, "row", dp)
    out_weight = P("row", dp, "col")
    feature = P("col")
    unit = P(("z", "core", "row"))
    in_specs = (
        rows,
        P(("z", "core", "col"), None),
        feature,
        feature,
        qkv_weight,
        qkv_bias,
        out_weight,
        feature,
        feature,
        feature,
        rows,
        unit,
        rows,
        feature,
        rows,
    )
    out_specs = (
        rows,
        rows,
        feature,
        feature,
        qkv_weight,
        qkv_bias,
        out_weight,
        feature,
        feature,
        feature,
        rows,
        unit,
        rows,
        feature,
    )
    return jax.shard_map(
        make_local(nz, ncore, nrow, ncol),
        mesh=fine,
        in_specs=in_specs,
        out_specs=out_specs,
        check_vma=False,
    )
```

```python
import functools
import itertools

import jax
import jax.numpy as jnp
from jax import lax
from jax.experimental import pallas as pl
from jax.experimental.pallas import tpu as pltpu
from jax.sharding import Mesh, PartitionSpec as P

HD = 64
PAIR = 2 * HD
BUF = 64
LEN = 320
masked_fill = -1000000000.0
norm_epsilon = 1e-06
attn_scale = 0.125
exp2_scale = attn_scale * 1.4426950408889634
root_half = 0.7071067811865476
density = 0.3989422804014327
bf16 = jnp.bfloat16
f32 = jnp.float32
MIB = 1 << 20


def contract_last(left, right):
    return lax.dot_general(left, right, (((1,), (1,)), ((), ())), preferred_element_type=f32)


def contract_first(left, right):
    return lax.dot_general(left, right, (((0,), (0,)), ((), ())), preferred_element_type=f32)


def matmul(left, right):
    return lax.dot_general(left, right, (((1,), (0,)), ((), ())), preferred_element_type=f32)


def whole(shape):
    return pl.BlockSpec(shape, lambda *_: (0,) * len(shape), pipeline_mode=pl.Buffered(1))


def summed(shape):
    return pl.BlockSpec(shape, lambda *_: (0,) * len(shape))


def call(kernel, grid, in_specs, out_specs, out_shape, flops, moved, name, vmem=48, scratch=()):
    return pl.pallas_call(
        kernel,
        grid=grid,
        in_specs=in_specs,
        out_specs=out_specs,
        out_shape=out_shape,
        scratch_shapes=scratch,
        name=name,
        compiler_params=pltpu.CompilerParams(vmem_limit_bytes=vmem * MIB),
        cost_estimate=pl.CostEstimate(flops=flops, bytes_accessed=moved, transcendentals=0),
    )


def unit_norm(values):
    center = jnp.mean(values, axis=1, keepdims=True)
    centered = values - center
    spread = jnp.mean(centered * centered, axis=1, keepdims=True)
    inverse = lax.rsqrt(spread + norm_epsilon)
    return centered * inverse, inverse


def norm_pull(grad, gain, unit, inverse):
    scaled = grad * gain
    total = jnp.mean(scaled, axis=1, keepdims=True)
    paired = jnp.mean(scaled * unit, axis=1, keepdims=True)
    return inverse * (scaled - total - unit * paired)


def head_weight(layout, refs):
    if layout is None:
        return refs[1:], lambda: None, lambda i: refs[0][i]
    places, kinds = layout
    held, sem = refs[-2:]
    operands = 1 + max(place[0] for place in places)

    def copies(kind):
        for operand, index, head, row, lane in places:
            source = refs[operand].at[index + (kind,)]
            part, piece, width = source.shape
            target = held.at[kind, pl.ds(head, part), pl.ds(row, piece), pl.ds(lane, width)]
            yield pltpu.make_async_copy(source, target, sem.at[kind])

    def fetch():
        @pl.when(pl.program_id(0) == 0)
        def _():
            for kind in range(kinds):
                for copy in copies(kind):
                    copy.start()

    def read(kind):
        @pl.when(pl.program_id(0) == 0)
        def _():
            for copy in copies(kind):
                copy.wait()

        return held[kind].reshape(held.shape[1] * held.shape[2], held.shape[3])

    return refs[operands:-2], fetch, read


def qkv_kernel(layout, x_ref, gain_ref, shift_ref, bias_ref, *refs):
    (a_ref, out_ref), fetch, read = head_weight(layout, refs)
    fetch()
    unit, _ = unit_norm(x_ref[...].astype(f32))
    a = (unit * gain_ref[...] + shift_ref[...]).astype(bf16)
    a_ref[...] = a
    for i in range(3):
        value = contract_last(a, read(i))
        if i != 1:
            value = value + bias_ref[i // 2 : i // 2 + 1]
        out_ref[i] = value.astype(bf16)


def split_heads(pair):
    first = lax.broadcasted_iota(jnp.int32, pair.shape, 1) < HD
    zero = jnp.zeros_like(pair)
    return jnp.concatenate([jnp.where(first, pair, zero), jnp.where(first, zero, pair)], axis=0)


def join_heads(both):
    rows = both.shape[0] // 2
    first = lax.broadcasted_iota(jnp.int32, (rows, both.shape[1]), 1) < HD
    return jnp.where(first, both[:rows], both[rows:])


def attend_kernel(qkv_ref, mask_ref, out_ref):
    seen = mask_ref[0] > 0
    scores = contract_last(split_heads(qkv_ref[0]), qkv_ref[1])
    scores = jnp.where(seen, scores, masked_fill / attn_scale)
    top = jnp.max(scores, axis=1, keepdims=True)
    grown = jnp.exp2((scores - top) * exp2_scale)
    total = jnp.sum(grown, axis=1, keepdims=True)
    mixed = matmul(grown.astype(bf16), qkv_ref[2]) / total
    out_ref[...] = join_heads(mixed).astype(bf16)


def attend_pull_kernel(qkv_ref, mask_ref, do_ref, out_ref):
    seen = mask_ref[0] > 0
    both = split_heads(qkv_ref[0])
    keys = qkv_ref[1]
    vals = qkv_ref[2]
    pulled = split_heads(do_ref[...])
    scores = contract_last(keys, both)
    scores = jnp.where(seen, scores, masked_fill / attn_scale)
    top = jnp.max(scores, axis=0, keepdims=True)
    grown = jnp.exp2((scores - top) * exp2_scale)
    probs = grown * (1.0 / jnp.sum(grown, axis=0, keepdims=True))
    prob_grad = contract_last(vals, pulled)
    out_ref[2] = matmul(probs.astype(bf16), pulled).astype(bf16)
    inner = jnp.sum(prob_grad * probs, axis=0, keepdims=True)
    score_grad = (probs * (prob_grad - inner)).astype(bf16)
    out_ref[1] = (matmul(score_grad, both) * attn_scale).astype(bf16)
    query_grad = contract_first(score_grad, keys) * attn_scale
    out_ref[0] = join_heads(query_grad).astype(bf16)


def out_kernel(layout, x_ref, o_ref, bias_ref, gain_ref, shift_ref, *refs):
    (middle_ref, a_ref), fetch, read = head_weight(layout, refs)
    fetch()
    middle = x_ref[...].astype(f32) + (matmul(o_ref[...], read(0)) + bias_ref[...])
    middle_ref[...] = middle
    unit, _ = unit_norm(middle)
    a_ref[...] = (unit * gain_ref[...] + shift_ref[...]).astype(bf16)


def pieces_of(dims, refs):
    ncol, nrow, ncore, places = dims
    w_refs, rest = refs[: len(places)], refs[len(places) :]

    def piece(block, col):
        core, within = divmod(block, 2 * nrow)
        row, half = divmod(within, 2)
        lead, second = (row, col) if half else (col, row)
        for ref, (in_core, in_half, first) in zip(w_refs, places):
            if (in_core, in_half) == (core, half) and first <= lead < first + ref.shape[0]:
                return ref[lead - first, second]

    return piece, 2 * ncore * nrow, w_refs[0].shape[2], w_refs[0].shape[3], rest


def up_kernel(dims, a_ref, bias_ref, *refs):
    piece, blocks, step, width, (hid_ref, slope_ref) = pieces_of(dims, refs)
    for b in range(blocks):
        rows = slice(b * step, (b + 1) * step)
        value = bias_ref[:, rows]
        for c in range(dims[0]):
            value = value + contract_last(a_ref[:, c * width : (c + 1) * width], piece(b, c))
        cdf = 0.5 + 0.5 * lax.erf(value * root_half)
        pdf = jnp.exp(-0.5 * value * value) * density
        hid_ref[:, rows] = (value * cdf).astype(bf16)
        slope_ref[:, rows] = (cdf + value * pdf).astype(bf16)


def down_kernel(dims, hid_ref, middle_ref, bias_ref, *refs):
    piece, blocks, step, width, (own_ref, other_ref) = pieces_of(dims, refs)
    for c in range(dims[0]):
        lanes = slice(c * width, (c + 1) * width)
        value = middle_ref[:, lanes] + bias_ref[:, lanes]
        for b in range(blocks):
            value = value + matmul(hid_ref[:, b * step : (b + 1) * step], piece(b, c))
        if c == 0:
            own_ref[...] = value.astype(bf16)
        else:
            other_ref[c - 1] = value.astype(bf16)


def hidden_pull_kernel(dims, g_ref, slope_ref, *refs):
    piece, blocks, step, width, (du_ref, sum_ref) = pieces_of(dims, refs)

    @pl.when(pl.program_id(0) == 0)
    def _():
        sum_ref[...] = jnp.zeros_like(sum_ref)

    for b in range(blocks):
        rows = slice(b * step, (b + 1) * step)
        value = contract_last(g_ref[:, :width], piece(b, 0))
        for c in range(1, dims[0]):
            value = value + contract_last(g_ref[:, c * width : (c + 1) * width], piece(b, c))
        low = (value * slope_ref[:, rows].astype(f32)).astype(bf16)
        du_ref[:, rows] = low
        sum_ref[:, rows] += jnp.sum(low.astype(f32), axis=0, keepdims=True)


def middle_pull_kernel(dims, layout, du_ref, middle_ref, g_ref, gain_ref, *refs):
    piece, blocks, step, width, rest = pieces_of(dims, refs)
    (grad_ref, low_ref, do_ref, sum_ref), fetch, read = head_weight(layout, rest)
    fetch()

    @pl.when(pl.program_id(0) == 0)
    def _():
        sum_ref[...] = jnp.zeros_like(sum_ref)

    parts = []
    for c in range(dims[0]):
        value = matmul(du_ref[:, :step], piece(0, c))
        for b in range(1, blocks):
            value = value + matmul(du_ref[:, b * step : (b + 1) * step], piece(b, c))
        parts.append(value)
    grad = jnp.concatenate(parts, axis=1)
    unit, inverse = unit_norm(middle_ref[...])
    out_grad = g_ref[...].astype(f32)
    total = out_grad + norm_pull(grad, gain_ref[...], unit, inverse)
    grad_ref[...] = total
    low = total.astype(bf16)
    low_ref[...] = low
    do_ref[...] = contract_last(low, read(0)).astype(bf16)
    sum_ref[0:1] += jnp.sum(low.astype(f32), axis=0, keepdims=True)
    sum_ref[1:2] += jnp.sum(grad * unit, axis=0, keepdims=True)
    sum_ref[2:3] += jnp.sum(grad, axis=0, keepdims=True)
    sum_ref[3:4] += jnp.sum(out_grad, axis=0, keepdims=True)


def token_pull_kernel(ncol, layout, near_ref, far_ref, x_ref, grad_ref, gain_ref, *refs):
    (own_ref, other_ref, sum_ref), fetch, read = head_weight(layout, refs)
    fetch()

    @pl.when(pl.program_id(0) == 0)
    def _():
        sum_ref[...] = jnp.zeros_like(sum_ref)

    grad = None
    for i in range(3):
        weight = read(i)
        middle = weight.shape[0] // 2
        value = matmul(near_ref[i], weight[:middle]) + matmul(far_ref[i], weight[middle:])
        grad = value if grad is None else grad + value
    unit, inverse = unit_norm(x_ref[...].astype(f32))
    total = grad_ref[...] + norm_pull(grad, gain_ref[...], unit, inverse)
    width = total.shape[1] // ncol
    own_ref[...] = total[:, :width]
    for c in range(1, ncol):
        other_ref[c - 1] = total[:, c * width : (c + 1) * width].astype(bf16)
    sum_ref[0:1] += jnp.sum(grad * unit, axis=0, keepdims=True)
    sum_ref[1:2] += jnp.sum(grad, axis=0, keepdims=True)


def ffn_sent_kernel(ncol, l_ref, r_ref, out_ref):
    width = r_ref.shape[1] // ncol
    left = l_ref[...]
    for c in range(ncol):
        out_ref[0, 0, c] = contract_first(left, r_ref[:, c * width : (c + 1) * width]).astype(bf16)


def ffn_kept_kernel(ncol, nrow, l_ref, r_ref, got_ref, *out_refs):
    by_col, by_row = out_refs[:ncol], out_refs[ncol:]
    width = r_ref.shape[1] // ncol
    left = l_ref[...]
    half, row = pl.program_id(0), pl.program_id(1)
    values = []
    for c in range(ncol):
        value = contract_first(left, r_ref[:, c * width : (c + 1) * width])
        values.append((value + got_ref[0, 0, c].astype(f32)).astype(bf16))

    @pl.when(half == 0)
    def _():
        for c in range(ncol):
            by_col[c][0] = values[c]

    for r in range(nrow):

        @pl.when((half == 1) & (row == r))
        def _(r=r):
            for c in range(ncol):
                by_row[r][c] = values[c]


def head_grad_kernel(sizes, l_ref, r_ref, *refs):
    ncore, ncol, nz, part, piece = sizes
    width = r_ref.shape[1] // ncol
    left = l_ref[0]
    for c in range(ncol):
        value = contract_first(left, r_ref[:, c * width : (c + 1) * width]).astype(bf16)
        value = value.reshape(part, ncore, nz, piece, width)
        for core in range(ncore):
            for z in range(nz):
                refs[core][0, c, z, 0] = value[:, core, z]
    for sum_ref in refs[ncore:]:
        sum_ref[0] = jnp.sum(left.astype(f32), axis=0, keepdims=True)


def make_local(nz, ncore, nrow, ncol):
    blocks = ncore * nrow
    sizes = {"z": nz, "core": ncore, "row": nrow, "col": ncol}

    def bits(axis):
        return [1 << k for k in range(sizes[axis].bit_length() - 1)]

    def exchange(values, axis, bit):
        return lax.ppermute(values, axis, [(i, i ^ bit) for i in range(sizes[axis])])

    class Slots:
        def __init__(self):
            self.before, self.now = [], []

        def advance(self):
            self.before, self.now = self.now, []

        def note(self, *values):
            self.now.extend(values)

        def gate(self, *values):
            if not self.before:
                return values
            return lax.optimization_barrier((*values, *self.before))[: len(values)]

        def move(self, values, axis, bit):
            got = exchange(values, axis, bit)
            self.now.append(got)
            return got

        def send(self, values, axis, bit):
            return self.move(self.gate(values)[0], axis, bit)

        def widen(self, parts, axis, lead=True):
            parts = list(self.gate(*parts))
            if lead:
                parts = [joined(parts)[None]]
            for bit in bits(axis):
                values = joined(parts)
                parts = [values, self.move(values, axis, bit)]
            return parts

        def fold(self, held, axis, dim):
            arrays = self.gate(*[view[0] for view in held])
            held = [(array, view[1]) for array, view in zip(arrays, held)]
            for bit in [bit for bit in reversed(bits(axis)) if bit < held[0][1][dim][1]]:
                got = self.move(total([half_of(view, dim, 1) for view in held]).astype(bf16), axis, bit)
                held = [half_of(view, dim, 0) for view in held] + [view_of(got)]
            return held

    def joined(parts):
        return parts[0] if len(parts) == 1 else jnp.concatenate(parts)

    def view_of(array):
        return (array, tuple((0, n) for n in array.shape[:3]))

    def half_of(view, dim, which):
        array, spans = view
        start, size = spans[dim]
        size //= 2
        return (array, spans[:dim] + ((start + which * size, size),) + spans[dim + 1 :])

    def total(held):
        value = None
        for array, spans in held:
            part = array[tuple(slice(start, start + size) for start, size in spans)].astype(f32)
            value = part if value is None else value + part
        return value

    class Gather:
        def __init__(self, name, slots, shard):
            self.name, self.slots, self.low = name, slots, [shard[None]]

        def z_all(self):
            (values,) = self.slots.gate(*self.low)
            near = nz // 2
            parts = [values] + [self.slots.move(values, "z", k) for k in range(1, nz)]
            self.low, self.high = parts[:near], parts[near:]

        def z_low(self):
            parts = list(self.slots.gate(*self.low))
            for bit in bits("z")[:-1]:
                values = joined(parts)
                parts = [values, self.slots.move(values, "z", bit)]
            self.low = parts

        def z_high(self):
            values = joined(list(self.slots.gate(*self.low)))
            self.low = [values]
            self.high = [self.slots.move(values, "z", bits("z")[-1])]

        def z_high_first(self):
            values = joined(list(self.slots.gate(*self.low)))
            half = values.shape[0] // 2
            self.low = [values[:half], values[half:]]
            self.high = [self.slots.move(self.low[0], "z", bits("z")[-1])]

        def z_high_second(self):
            (values,) = self.slots.gate(self.low[1])
            self.high.append(self.slots.move(values, "z", bits("z")[-1]))

        def x_low(self):
            self.low_row = self.slots.widen(self.low, "row")

        def y_high(self):
            self.high_col = self.slots.widen(self.high, "col")

        def y_low(self):
            self.low_all = self.slots.widen(self.low_row, "col")

        def x_high(self):
            self.high_all = self.slots.widen(self.high_col, "row")

        def y(self):
            self.all_col = self.slots.widen(self.low + self.high, "col")

        def x(self):
            self.all_row = self.slots.widen(self.all_col, "row")

        def core(self):
            if hasattr(self, "all_row"):
                lists = [(2, self.all_row)]
            else:
                lists = [(0, self.low_all), (1, self.high_all)]
            self.places, self.pieces = [], []
            for half, parts in lists:
                parts = self.slots.gate(*parts)
                for k in range(ncore):
                    first = 0
                    for values in parts:
                        self.places.append((k, half, first))
                        self.pieces.append(self.slots.move(values, "core", k) if k else values)
                        first += values.shape[0]

    class Scatter:
        def __init__(self, name, slots):
            self.name, self.slots, self.low, self.high = name, slots, [], []

        def halve(self, arrays):
            views = [view_of(array) for array in arrays]
            self.low = self.low + [half_of(view, 2, 0) for view in views]
            self.high = self.high + [half_of(view, 2, 1) for view in views]

        def first_fold(self, parts, axis, dim):
            parts = list(self.slots.gate(*parts))
            held = []
            for bit in reversed(bits(axis)):
                value = parts[bit] if bit == 1 else jnp.concatenate(parts[bit : 2 * bit], axis=dim)
                if held:
                    value = (value.astype(f32) + total([half_of(view, dim, 1) for view in held])).astype(bf16)
                got = self.slots.move(value, axis, bit)
                held = [half_of(view, dim, 0) for view in held] + [view_of(got)]
            return [view_of(parts[0])] + held

        def x_high_first(self, by_row):
            self.high = self.first_fold(by_row, "row", 0)

        def y_low_first(self, by_col):
            self.low = self.first_fold(by_col, "col", 1)

        def x_high(self):
            self.high = self.slots.fold(self.high, "row", 0)

        def y_low(self):
            self.low = self.slots.fold(self.low, "col", 1)

        def y_high(self):
            self.high = self.slots.fold(self.high, "col", 1)

        def x_low(self):
            self.low = self.slots.fold(self.low, "row", 0)

        def z_high(self):
            arrays = self.slots.gate(*[view[0] for view in self.high])
            value = total([(array, view[1]) for array, view in zip(arrays, self.high)])
            self.low = self.low + [view_of(self.slots.move(value.astype(bf16), "z", nz // 2))]

        def z_low(self):
            arrays = self.slots.gate(*[view[0] for view in self.low])
            held = [(array, view[1]) for array, view in zip(arrays, self.low)]
            for bit in reversed(bits("z")[:-1]):
                got = self.slots.move(total([half_of(view, 2, 1) for view in held]).astype(bf16), "z", bit)
                held = [half_of(view, 2, 0) for view in held] + [view_of(got)]
            self.low = held

        def result(self):
            arrays = self.slots.gate(*[view[0] for view in self.low])
            return total([(array, view[1]) for array, view in zip(arrays, self.low)])[0, 0, 0]

    class TokensIn:
        def __init__(self, name, slots, values):
            self.name, self.slots, self.values, self.parts = name, slots, values, []

        def step(self, which, steps):
            rows = self.values.shape[0] // ncol
            here = lax.axis_index("col")
            (values,) = self.slots.gate(self.values)
            size = rows // steps
            parts = [lax.dynamic_slice_in_dim(values, here * rows + which * size, size, 0)]
            for k in range(1, ncol):
                block = lax.dynamic_slice_in_dim(values, (here ^ k) * rows + which * size, size, 0)
                parts.append(self.slots.move(block, "col", k))
            self.parts.append(parts)

        def first(self):
            self.step(0, 2)

        def second(self):
            self.step(1, 2)

        def end(self):
            count = len(self.parts[0])
            flat = self.slots.gate(*[part for parts in self.parts for part in parts])
            rows = [jnp.concatenate(flat[i : i + count], axis=1) for i in range(0, len(flat), count)]
            return jnp.concatenate(rows)

    def do(job, *stages):
        for stage in stages:
            with jax.named_scope(job.name + "_" + stage):
                getattr(job, stage)()

    class TokensOut:
        def __init__(self, name, slots, own, other):
            self.name, self.slots, self.own, self.other = name, slots, own, other

        def send(self):
            self.blocks = [self.slots.send(self.other[k - 1], "col", k) for k in range(1, ncol)]

        def end(self):
            rows = self.own.shape[0]
            here = lax.axis_index("col")
            first, *rest = self.slots.gate(self.own, *self.blocks)
            result = jnp.zeros((rows * ncol, self.own.shape[1]), self.own.dtype)
            result = lax.dynamic_update_slice_in_dim(result, first, here * rows, 0)
            for k, block in enumerate(rest):
                result = lax.dynamic_update_slice_in_dim(
                    result, block.astype(self.own.dtype), (here ^ (k + 1)) * rows, 0
                )
            return result

    def local(
        tokens,
        key_mask,
        first_gain,
        first_shift,
        qkv_weight,
        qkv_bias,
        out_weight,
        out_bias,
        second_gain,
        second_shift,
        up_weight,
        up_bias,
        down_weight,
        down_bias,
        cotangent,
    ):
        count = tokens.shape[0] // ncol
        seqs = count // LEN
        part, piece, width = out_weight.shape
        heads = part * nrow
        flat = heads * HD
        hidden_part = up_weight.shape[0]
        step = nz * hidden_part
        dim = width * ncol
        hidden = step * blocks
        pairs = heads // 2
        moved = count * dim

        def tile(shape, index=None):
            return pl.BlockSpec(shape, index or (lambda t: (t,) + (0,) * (len(shape) - 1)))

        slots = Slots()
        q = Gather("qkv", slots, qkv_weight.astype(bf16))
        o = Gather("out", slots, out_weight[None].astype(bf16))
        u = Gather("up", slots, up_weight.astype(bf16))
        d = Gather("down", slots, down_weight.astype(bf16))
        tok = TokensIn("tokens", slots, tokens)
        cot = TokensIn("cotangent", slots, cotangent)
        small = [jnp.concatenate([qkv_bias.reshape(-1), up_bias]).astype(bf16)[None]]
        vectors = jnp.stack([first_gain, first_shift, second_gain, second_shift, out_bias, down_bias])

        do(q, "z_all")
        do(tok, "first")
        vectors = slots.widen([vectors], "col")
        slots.advance()
        do(q, "x_low", "y_high")
        do(o, "z_low")
        do(u, "z_low")
        small = slots.widen(small, "z", False)
        slots.advance()
        do(q, "y_low", "x_high")
        do(o, "z_high")
        do(u, "z_high_first")
        small = slots.widen(small, "row")
        nearby = slots.widen([key_mask], "col")
        slots.advance()
        do(q, "core")
        do(u, "z_high_second", "x_low")
        do(tok, "second")
        do(d, "z_low")
        do(o, "y")
        small = slots.widen(small, "core")
        slots.advance()
        inputs = tok.end()
        vectors = jnp.transpose(joined(list(slots.gate(*vectors))), (1, 0, 2)).reshape(6, dim)
        gain_one, shift_one, gain_two, shift_two, out_offset, down_offset = [vectors[i : i + 1] for i in range(6)]
        small_all = joined(list(slots.gate(*small))).astype(f32)
        qkv_count = qkv_bias.size
        qkv_offset = small_all[..., :qkv_count].reshape(ncore, nrow, nz, 2, part, piece)
        qkv_offset = jnp.transpose(qkv_offset, (3, 1, 4, 0, 2, 5)).reshape(2, flat)
        up_offset = small_all[..., qkv_count:].reshape(1, hidden)
        here = lax.axis_index("col")
        nearby = joined(nearby)
        masks = jnp.zeros_like(nearby)
        for k in range(ncol):
            masks = lax.dynamic_update_slice_in_dim(masks, nearby[k : k + 1], here ^ k, 0)
        masks = masks.reshape(-1, key_mask.shape[1])
        first_seq = (lax.axis_index("row") * ncol + here) * seqs
        masks = lax.dynamic_slice_in_dim(masks, first_seq, seqs, 0)
        visible = jnp.concatenate([jnp.ones((seqs, BUF), jnp.int32), masks], axis=1)

        def head_operands(w, kinds):
            half = nz // 2
            places = []
            for k, r, c, z in itertools.product(range(ncore), range(nrow), range(ncol), range(nz)):
                for n, ((in_core, in_half, first), values) in enumerate(zip(w.places, w.pieces)):
                    lead, second, inner = (c, r, z) if in_half == 0 else (r, c, z - half * (in_half == 1))
                    held = in_half == 2 or in_half == z // half
                    if held and in_core == k and first <= lead < first + values.shape[0]:
                        index = (lead - first, second, inner)
                        places.append((n, index, r * part, (k * nz + z) * piece, c * width))
            if piece % 8 == 0:
                specs = [pl.BlockSpec(memory_space=pl.ANY)] * len(w.pieces)
                scratch = [pltpu.VMEM((kinds, heads, HD, dim), bf16), pltpu.SemaphoreType.DMA((kinds,))]
                return w.pieces, specs, scratch, (tuple(places), kinds)
            matrix = jnp.zeros((kinds, heads, HD, dim), bf16)
            for n, index, head, row, lane in places:
                matrix = lax.dynamic_update_slice(matrix, w.pieces[n][index], (0, head, row, lane))
            return [matrix.reshape(kinds, flat, dim)], [whole((kinds, flat, dim))], [], None

        qkv_ops, qkv_specs, qkv_scratch, qkv_layout = head_operands(q, 3)

        tokens_spec = tile((LEN, dim))
        hidden_spec = tile((LEN, hidden))
        half_step = step // 2
        vector_spec = whole((1, dim))
        three = pl.BlockSpec((3, LEN, flat), lambda t: (0, t, 0))
        pair_spec = pl.BlockSpec((3, LEN, PAIR), lambda s, p: (0, s, p))
        one_pair = pl.BlockSpec((LEN, PAIR), lambda s, p: (s, p))
        own_spec = tile((LEN, width))
        other_spec = pl.BlockSpec((ncol - 1, LEN, width), lambda t: (0, t, 0))

        def out_of(*shape, dtype=bf16):
            return jax.ShapeDtypeStruct(shape, dtype)

        def ffn_operands(w):
            operands = [p.reshape(p.shape[0], p.shape[1], half_step, width) for p in w.pieces]
            return operands, [whole(p.shape) for p in operands], (ncol, nrow, ncore, tuple(w.places))

        do(u, "y_high")
        do(o, "x")
        do(d, "z_high_first")
        do(cot, "first")
        normed, qkv = call(
            functools.partial(qkv_kernel, qkv_layout),
            (seqs,),
            [tokens_spec, vector_spec, vector_spec, whole((2, flat))] + qkv_specs,
            [tokens_spec, three],
            [out_of(count, dim), out_of(3, count, flat)],
            6 * moved * flat,
            6 * flat * dim + 10 * moved,
            "qkv",
            scratch=qkv_scratch,
        )(inputs, gain_one, shift_one, qkv_offset, *qkv_ops)
        slots.note(qkv)
        slots.advance()

        do(u, "y_low", "x_high")
        do(d, "z_high_second")
        do(o, "core")
        attended = call(
            attend_kernel,
            (seqs, pairs),
            [pair_spec, pl.BlockSpec((1, 1, LEN), lambda s, p: (s, 0, 0))],
            one_pair,
            out_of(count, flat),
            16 * count * LEN * flat,
            8 * moved,
            "attend",
        )(slots.gate(qkv)[0], visible[:, None, :])
        slots.note(attended)
        slots.advance()

        do(u, "core")
        do(d, "x_low", "y_high")
        do(cot, "second")
        out_ops, out_specs, out_scratch, out_layout = head_operands(o, 1)
        middle, normed_two = call(
            functools.partial(out_kernel, out_layout),
            (seqs,),
            [tokens_spec, tile((LEN, flat)), vector_spec, vector_spec, vector_spec] + out_specs,
            [tokens_spec, tokens_spec],
            [out_of(count, dim, dtype=f32), out_of(count, dim)],
            2 * moved * flat,
            2 * flat * dim + 10 * moved,
            "out",
            scratch=out_scratch,
        )(inputs, slots.gate(attended)[0], out_offset, gain_two, shift_two, *out_ops)
        up_ops, up_specs, up_dims = ffn_operands(u)
        hid, slope = call(
            functools.partial(up_kernel, up_dims),
            (seqs,),
            [tokens_spec, whole((1, hidden))] + up_specs,
            [hidden_spec, hidden_spec],
            [out_of(count, hidden), out_of(count, hidden)],
            8 * moved * hidden,
            2 * hidden * dim + 4 * count * hidden,
            "up",
        )(normed_two, up_offset, *up_ops)
        slots.note(hid)
        slots.advance()

        def ffn_sent(left, right, name):
            return call(
                functools.partial(ffn_sent_kernel, ncol),
                (2, nrow),
                [
                    pl.BlockSpec((count, half_step), lambda h, r: (0, (nrow + r) * 2 + h)),
                    whole((count, dim)),
                ],
                pl.BlockSpec((1, 1, ncol, half_step, width), lambda h, r: (h, r, 0, 0, 0)),
                out_of(2, nrow, ncol, half_step, width),
                2 * moved * hidden // ncore,
                2 * (hidden * dim + count * hidden) // ncore + 2 * moved,
                name,
            )(slots.gate(left)[0], right)

        def ffn_kept(left, right, got, name):
            by_col = pl.BlockSpec((1, half_step, width), lambda h, r: (jnp.where(h == 0, r, nrow - 1), 0, 0))
            out = call(
                functools.partial(ffn_kept_kernel, ncol, nrow),
                (2, nrow),
                [
                    pl.BlockSpec((count, half_step), lambda h, r: (0, r * 2 + h)),
                    whole((count, dim)),
                    pl.BlockSpec((1, 1, ncol, half_step, width), lambda h, r: (h, r, 0, 0, 0)),
                ],
                [by_col] * ncol + [summed((ncol, half_step, width))] * nrow,
                [out_of(nrow, half_step, width)] * ncol + [out_of(ncol, half_step, width)] * nrow,
                2 * moved * hidden // ncore,
                3 * (hidden * dim + count * hidden) // ncore + 2 * moved,
                name,
            )(left, right, got)
            shape = (nz // 2, hidden_part, width)
            slots.note(out[0])
            low = [values.reshape((nrow, 1) + shape) for values in out[:ncol]]
            return low, [values.reshape((1, ncol) + shape) for values in out[ncol:]]

        def head_grad(left, right, first, name, sums=False):
            kinds, _, lanes = left.shape
            rows = lanes // (part * HD)
            out = call(
                functools.partial(head_grad_kernel, (ncore, ncol, nz, part, piece)),
                (kinds, rows),
                [
                    pl.BlockSpec((1, count, part * HD), lambda i, r: (i, 0, r)),
                    whole((count, dim)),
                ],
                [pl.BlockSpec((1, ncol, nz, 1, part, piece, width), lambda i, r: (r, 0, 0, i, 0, 0, 0))] * ncore
                + [pl.BlockSpec((1, 1, part * HD), lambda i, r: (i, 0, r))] * sums,
                [out_of(rows, ncol, nz, kinds, part, piece, width)] * ncore
                + [out_of(kinds, 1, lanes, dtype=f32)] * sums,
                2 * moved * lanes * kinds,
                2 * kinds * (lanes * dim + count * lanes) + 2 * moved,
                name,
            )(left, right)
            slots.note(out[0])
            return out[:ncore], out[ncore:]

        def core_fold(name, sums):
            with jax.named_scope(name + "_core"):
                return [sums[0]] + [slots.send(sums[k], "core", k) for k in range(1, ncore)]

        def pull(first, rows):
            low = first * part // 2
            high = rows * part // 2
            return call(
                attend_pull_kernel,
                (seqs, high),
                [
                    pl.BlockSpec((3, LEN, PAIR), lambda s, p: (0, s, low + p)),
                    pl.BlockSpec((1, LEN, 1), lambda s, p: (s, 0, 0)),
                    pl.BlockSpec((LEN, PAIR), lambda s, p: (s, low + p)),
                ],
                pair_spec,
                out_of(3, count, rows * part * HD),
                30 * count * LEN * rows * part * HD,
                14 * moved * rows // nrow,
                "attend_pull",
            )(qkv, visible[:, :, None], slots.gate(attended_grad)[0])

        do(d, "y_low", "x_high")
        grad_low = cot.end()
        sent = ffn_sent(hid, grad_low, "down_grad")
        (got,) = core_fold("down_grad", [sent, sent])[1:]
        down_low, down_high = ffn_kept(hid, grad_low, got, "down_grad")
        slots.advance()

        dg, ug, og, qg = [Scatter(name, slots) for name in ("down_grad", "up_grad", "out_grad", "qkv_grad")]
        do(d, "core")
        with jax.named_scope("down_grad_first"):
            dg.x_high_first(down_high)
            dg.y_low_first(down_low)
        down_ops, down_specs, down_dims = ffn_operands(d)
        upward_grad, up_bias_sum = call(
            functools.partial(hidden_pull_kernel, down_dims),
            (seqs,),
            [tokens_spec, hidden_spec] + down_specs,
            [hidden_spec, summed((1, hidden))],
            [out_of(count, hidden), out_of(1, hidden, dtype=f32)],
            2 * moved * hidden,
            2 * hidden * dim + 4 * count * hidden,
            "hidden_pull",
        )(grad_low, slope, *down_ops)
        slots.note(upward_grad)
        slots.advance()

        do(dg, "y_high", "x_low")
        sent = ffn_sent(upward_grad, normed_two, "up_grad")
        (got,) = core_fold("up_grad", [sent, sent])[1:]
        own, other = call(
            functools.partial(down_kernel, down_dims),
            (seqs,),
            [hidden_spec, tokens_spec, vector_spec] + down_specs,
            [own_spec, other_spec],
            [out_of(count, width), out_of(ncol - 1, count, width)],
            2 * moved * hidden,
            2 * hidden * dim + 2 * count * hidden + 6 * moved,
            "down",
        )(slots.gate(hid)[0], middle, down_offset, *down_ops)
        slots.note(own)
        up_low, up_high = ffn_kept(upward_grad, normed_two, got, "up_grad")
        slots.advance()

        with jax.named_scope("up_grad_first"):
            ug.x_high_first(up_high)
            ug.y_low_first(up_low)
        do(dg, "z_high")
        middle_grad, branch_low, attended_grad, sums_two = call(
            functools.partial(middle_pull_kernel, up_dims, out_layout),
            (seqs,),
            [hidden_spec, tokens_spec, tokens_spec, vector_spec] + up_specs + out_specs,
            [tokens_spec, tokens_spec, tile((LEN, flat)), summed((4, dim))],
            [
                out_of(count, dim, dtype=f32),
                out_of(count, dim),
                out_of(count, flat),
                out_of(4, dim, dtype=f32),
            ],
            2 * moved * (hidden + flat),
            2 * hidden * dim + 2 * count * hidden + 14 * moved,
            "middle_pull",
            scratch=out_scratch,
        )(slots.gate(upward_grad)[0], middle, grad_low, gain_two, *up_ops, *out_ops)
        slots.note(attended_grad)
        slots.advance()

        do(ug, "y_high", "x_low")
        do(dg, "z_low")
        far = pull(nrow // 2, nrow // 2)
        slots.note(far)
        slots.advance()

        do(ug, "z_high")
        activations = TokensOut("activations", slots, own, other)
        do(activations, "send")
        far_sums, (far_own,) = head_grad(slots.gate(far)[0], normed, nrow // 2, "qkv_grad", True)
        far_held = core_fold("qkv_grad_far", far_sums)
        near = pull(0, nrow // 2)
        slots.note(near)
        slots.advance()

        with jax.named_scope("qkv_grad_x"):
            arrays = slots.gate(*far_held)
            got = slots.move(total([view_of(array) for array in arrays]).astype(bf16), "row", nrow // 2)
        do(ug, "z_low")
        near_sums, (near_own,) = head_grad(slots.gate(near)[0], normed, 0, "qkv_grad", True)
        near_held = core_fold("qkv_grad_near", near_sums)
        out_sums, _ = head_grad(slots.gate(attended)[0][None], branch_low, 0, "out_grad")
        out_held = core_fold("out_grad", out_sums)
        slots.advance()

        qg.halve(near_held + [got])
        if nrow > 2:
            do(qg, "x_high", "x_low")
        do(qg, "y_high", "y_low")
        og.halve(out_held)
        do(og, "x_high", "x_low")
        own_grad, other_grad, sums_one = call(
            functools.partial(token_pull_kernel, ncol, qkv_layout),
            (seqs,),
            [pl.BlockSpec((3, LEN, flat // 2), lambda t: (0, t, 0))] * 2
            + [tokens_spec, tokens_spec, vector_spec]
            + qkv_specs,
            [own_spec, other_spec, summed((2, dim))],
            [
                out_of(count, width, dtype=f32),
                out_of(ncol - 1, count, width),
                out_of(2, dim, dtype=f32),
            ],
            6 * moved * flat,
            6 * flat * dim + 14 * moved,
            "token_pull",
            scratch=qkv_scratch,
        )(slots.gate(near)[0], far, inputs, middle_grad, gain_one, *qkv_ops)
        slots.note(own_grad)
        slots.advance()

        bias_sum = jnp.concatenate([near_own, far_own], axis=2)[::2].reshape(2, nrow, part, ncore, nz, piece)
        bias_sum = jnp.transpose(bias_sum, (3, 1, 4, 0, 2, 5)).reshape(ncore, nrow, nz, qkv_count)
        bias_sum = jnp.concatenate([bias_sum, up_bias_sum.reshape(ncore, nrow, nz, hidden_part)], axis=-1)
        sums = jnp.concatenate([sums_one, sums_two])
        size = sums.shape[0] * width
        flat_bias = bias_sum.reshape(-1)
        packs = [jnp.concatenate([sums[:, :width].reshape(-1), flat_bias])]

        def small_sums(axis):
            (pack,) = slots.gate(packs[0])
            if axis == "col":
                for k in range(1, ncol):
                    far = sums[:, k * width : (k + 1) * width].reshape(-1)
                    packs[0] = packs[0] + slots.send(jnp.concatenate([far, flat_bias]), axis, k)
                return
            for bit in reversed(bits(axis)):
                rest = pack[size:]
                half = rest.size // 2
                got = slots.move(jnp.concatenate([pack[:size], rest[half:]]), axis, bit)
                pack = pack[: size + half] + got
            packs[0] = pack

        token_grad = TokensOut("token_grad", slots, own_grad, other_grad)
        do(qg, "z_high")
        do(og, "y_high", "y_low")
        do(token_grad, "send")
        small_sums("col")
        slots.advance()

        do(qg, "z_low")
        do(og, "z_high")
        small_sums("core")
        slots.advance()

        do(og, "z_low")
        small_sums("row")
        slots.advance()

        small_sums("z")
        activations, token_grad = activations.end(), token_grad.end()
        down_grad, up_grad, out_grad, qkv_grad = dg.result(), ug.result(), og.result(), qg.result()

        pack = packs[0]
        sums = pack[:size].reshape(-1, width)
        bias_sum = pack[size:]
        return (
            activations,
            token_grad,
            sums[0],
            sums[1],
            qkv_grad,
            bias_sum[:qkv_count].reshape(qkv_bias.shape),
            out_grad[0],
            sums[2],
            sums[3],
            sums[4],
            up_grad,
            bias_sum[qkv_count:],
            down_grad,
            sums[5],
        )

    return local


def solution(mesh):
    devices = mesh.devices
    nz, ncore = devices.shape[0] // 2, 2
    nrow, ncol = devices.shape[1], devices.shape[2]
    fine = Mesh(devices.reshape(nz, ncore, nrow, ncol), ("z", "core", "row", "col"))
    dp = ("z", "core")
    rows = P(("z", "core", "row"), "col")
    qkv_weight = P(None, "row", dp, "col")
    qkv_bias = P(None, "row", dp)
    out_weight = P("row", dp, "col")
    feature = P("col")
    unit = P(("z", "core", "row"))
    in_specs = (
        rows,
        P(("z", "core", "col"), None),
        feature,
        feature,
        qkv_weight,
        qkv_bias,
        out_weight,
        feature,
        feature,
        feature,
        rows,
        unit,
        rows,
        feature,
        rows,
    )
    out_specs = (
        rows,
        rows,
        feature,
        feature,
        qkv_weight,
        qkv_bias,
        out_weight,
        feature,
        feature,
        feature,
        rows,
        unit,
        rows,
        feature,
    )
    return jax.shard_map(
        make_local(nz, ncore, nrow, ncol),
        mesh=fine,
        in_specs=in_specs,
        out_specs=out_specs,
        check_vma=False,
    )
```

```python
import functools
import itertools

import jax
import jax.numpy as jnp
from jax import lax
from jax.experimental import pallas as pl
from jax.experimental.pallas import tpu as pltpu
from jax.sharding import Mesh, PartitionSpec as P

HD = 64
HELD = 4
QUAD = HELD * HD
STEP = 2
BUF = 64
LEN = 320
masked_fill = -1000000000.0
norm_epsilon = 1e-06
attn_scale = 0.125
exp2_scale = attn_scale * 1.4426950408889634
root_half = 0.7071067811865476
density = 0.3989422804014327
bf16 = jnp.bfloat16
f32 = jnp.float32
MIB = 1 << 20


def contract_last(left, right):
    return lax.dot_general(left, right, (((1,), (1,)), ((), ())), preferred_element_type=f32)


def contract_first(left, right):
    return lax.dot_general(left, right, (((0,), (0,)), ((), ())), preferred_element_type=f32)


def matmul(left, right):
    return lax.dot_general(left, right, (((1,), (0,)), ((), ())), preferred_element_type=f32)


def whole(shape):
    return pl.BlockSpec(shape, lambda *_: (0,) * len(shape), pipeline_mode=pl.Buffered(1))


def summed(shape):
    return pl.BlockSpec(shape, lambda *_: (0,) * len(shape))


def call(kernel, grid, in_specs, out_specs, out_shape, flops, moved, name, vmem=48, scratch=()):
    return pl.pallas_call(
        kernel,
        grid=grid,
        in_specs=in_specs,
        out_specs=out_specs,
        out_shape=out_shape,
        scratch_shapes=scratch,
        name=name,
        compiler_params=pltpu.CompilerParams(vmem_limit_bytes=vmem * MIB),
        cost_estimate=pl.CostEstimate(flops=flops, bytes_accessed=moved, transcendentals=0),
    )


def unit_norm(values):
    center = jnp.mean(values, axis=1, keepdims=True)
    centered = values - center
    spread = jnp.mean(centered * centered, axis=1, keepdims=True)
    inverse = lax.rsqrt(spread + norm_epsilon)
    return centered * inverse, inverse


def norm_pull(grad, gain, unit, inverse):
    scaled = grad * gain
    total = jnp.mean(scaled, axis=1, keepdims=True)
    paired = jnp.mean(scaled * unit, axis=1, keepdims=True)
    return inverse * (scaled - total - unit * paired)


def head_weight(layout, refs):
    if layout is None:
        return refs[1:], lambda: None, lambda i: refs[0][i]
    places, kinds = layout
    held, sem = refs[-2:]
    operands = 1 + max(place[0] for place in places)

    def copies(kind):
        for operand, index, head, row, lane in places:
            source = refs[operand].at[index + (kind,)]
            part, piece, width = source.shape
            target = held.at[kind, pl.ds(head, part), pl.ds(row, piece), pl.ds(lane, width)]
            yield pltpu.make_async_copy(source, target, sem.at[kind])

    def fetch():
        @pl.when(pl.program_id(0) == 0)
        def _():
            for kind in range(kinds):
                for copy in copies(kind):
                    copy.start()

    def read(kind):
        @pl.when(pl.program_id(0) == 0)
        def _():
            for copy in copies(kind):
                copy.wait()

        return held[kind].reshape(held.shape[1] * held.shape[2], held.shape[3])

    return refs[operands:-2], fetch, read


def qkv_kernel(layout, x_ref, gain_ref, shift_ref, bias_ref, *refs):
    (a_ref, out_ref), fetch, read = head_weight(layout, refs)
    fetch()
    unit, _ = unit_norm(x_ref[...].astype(f32))
    a = (unit * gain_ref[...] + shift_ref[...]).astype(bf16)
    a_ref[...] = a
    for i in range(3):
        value = contract_last(a, read(i))
        if i != 1:
            value = value + bias_ref[i // 2 : i // 2 + 1]
        out_ref[i] = value.astype(bf16)


def split_heads(held):
    head = lax.broadcasted_iota(jnp.int32, held.shape, 1) // HD
    zero = jnp.zeros_like(held)
    return jnp.concatenate([jnp.where(head == h, held, zero) for h in range(HELD)], axis=0)


def join_heads(all_heads):
    rows = all_heads.shape[0] // HELD
    head = lax.broadcasted_iota(jnp.int32, (rows, all_heads.shape[1]), 1) // HD
    value = all_heads[:rows]
    for h in range(1, HELD):
        value = jnp.where(head == h, all_heads[h * rows : (h + 1) * rows], value)
    return value


def attend_kernel(qkv_ref, mask_ref, out_ref, probs_ref):
    seen = mask_ref[0] > 0
    for n in range(STEP):
        lanes = slice(n * QUAD, (n + 1) * QUAD)
        scores = contract_last(qkv_ref[1, :, lanes], split_heads(qkv_ref[0, :, lanes]))
        scores = jnp.where(seen, scores, masked_fill / attn_scale)
        top = jnp.max(scores, axis=0, keepdims=True)
        grown = jnp.exp2((scores - top) * exp2_scale)
        probs = (grown * (1.0 / jnp.sum(grown, axis=0, keepdims=True))).astype(bf16)
        probs_ref[0, n] = probs
        out_ref[:, lanes] = join_heads(contract_first(probs, qkv_ref[2, :, lanes])).astype(bf16)


def attend_pull_kernel(seqs, sizes, qkv_ref, probs_ref, do_ref, normed_ref, out_ref, *refs):
    ncore, ncol, nz, part, piece = sizes
    sum_refs, (sum_ref, held) = refs[:ncore], refs[ncore:]
    at = pl.program_id(0)
    rows = held.shape[2] // (part * HD)

    @pl.when(at < seqs)
    def _():
        place = pl.ds(pl.multiple_of(at * LEN, LEN), LEN)
        for n in range(STEP):
            lanes = slice(n * QUAD, (n + 1) * QUAD)
            queries = split_heads(qkv_ref[0, :, lanes])
            keys = qkv_ref[1, :, lanes]
            pulled = split_heads(do_ref[:, lanes])
            low = probs_ref[0, n]
            probs = low.astype(f32)
            prob_grad = contract_last(qkv_ref[2, :, lanes], pulled)
            inner = jnp.sum(prob_grad * probs, axis=0, keepdims=True)
            score_grad = (probs * (prob_grad - inner)).astype(bf16)
            value_grad = matmul(low, pulled).astype(bf16)
            key_grad = (matmul(score_grad, queries) * attn_scale).astype(bf16)
            query_grad = join_heads(contract_first(score_grad, keys) * attn_scale).astype(bf16)
            for i, value in enumerate((query_grad, key_grad, value_grad)):
                out_ref[i, :, lanes] = value
                held[i, place, lanes] = value

    @pl.when(at >= seqs)
    def _():
        width = normed_ref.shape[1] // ncol
        kind, row = (at - seqs) // rows, (at - seqs) % rows
        size = part * HD
        left = held[kind, :, pl.ds(pl.multiple_of(row * size, size), size)] if rows > 1 else held[kind]
        for c in range(ncol):
            value = contract_first(left, normed_ref[:, c * width : (c + 1) * width]).astype(bf16)
            value = value.reshape(part, ncore, nz, piece, width)
            for core in range(ncore):
                for z in range(nz):
                    sum_refs[core][0, c, z, 0] = value[:, core, z]
        sum_ref[0] = jnp.sum(left.astype(f32), axis=0, keepdims=True)


def out_kernel(layout, x_ref, o_ref, bias_ref, gain_ref, shift_ref, *refs):
    (middle_ref, a_ref), fetch, read = head_weight(layout, refs)
    fetch()
    middle = x_ref[...].astype(f32) + (matmul(o_ref[...], read(0)) + bias_ref[...])
    middle_ref[...] = middle
    unit, _ = unit_norm(middle)
    a_ref[...] = (unit * gain_ref[...] + shift_ref[...]).astype(bf16)


def pieces_of(dims, refs):
    ncol, nrow, ncore, places = dims
    w_refs, rest = refs[: len(places)], refs[len(places) :]

    def piece(block, col):
        core, within = divmod(block, 2 * nrow)
        row, half = divmod(within, 2)
        lead, second = (row, col) if half else (col, row)
        for ref, (in_core, in_half, first) in zip(w_refs, places):
            if (in_core, in_half) == (core, half) and first <= lead < first + ref.shape[0]:
                return ref[lead - first, second]

    return piece, 2 * ncore * nrow, w_refs[0].shape[2], w_refs[0].shape[3], rest


def up_kernel(dims, a_ref, bias_ref, *refs):
    piece, blocks, step, width, (hid_ref, slope_ref) = pieces_of(dims, refs)
    for b in range(blocks):
        rows = slice(b * step, (b + 1) * step)
        value = bias_ref[:, rows]
        for c in range(dims[0]):
            value = value + contract_last(a_ref[:, c * width : (c + 1) * width], piece(b, c))
        cdf = 0.5 + 0.5 * lax.erf(value * root_half)
        pdf = jnp.exp(-0.5 * value * value) * density
        hid_ref[:, rows] = (value * cdf).astype(bf16)
        slope_ref[:, rows] = (cdf + value * pdf).astype(bf16)


def down_kernel(dims, hid_ref, middle_ref, bias_ref, *refs):
    piece, blocks, step, width, (own_ref, other_ref) = pieces_of(dims, refs)
    for c in range(dims[0]):
        lanes = slice(c * width, (c + 1) * width)
        value = middle_ref[:, lanes] + bias_ref[:, lanes]
        for b in range(blocks):
            value = value + matmul(hid_ref[:, b * step : (b + 1) * step], piece(b, c))
        if c == 0:
            own_ref[...] = value.astype(bf16)
        else:
            other_ref[c - 1] = value.astype(bf16)


def hidden_pull_kernel(dims, g_ref, slope_ref, *refs):
    piece, blocks, step, width, (du_ref, sum_ref) = pieces_of(dims, refs)

    @pl.when(pl.program_id(0) == 0)
    def _():
        sum_ref[...] = jnp.zeros_like(sum_ref)

    for b in range(blocks):
        rows = slice(b * step, (b + 1) * step)
        value = contract_last(g_ref[:, :width], piece(b, 0))
        for c in range(1, dims[0]):
            value = value + contract_last(g_ref[:, c * width : (c + 1) * width], piece(b, c))
        low = (value * slope_ref[:, rows].astype(f32)).astype(bf16)
        du_ref[:, rows] = low
        sum_ref[:, rows] += jnp.sum(low.astype(f32), axis=0, keepdims=True)


def middle_pull_kernel(dims, layout, du_ref, middle_ref, g_ref, gain_ref, *refs):
    piece, blocks, step, width, rest = pieces_of(dims, refs)
    (grad_ref, low_ref, do_ref, sum_ref), fetch, read = head_weight(layout, rest)
    fetch()

    @pl.when(pl.program_id(0) == 0)
    def _():
        sum_ref[...] = jnp.zeros_like(sum_ref)

    parts = []
    for c in range(dims[0]):
        value = matmul(du_ref[:, :step], piece(0, c))
        for b in range(1, blocks):
            value = value + matmul(du_ref[:, b * step : (b + 1) * step], piece(b, c))
        parts.append(value)
    grad = jnp.concatenate(parts, axis=1)
    unit, inverse = unit_norm(middle_ref[...])
    out_grad = g_ref[...].astype(f32)
    total = out_grad + norm_pull(grad, gain_ref[...], unit, inverse)
    grad_ref[...] = total
    low = total.astype(bf16)
    low_ref[...] = low
    do_ref[...] = contract_last(low, read(0)).astype(bf16)
    sum_ref[0:1] += jnp.sum(low.astype(f32), axis=0, keepdims=True)
    sum_ref[1:2] += jnp.sum(grad * unit, axis=0, keepdims=True)
    sum_ref[2:3] += jnp.sum(grad, axis=0, keepdims=True)
    sum_ref[3:4] += jnp.sum(out_grad, axis=0, keepdims=True)


def token_pull_kernel(ncol, layout, near_ref, far_ref, x_ref, grad_ref, gain_ref, *refs):
    (own_ref, other_ref, sum_ref), fetch, read = head_weight(layout, refs)
    fetch()

    @pl.when(pl.program_id(0) == 0)
    def _():
        sum_ref[...] = jnp.zeros_like(sum_ref)

    grad = None
    for i in range(3):
        weight = read(i)
        middle = weight.shape[0] // 2
        value = matmul(near_ref[i], weight[:middle]) + matmul(far_ref[i], weight[middle:])
        grad = value if grad is None else grad + value
    unit, inverse = unit_norm(x_ref[...].astype(f32))
    total = grad_ref[...] + norm_pull(grad, gain_ref[...], unit, inverse)
    width = total.shape[1] // ncol
    own_ref[...] = total[:, :width]
    for c in range(1, ncol):
        other_ref[c - 1] = total[:, c * width : (c + 1) * width].astype(bf16)
    sum_ref[0:1] += jnp.sum(grad * unit, axis=0, keepdims=True)
    sum_ref[1:2] += jnp.sum(grad, axis=0, keepdims=True)


def ffn_sent_kernel(ncol, l_ref, r_ref, out_ref):
    width = r_ref.shape[1] // ncol
    left = l_ref[...]
    for c in range(ncol):
        out_ref[0, 0, c] = contract_first(left, r_ref[:, c * width : (c + 1) * width]).astype(bf16)


def ffn_kept_kernel(ncol, nrow, l_ref, r_ref, got_ref, *out_refs):
    by_col, by_row = out_refs[:ncol], out_refs[ncol:]
    width = r_ref.shape[1] // ncol
    left = l_ref[...]
    half, row = pl.program_id(0), pl.program_id(1)
    values = []
    for c in range(ncol):
        value = contract_first(left, r_ref[:, c * width : (c + 1) * width])
        values.append((value + got_ref[0, 0, c].astype(f32)).astype(bf16))

    @pl.when(half == 0)
    def _():
        for c in range(ncol):
            by_col[c][0] = values[c]

    for r in range(nrow):

        @pl.when((half == 1) & (row == r))
        def _(r=r):
            for c in range(ncol):
                by_row[r][c] = values[c]


def head_grad_kernel(sizes, l_ref, r_ref, *refs):
    ncore, ncol, nz, part, piece = sizes
    width = r_ref.shape[1] // ncol
    left = l_ref[0]
    for c in range(ncol):
        value = contract_first(left, r_ref[:, c * width : (c + 1) * width]).astype(bf16)
        value = value.reshape(part, ncore, nz, piece, width)
        for core in range(ncore):
            for z in range(nz):
                refs[core][0, c, z, 0] = value[:, core, z]
    for sum_ref in refs[ncore:]:
        sum_ref[0] = jnp.sum(left.astype(f32), axis=0, keepdims=True)


def make_local(nz, ncore, nrow, ncol):
    blocks = ncore * nrow
    sizes = {"z": nz, "core": ncore, "row": nrow, "col": ncol}

    def bits(axis):
        return [1 << k for k in range(sizes[axis].bit_length() - 1)]

    def exchange(values, axis, bit):
        return lax.ppermute(values, axis, [(i, i ^ bit) for i in range(sizes[axis])])

    class Slots:
        def __init__(self):
            self.before, self.now = [], []

        def advance(self):
            self.before, self.now = self.now, []

        def note(self, *values):
            self.now.extend(values)

        def gate(self, *values):
            if not self.before:
                return values
            return lax.optimization_barrier((*values, *self.before))[: len(values)]

        def move(self, values, axis, bit):
            got = exchange(values, axis, bit)
            self.now.append(got)
            return got

        def send(self, values, axis, bit):
            return self.move(self.gate(values)[0], axis, bit)

        def widen(self, parts, axis, lead=True):
            parts = list(self.gate(*parts))
            if lead:
                parts = [joined(parts)[None]]
            for bit in bits(axis):
                values = joined(parts)
                parts = [values, self.move(values, axis, bit)]
            return parts

        def fold(self, held, axis, dim):
            arrays = self.gate(*[view[0] for view in held])
            held = [(array, view[1]) for array, view in zip(arrays, held)]
            for bit in [bit for bit in reversed(bits(axis)) if bit < held[0][1][dim][1]]:
                got = self.move(total([half_of(view, dim, 1) for view in held]).astype(bf16), axis, bit)
                held = [half_of(view, dim, 0) for view in held] + [view_of(got)]
            return held

    def joined(parts):
        return parts[0] if len(parts) == 1 else jnp.concatenate(parts)

    def view_of(array):
        return (array, tuple((0, n) for n in array.shape[:3]))

    def half_of(view, dim, which):
        array, spans = view
        start, size = spans[dim]
        size //= 2
        return (array, spans[:dim] + ((start + which * size, size),) + spans[dim + 1 :])

    def total(held):
        value = None
        for array, spans in held:
            part = array[tuple(slice(start, start + size) for start, size in spans)].astype(f32)
            value = part if value is None else value + part
        return value

    class Gather:
        together = None

        def __init__(self, name, slots, shard):
            self.name, self.slots, self.low = name, slots, [shard[None]]

        def z_all(self):
            (values,) = self.slots.gate(*self.low)
            near = nz // 2
            parts = [values] + [self.slots.move(values, "z", k) for k in range(1, nz)]
            self.low, self.high = parts[:near], parts[near:]

        def z_low(self):
            parts = list(self.slots.gate(*self.low))
            for bit in bits("z")[:-1]:
                values = joined(parts)
                parts = [values, self.slots.move(values, "z", bit)]
            self.low = parts

        def z_high(self):
            values = joined(list(self.slots.gate(*self.low)))
            self.low = [values]
            self.high = [self.slots.move(values, "z", bits("z")[-1])]

        def z_high_first(self):
            values = joined(list(self.slots.gate(*self.low)))
            half = values.shape[0] // 2
            self.low = [values[:half], values[half:]]
            self.high = [self.slots.move(self.low[0], "z", bits("z")[-1])]

        def z_high_second(self):
            (values,) = self.slots.gate(self.low[1])
            self.high.append(self.slots.move(values, "z", bits("z")[-1]))

        def x_low(self):
            self.low_row = self.slots.widen(self.low, "row")

        def y_high(self):
            self.high_col = self.slots.widen(self.high, "col")

        def y_low(self):
            self.low_all = self.slots.widen(self.low_row, "col")

        def x_high(self):
            self.high_all = self.slots.widen(self.high_col, "row")

        def y(self):
            self.all_col = self.slots.widen(self.low + self.high, "col")

        def x(self):
            self.all_row = self.slots.widen(self.all_col, "row")

        def core(self):
            if hasattr(self, "all_row"):
                lists = [(2, self.all_row)]
            else:
                lists = [(0, self.low_all), (1, self.high_all)]
            self.places, self.pieces = [], []
            for half, parts in lists:
                parts = self.slots.gate(*parts)
                if half == self.together:
                    parts = [joined(list(parts))]
                for k in range(ncore):
                    first = 0
                    for values in parts:
                        self.places.append((k, half, first))
                        self.pieces.append(self.slots.move(values, "core", k) if k else values)
                        first += values.shape[0]

    class Scatter:
        def __init__(self, name, slots):
            self.name, self.slots, self.low, self.high = name, slots, [], []

        def halve(self, arrays):
            views = [view_of(array) for array in arrays]
            self.low = self.low + [half_of(view, 2, 0) for view in views]
            self.high = self.high + [half_of(view, 2, 1) for view in views]

        def first_fold(self, parts, axis, dim):
            parts = list(self.slots.gate(*parts))
            held = []
            for bit in reversed(bits(axis)):
                value = parts[bit] if bit == 1 else jnp.concatenate(parts[bit : 2 * bit], axis=dim)
                if held:
                    value = (value.astype(f32) + total([half_of(view, dim, 1) for view in held])).astype(bf16)
                got = self.slots.move(value, axis, bit)
                held = [half_of(view, dim, 0) for view in held] + [view_of(got)]
            return [view_of(parts[0])] + held

        def x_high_first(self, by_row):
            self.high = self.first_fold(by_row, "row", 0)

        def y_low_first(self, by_col):
            self.low = self.first_fold(by_col, "col", 1)

        def x_high(self):
            self.high = self.slots.fold(self.high, "row", 0)

        def y_low(self):
            self.low = self.slots.fold(self.low, "col", 1)

        def y_high(self):
            self.high = self.slots.fold(self.high, "col", 1)

        def x_low(self):
            self.low = self.slots.fold(self.low, "row", 0)

        def z_high(self):
            arrays = self.slots.gate(*[view[0] for view in self.high])
            value = total([(array, view[1]) for array, view in zip(arrays, self.high)])
            self.low = self.low + [view_of(self.slots.move(value.astype(bf16), "z", nz // 2))]

        def z_low(self):
            arrays = self.slots.gate(*[view[0] for view in self.low])
            held = [(array, view[1]) for array, view in zip(arrays, self.low)]
            for bit in reversed(bits("z")[:-1]):
                got = self.slots.move(total([half_of(view, 2, 1) for view in held]).astype(bf16), "z", bit)
                held = [half_of(view, 2, 0) for view in held] + [view_of(got)]
            self.low = held

        def result(self):
            arrays = self.slots.gate(*[view[0] for view in self.low])
            return total([(array, view[1]) for array, view in zip(arrays, self.low)])[0, 0, 0]

    class TokensIn:
        def __init__(self, name, slots, values):
            self.name, self.slots, self.parts, self.blocks = name, slots, [], []
            rows = values.shape[0] // ncol
            here = lax.axis_index("col")
            size = rows // 2
            for which in range(2):
                starts = [(here ^ k) * rows + which * size for k in range(ncol)]
                self.blocks.append([lax.dynamic_slice_in_dim(values, start, size, 0) for start in starts])

        def step(self, which):
            own, *sent = self.blocks[which]
            sent = self.slots.gate(*sent)
            self.parts.append([own] + [self.slots.move(block, "col", k + 1) for k, block in enumerate(sent)])

        def first(self):
            self.step(0)

        def second(self):
            self.step(1)

        def end(self):
            count = len(self.parts[0])
            flat = self.slots.gate(*[part for parts in self.parts for part in parts])
            rows = [jnp.concatenate(flat[i : i + count], axis=1) for i in range(0, len(flat), count)]
            return jnp.concatenate(rows)

    def do(job, *stages):
        for stage in stages:
            with jax.named_scope(job.name + "_" + stage):
                getattr(job, stage)()

    class TokensOut:
        def __init__(self, name, slots, own, other):
            self.name, self.slots, self.own, self.other = name, slots, own, other

        def send(self):
            self.blocks = [self.slots.send(self.other[k - 1], "col", k) for k in range(1, ncol)]

        def end(self):
            rows = self.own.shape[0]
            here = lax.axis_index("col")
            first, *rest = self.slots.gate(self.own, *self.blocks)
            result = jnp.zeros((rows * ncol, self.own.shape[1]), self.own.dtype)
            result = lax.dynamic_update_slice_in_dim(result, first, here * rows, 0)
            for k, block in enumerate(rest):
                result = lax.dynamic_update_slice_in_dim(
                    result, block.astype(self.own.dtype), (here ^ (k + 1)) * rows, 0
                )
            return result

    def local(
        tokens,
        key_mask,
        first_gain,
        first_shift,
        qkv_weight,
        qkv_bias,
        out_weight,
        out_bias,
        second_gain,
        second_shift,
        up_weight,
        up_bias,
        down_weight,
        down_bias,
        cotangent,
    ):
        count = tokens.shape[0] // ncol
        seqs = count // LEN
        part, piece, width = out_weight.shape
        heads = part * nrow
        flat = heads * HD
        hidden_part = up_weight.shape[0]
        step = nz * hidden_part
        dim = width * ncol
        hidden = step * blocks
        pairs = heads // 2
        moved = count * dim

        def tile(shape, index=None):
            return pl.BlockSpec(shape, index or (lambda t: (t,) + (0,) * (len(shape) - 1)))

        slots = Slots()
        q = Gather("qkv", slots, qkv_weight.astype(bf16))
        o = Gather("out", slots, out_weight[None].astype(bf16))
        u = Gather("up", slots, up_weight.astype(bf16))
        d = Gather("down", slots, down_weight.astype(bf16))
        tok = TokensIn("tokens", slots, tokens)
        cot = TokensIn("cotangent", slots, cotangent)
        small = [jnp.concatenate([qkv_bias.reshape(-1), up_bias]).astype(bf16)[None]]
        vectors = jnp.stack([first_gain, first_shift, second_gain, second_shift, out_bias, down_bias])

        do(q, "z_all")
        do(tok, "first")
        vectors = slots.widen([vectors], "col")
        slots.advance()
        do(q, "x_low", "y_high")
        do(o, "z_low")
        do(u, "z_low")
        small = slots.widen(small, "z", False)
        slots.advance()
        do(q, "y_low", "x_high")
        do(o, "z_high")
        do(u, "z_high_first")
        small = slots.widen(small, "row")
        nearby = slots.widen([key_mask], "col")
        slots.advance()
        do(q, "core")
        do(u, "z_high_second")
        do(tok, "second")
        do(o, "y")
        small = slots.widen(small, "core")
        slots.advance()
        inputs = tok.end()
        vectors = jnp.transpose(joined(list(slots.gate(*vectors))), (1, 0, 2)).reshape(6, dim)
        gain_one, shift_one, gain_two, shift_two, out_offset, down_offset = [vectors[i : i + 1] for i in range(6)]
        small_all = joined(list(slots.gate(*small))).astype(f32)
        qkv_count = qkv_bias.size
        qkv_offset = small_all[..., :qkv_count].reshape(ncore, nrow, nz, 2, part, piece)
        qkv_offset = jnp.transpose(qkv_offset, (3, 1, 4, 0, 2, 5)).reshape(2, flat)
        up_offset = small_all[..., qkv_count:].reshape(1, hidden)
        here = lax.axis_index("col")
        nearby = joined(nearby)
        masks = jnp.zeros_like(nearby)
        for k in range(ncol):
            masks = lax.dynamic_update_slice_in_dim(masks, nearby[k : k + 1], here ^ k, 0)
        masks = masks.reshape(-1, key_mask.shape[1])
        first_seq = (lax.axis_index("row") * ncol + here) * seqs
        masks = lax.dynamic_slice_in_dim(masks, first_seq, seqs, 0)
        visible = jnp.concatenate([jnp.ones((seqs, BUF), jnp.int32), masks], axis=1)

        def head_operands(w, kinds):
            half = nz // 2
            places = []
            for k, r, c, z in itertools.product(range(ncore), range(nrow), range(ncol), range(nz)):
                for n, ((in_core, in_half, first), values) in enumerate(zip(w.places, w.pieces)):
                    lead, second, inner = (c, r, z) if in_half == 0 else (r, c, z - half * (in_half == 1))
                    held = in_half == 2 or in_half == z // half
                    if held and in_core == k and first <= lead < first + values.shape[0]:
                        index = (lead - first, second, inner)
                        places.append((n, index, r * part, (k * nz + z) * piece, c * width))
            if piece % 8 == 0:
                specs = [pl.BlockSpec(memory_space=pl.ANY)] * len(w.pieces)
                scratch = [pltpu.VMEM((kinds, heads, HD, dim), bf16), pltpu.SemaphoreType.DMA((kinds,))]
                return w.pieces, specs, scratch, (tuple(places), kinds)
            matrix = jnp.zeros((kinds, heads, HD, dim), bf16)
            for n, index, head, row, lane in places:
                matrix = lax.dynamic_update_slice(matrix, w.pieces[n][index], (0, head, row, lane))
            return [matrix.reshape(kinds, flat, dim)], [whole((kinds, flat, dim))], [], None

        qkv_ops, qkv_specs, qkv_scratch, qkv_layout = head_operands(q, 3)

        tokens_spec = tile((LEN, dim))
        hidden_spec = tile((LEN, hidden))
        half_step = step // 2
        vector_spec = whole((1, dim))
        three = pl.BlockSpec((3, LEN, flat), lambda t: (0, t, 0))
        own_spec = tile((LEN, width))
        other_spec = pl.BlockSpec((ncol - 1, LEN, width), lambda t: (0, t, 0))

        def out_of(*shape, dtype=bf16):
            return jax.ShapeDtypeStruct(shape, dtype)

        def ffn_operands(w):
            operands = [p.reshape(p.shape[0], p.shape[1], half_step, width) for p in w.pieces]
            return operands, [whole(p.shape) for p in operands], (ncol, nrow, ncore, tuple(w.places))

        do(u, "x_low", "y_high")
        do(o, "x")
        do(d, "z_low")
        do(cot, "first")
        normed, qkv = call(
            functools.partial(qkv_kernel, qkv_layout),
            (seqs,),
            [tokens_spec, vector_spec, vector_spec, whole((2, flat))] + qkv_specs,
            [tokens_spec, three],
            [out_of(count, dim), out_of(3, count, flat)],
            6 * moved * flat,
            6 * flat * dim + 10 * moved,
            "qkv",
            scratch=qkv_scratch,
        )(inputs, gain_one, shift_one, qkv_offset, *qkv_ops)
        slots.note(qkv)
        slots.advance()

        do(u, "y_low", "x_high")
        do(d, "z_high")
        do(o, "core")
        quads = flat // QUAD
        step_lanes = STEP * QUAD
        queries = HELD * LEN
        attended, probs = call(
            attend_kernel,
            (seqs, quads // STEP),
            [
                pl.BlockSpec((3, LEN, step_lanes), lambda s, p: (0, s, p)),
                pl.BlockSpec((1, LEN, 1), lambda s, p: (s, 0, 0)),
            ],
            [
                pl.BlockSpec((LEN, step_lanes), lambda s, p: (s, p)),
                pl.BlockSpec((1, STEP, LEN, queries), lambda s, p: (s, p, 0, 0)),
            ],
            [out_of(count, flat), out_of(seqs, quads, LEN, queries)],
            16 * count * LEN * flat,
            8 * moved + 2 * seqs * quads * LEN * queries,
            "attend",
        )(slots.gate(qkv)[0], visible[:, :, None])
        slots.note(attended)
        slots.advance()

        u.together = 0
        do(u, "core")
        do(d, "x_low", "y_high")
        out_ops, out_specs, out_scratch, out_layout = head_operands(o, 1)
        middle, normed_two = call(
            functools.partial(out_kernel, out_layout),
            (seqs,),
            [tokens_spec, tile((LEN, flat)), vector_spec, vector_spec, vector_spec] + out_specs,
            [tokens_spec, tokens_spec],
            [out_of(count, dim, dtype=f32), out_of(count, dim)],
            2 * moved * flat,
            2 * flat * dim + 10 * moved,
            "out",
            scratch=out_scratch,
        )(inputs, slots.gate(attended)[0], out_offset, gain_two, shift_two, *out_ops)
        slots.note(normed_two)
        slots.advance()

        do(d, "y_low", "x_high")
        up_ops, up_specs, up_dims = ffn_operands(u)
        hid, slope = call(
            functools.partial(up_kernel, up_dims),
            (seqs,),
            [tokens_spec, whole((1, hidden))] + up_specs,
            [hidden_spec, hidden_spec],
            [out_of(count, hidden), out_of(count, hidden)],
            8 * moved * hidden,
            2 * hidden * dim + 4 * count * hidden,
            "up",
        )(slots.gate(normed_two)[0], up_offset, *up_ops)
        slots.note(hid)
        slots.advance()

        def ffn_sent(left, right, name):
            return call(
                functools.partial(ffn_sent_kernel, ncol),
                (2, nrow),
                [
                    pl.BlockSpec((count, half_step), lambda h, r: (0, (nrow + r) * 2 + h)),
                    whole((count, dim)),
                ],
                pl.BlockSpec((1, 1, ncol, half_step, width), lambda h, r: (h, r, 0, 0, 0)),
                out_of(2, nrow, ncol, half_step, width),
                2 * moved * hidden // ncore,
                2 * (hidden * dim + count * hidden) // ncore + 2 * moved,
                name,
            )(slots.gate(left)[0], right)

        def ffn_kept(left, right, got, name):
            by_col = pl.BlockSpec((1, half_step, width), lambda h, r: (jnp.where(h == 0, r, nrow - 1), 0, 0))
            out = call(
                functools.partial(ffn_kept_kernel, ncol, nrow),
                (2, nrow),
                [
                    pl.BlockSpec((count, half_step), lambda h, r: (0, r * 2 + h)),
                    whole((count, dim)),
                    pl.BlockSpec((1, 1, ncol, half_step, width), lambda h, r: (h, r, 0, 0, 0)),
                ],
                [by_col] * ncol + [summed((ncol, half_step, width))] * nrow,
                [out_of(nrow, half_step, width)] * ncol + [out_of(ncol, half_step, width)] * nrow,
                2 * moved * hidden // ncore,
                3 * (hidden * dim + count * hidden) // ncore + 2 * moved,
                name,
            )(left, right, got)
            shape = (nz // 2, hidden_part, width)
            slots.note(out[0])
            low = [values.reshape((nrow, 1) + shape) for values in out[:ncol]]
            return low, [values.reshape((1, ncol) + shape) for values in out[ncol:]]

        def head_grad(left, right, first, name, sums=False):
            kinds, _, lanes = left.shape
            rows = lanes // (part * HD)
            out = call(
                functools.partial(head_grad_kernel, (ncore, ncol, nz, part, piece)),
                (kinds, rows),
                [
                    pl.BlockSpec((1, count, part * HD), lambda i, r: (i, 0, r)),
                    whole((count, dim)),
                ],
                [pl.BlockSpec((1, ncol, nz, 1, part, piece, width), lambda i, r: (r, 0, 0, i, 0, 0, 0))] * ncore
                + [pl.BlockSpec((1, 1, part * HD), lambda i, r: (i, 0, r))] * sums,
                [out_of(rows, ncol, nz, kinds, part, piece, width)] * ncore
                + [out_of(kinds, 1, lanes, dtype=f32)] * sums,
                2 * moved * lanes * kinds,
                2 * kinds * (lanes * dim + count * lanes) + 2 * moved,
                name,
            )(left, right)
            slots.note(out[0])
            return out[:ncore], out[ncore:]

        def core_fold(name, sums, gated=True):
            with jax.named_scope(name + "_core"):
                sent = slots.gate(*sums[1:]) if gated else sums[1:]
                return [sums[0]] + [slots.move(values, "core", k + 1) for k, values in enumerate(sent)]

        def pull(first, rows):
            lanes = rows * part * HD
            which = first // rows
            kinds = 3

            def seq(t):
                return jnp.minimum(t, seqs - 1)

            def kind_row(t):
                step_after = jnp.maximum(t - seqs, 0)
                return step_after // rows, step_after % rows

            def sums_at(t):
                kind, row = kind_row(t)
                return (row, 0, 0, kind, 0, 0, 0)

            def own_at(t):
                kind, row = kind_row(t)
                return (kind, 0, row)

            out = call(
                functools.partial(attend_pull_kernel, seqs, (ncore, ncol, nz, part, piece)),
                (seqs + kinds * rows,),
                [
                    pl.BlockSpec((kinds, LEN, lanes), lambda t: (0, seq(t), which)),
                    pl.BlockSpec((1, STEP, LEN, queries), lambda t: (seq(t), which, 0, 0)),
                    pl.BlockSpec((LEN, lanes), lambda t: (seq(t), which)),
                    whole((count, dim)),
                ],
                [pl.BlockSpec((kinds, LEN, lanes), lambda t: (0, seq(t), 0))]
                + [pl.BlockSpec((1, ncol, nz, 1, part, piece, width), sums_at)] * ncore
                + [pl.BlockSpec((1, 1, part * HD), own_at)],
                [out_of(kinds, count, lanes)]
                + [out_of(rows, ncol, nz, kinds, part, piece, width)] * ncore
                + [out_of(kinds, 1, lanes, dtype=f32)],
                30 * count * LEN * lanes + 2 * moved * lanes * kinds,
                14 * moved * rows // nrow,
                "attend_pull",
                scratch=[pltpu.VMEM((kinds, count, lanes), bf16)],
            )(qkv, probs, slots.gate(attended_grad)[0], normed)
            slots.note(out[0])
            return out[0], out[1 : 1 + ncore], out[1 + ncore]

        do(d, "core")
        do(cot, "second")
        down_ops, down_specs, down_dims = ffn_operands(d)
        own, other = call(
            functools.partial(down_kernel, down_dims),
            (seqs,),
            [hidden_spec, tokens_spec, vector_spec] + down_specs,
            [own_spec, other_spec],
            [out_of(count, width), out_of(ncol - 1, count, width)],
            2 * moved * hidden,
            2 * hidden * dim + 2 * count * hidden + 6 * moved,
            "down",
        )(hid, middle, down_offset, *down_ops)
        slots.note(own)
        slots.advance()

        dg, ug, og, qg = [Scatter(name, slots) for name in ("down_grad", "up_grad", "out_grad", "qkv_grad")]
        activations = TokensOut("activations", slots, own, other)
        do(activations, "send")
        grad_low = cot.end()
        sent = ffn_sent(hid, grad_low, "down_grad")
        (got,) = core_fold("down_grad", [sent, sent], False)[1:]
        upward_grad, up_bias_sum = call(
            functools.partial(hidden_pull_kernel, down_dims),
            (seqs,),
            [tokens_spec, hidden_spec] + down_specs,
            [hidden_spec, summed((1, hidden))],
            [out_of(count, hidden), out_of(1, hidden, dtype=f32)],
            2 * moved * hidden,
            2 * hidden * dim + 4 * count * hidden,
            "hidden_pull",
        )(slots.gate(grad_low)[0], slope, *down_ops)
        slots.note(upward_grad)
        down_low, down_high = ffn_kept(hid, grad_low, got, "down_grad")
        slots.advance()

        with jax.named_scope("down_grad_first"):
            dg.x_high_first(down_high)
            dg.y_low_first(down_low)
        sent = ffn_sent(upward_grad, normed_two, "up_grad")
        (got,) = core_fold("up_grad", [sent, sent], False)[1:]
        middle_grad, branch_low, attended_grad, sums_two = call(
            functools.partial(middle_pull_kernel, up_dims, out_layout),
            (seqs,),
            [hidden_spec, tokens_spec, tokens_spec, vector_spec] + up_specs + out_specs,
            [tokens_spec, tokens_spec, tile((LEN, flat)), summed((4, dim))],
            [
                out_of(count, dim, dtype=f32),
                out_of(count, dim),
                out_of(count, flat),
                out_of(4, dim, dtype=f32),
            ],
            2 * moved * (hidden + flat),
            2 * hidden * dim + 2 * count * hidden + 14 * moved,
            "middle_pull",
            scratch=out_scratch,
        )(slots.gate(upward_grad)[0], middle, grad_low, gain_two, *up_ops, *out_ops)
        slots.note(attended_grad)
        activations = activations.end()
        slots.note(activations)
        slots.advance()

        do(dg, "y_high", "x_low")
        up_low, up_high = ffn_kept(slots.gate(upward_grad)[0], normed_two, got, "up_grad")
        slots.advance()

        with jax.named_scope("up_grad_first"):
            ug.x_high_first(up_high)
            ug.y_low_first(up_low)
        do(dg, "z_high")
        far, far_sums, far_own = pull(nrow // 2, nrow // 2)
        slots.note(*far_sums)
        slots.advance()

        far_held = core_fold("qkv_grad_far", far_sums)
        do(ug, "y_high", "x_low")
        do(dg, "z_low")
        out_sums, _ = head_grad(slots.gate(attended)[0][None], branch_low, 0, "out_grad")
        slots.advance()

        far_low = Scatter("qkv_grad_far", slots)
        far_low.halve(far_held)
        with jax.named_scope("qkv_grad_far_x"):
            arrays = slots.gate(*[view[0] for view in far_low.high])
            value = total([(array, view[1]) for array, view in zip(arrays, far_low.high)])
            got_high = slots.move(value.astype(bf16), "row", nrow // 2)
        do(far_low, "y_low")
        do(ug, "z_high")
        out_held = core_fold("out_grad", out_sums)
        near, near_sums, near_own = pull(0, nrow // 2)
        slots.note(*near_sums)
        slots.advance()

        near_held = core_fold("qkv_grad_near", near_sums)
        with jax.named_scope("qkv_grad_far_x"):
            arrays = slots.gate(*[view[0] for view in far_low.low])
            value = total([(array, view[1]) for array, view in zip(arrays, far_low.low)])
            got_low = slots.move(value.astype(bf16), "row", nrow // 2)
        og.halve(out_held)
        do(og, "x_high", "y_low")
        down_grad = dg.result()
        slots.note(down_grad)
        slots.advance()

        qg.halve(near_held)
        qg.high = qg.high + [view_of(got_high)]
        if nrow > 2:
            do(qg, "x_high")
        do(qg, "y_high", "y_low")
        do(og, "y_high", "x_low")
        do(ug, "z_low")
        own_grad, other_grad, sums_one = call(
            functools.partial(token_pull_kernel, ncol, qkv_layout),
            (seqs,),
            [pl.BlockSpec((3, LEN, flat // 2), lambda t: (0, t, 0))] * 2
            + [tokens_spec, tokens_spec, vector_spec]
            + qkv_specs,
            [own_spec, other_spec, summed((2, dim))],
            [
                out_of(count, width, dtype=f32),
                out_of(ncol - 1, count, width),
                out_of(2, dim, dtype=f32),
            ],
            6 * moved * flat,
            6 * flat * dim + 14 * moved,
            "token_pull",
            scratch=qkv_scratch,
        )(slots.gate(near)[0], far, inputs, middle_grad, gain_one, *qkv_ops)
        slots.note(own_grad)
        slots.advance()

        bias_sum = jnp.concatenate([near_own, far_own], axis=2)[::2].reshape(2, nrow, part, ncore, nz, piece)
        bias_sum = jnp.transpose(bias_sum, (3, 1, 4, 0, 2, 5)).reshape(ncore, nrow, nz, qkv_count)
        bias_sum = jnp.concatenate([bias_sum, up_bias_sum.reshape(ncore, nrow, nz, hidden_part)], axis=-1)
        sums = jnp.concatenate([sums_one, sums_two])
        size = sums.shape[0] * width
        flat_bias = bias_sum.reshape(-1)
        packs = [jnp.concatenate([sums[:, :width].reshape(-1), flat_bias])]

        def small_sums():
            (pack,) = slots.gate(packs[0])
            for k in range(1, ncol):
                far_part = sums[:, k * width : (k + 1) * width].reshape(-1)
                pack = pack + slots.send(jnp.concatenate([far_part, flat_bias]), "col", k)
            for axis in ("core", "row", "z"):
                for bit in reversed(bits(axis)):
                    rest = pack[size:]
                    half = rest.size // 2
                    got = slots.move(jnp.concatenate([pack[:size], rest[half:]]), axis, bit)
                    pack = pack[: size + half] + got
            packs[0] = pack

        token_grad = TokensOut("token_grad", slots, own_grad, other_grad)
        do(token_grad, "send")
        qg.low = qg.low + [view_of(got_low)]
        if nrow > 2:
            do(qg, "x_low")
        do(qg, "z_high")
        do(og, "z_high")
        with jax.named_scope("small_sums"):
            small_sums()
        up_grad = ug.result()
        slots.note(up_grad)
        slots.advance()

        do(qg, "z_low")
        do(og, "z_low")
        token_grad = token_grad.end()
        out_grad, qkv_grad = og.result(), qg.result()

        pack = packs[0]
        sums = pack[:size].reshape(-1, width)
        bias_sum = pack[size:]
        return (
            activations,
            token_grad,
            sums[0],
            sums[1],
            qkv_grad,
            bias_sum[:qkv_count].reshape(qkv_bias.shape),
            out_grad[0],
            sums[2],
            sums[3],
            sums[4],
            up_grad,
            bias_sum[qkv_count:],
            down_grad,
            sums[5],
        )

    return local


def solution(mesh):
    devices = mesh.devices
    nz, ncore = devices.shape[0] // 2, 2
    nrow, ncol = devices.shape[1], devices.shape[2]
    fine = Mesh(devices.reshape(nz, ncore, nrow, ncol), ("z", "core", "row", "col"))
    dp = ("z", "core")
    rows = P(("z", "core", "row"), "col")
    qkv_weight = P(None, "row", dp, "col")
    qkv_bias = P(None, "row", dp)
    out_weight = P("row", dp, "col")
    feature = P("col")
    unit = P(("z", "core", "row"))
    in_specs = (
        rows,
        P(("z", "core", "col"), None),
        feature,
        feature,
        qkv_weight,
        qkv_bias,
        out_weight,
        feature,
        feature,
        feature,
        rows,
        unit,
        rows,
        feature,
        rows,
    )
    out_specs = (
        rows,
        rows,
        feature,
        feature,
        qkv_weight,
        qkv_bias,
        out_weight,
        feature,
        feature,
        feature,
        rows,
        unit,
        rows,
        feature,
    )
    return jax.shard_map(
        make_local(nz, ncore, nrow, ncol),
        mesh=fine,
        in_specs=in_specs,
        out_specs=out_specs,
        check_vma=False,
    )
```

```python
import functools
import itertools
import math

import jax
import jax.numpy as jnp
from jax import lax
from jax.experimental import pallas as pl
from jax.experimental.pallas import tpu as pltpu
from jax.sharding import Mesh, PartitionSpec as P

HD = 64
HELD = 4
QUAD = HELD * HD
STEP = 2
BUF = 64
LEN = 320
masked_fill = -1000000000.0
norm_epsilon = 1e-06
attn_scale = 0.125
exp2_scale = attn_scale * 1.4426950408889634
root_half = 0.7071067811865476
density = 0.3989422804014327
bf16 = jnp.bfloat16
f32 = jnp.float32
MIB = 1 << 20


def contract_last(left, right):
    return lax.dot_general(left, right, (((1,), (1,)), ((), ())), preferred_element_type=f32)


def contract_first(left, right):
    return lax.dot_general(left, right, (((0,), (0,)), ((), ())), preferred_element_type=f32)


def matmul(left, right):
    return lax.dot_general(left, right, (((1,), (0,)), ((), ())), preferred_element_type=f32)


def whole(shape):
    return pl.BlockSpec(shape, lambda *_: (0,) * len(shape), pipeline_mode=pl.Buffered(1))


def summed(shape):
    return pl.BlockSpec(shape, lambda *_: (0,) * len(shape))


def call(kernel, grid, in_specs, out_specs, out_shape, flops, moved, name, vmem=48, scratch=()):
    return pl.pallas_call(
        kernel,
        grid=grid,
        in_specs=in_specs,
        out_specs=out_specs,
        out_shape=out_shape,
        scratch_shapes=scratch,
        name=name,
        compiler_params=pltpu.CompilerParams(vmem_limit_bytes=vmem * MIB),
        cost_estimate=pl.CostEstimate(flops=flops, bytes_accessed=moved, transcendentals=0),
    )


def unit_norm(values):
    center = jnp.mean(values, axis=1, keepdims=True)
    centered = values - center
    spread = jnp.mean(centered * centered, axis=1, keepdims=True)
    inverse = lax.rsqrt(spread + norm_epsilon)
    return centered * inverse, inverse


def norm_pull(grad, gain, unit, inverse):
    scaled = grad * gain
    total = jnp.mean(scaled, axis=1, keepdims=True)
    paired = jnp.mean(scaled * unit, axis=1, keepdims=True)
    return inverse * (scaled - total - unit * paired)


def head_weight(layout, refs):
    if layout is None:
        return refs[1:], lambda: None, lambda i: refs[0][i]
    places, kinds, part = layout
    held, sem = refs[-2:]
    operands = 1 + max(place[0] for place in places)

    def copies(kind):
        for operand, index, head, row, lane in places:
            source = refs[operand].at[index + (pl.ds(kind * part, part),)]
            _, piece, width = source.shape
            target = held.at[kind, pl.ds(head, part), pl.ds(row, piece), pl.ds(lane, width)]
            yield pltpu.make_async_copy(source, target, sem.at[kind])

    def fetch():
        @pl.when(pl.program_id(0) == 0)
        def _():
            for kind in range(kinds):
                for copy in copies(kind):
                    copy.start()

    def read(kind):
        @pl.when(pl.program_id(0) == 0)
        def _():
            for copy in copies(kind):
                copy.wait()

        return held[kind].reshape(held.shape[1] * held.shape[2], held.shape[3])

    return refs[operands:-2], fetch, read


def token_tile(parts, refs):
    if parts == 1:
        return refs[0][...].astype(f32), refs[1:]
    half = parts // 2
    near = jnp.concatenate([ref[...] for ref in refs[:half]], axis=1).astype(f32)
    far = jnp.concatenate([ref[...] for ref in refs[half:parts]], axis=1).astype(f32)
    return jnp.where(pl.program_id(0) < pl.num_programs(0) // 2, near, far), refs[parts:]


def qkv_kernel(layout, parts, gain_ref, shift_ref, bias_ref, *refs):
    x, refs = token_tile(parts, refs)
    (a_ref, out_ref), fetch, read = head_weight(layout, refs)
    fetch()
    unit, _ = unit_norm(x)
    a = (unit * gain_ref[...] + shift_ref[...]).astype(bf16)
    a_ref[...] = a
    for i in range(3):
        value = contract_last(a, read(i))
        if i != 1:
            value = value + bias_ref[i // 2 : i // 2 + 1]
        out_ref[i] = value.astype(bf16)


def split_heads(held):
    head = lax.broadcasted_iota(jnp.int32, held.shape, 1) // HD
    zero = jnp.zeros_like(held)
    return jnp.concatenate([jnp.where(head == h, held, zero) for h in range(HELD)], axis=0)


def join_heads(all_heads):
    rows = all_heads.shape[0] // HELD
    head = lax.broadcasted_iota(jnp.int32, (rows, all_heads.shape[1]), 1) // HD
    value = all_heads[:rows]
    for h in range(1, HELD):
        value = jnp.where(head == h, all_heads[h * rows : (h + 1) * rows], value)
    return value


def attend_kernel(qkv_ref, mask_ref, out_ref, probs_ref):
    seen = mask_ref[0] > 0
    for n in range(STEP):
        lanes = slice(n * QUAD, (n + 1) * QUAD)
        scores = contract_last(qkv_ref[1, :, lanes], split_heads(qkv_ref[0, :, lanes]))
        scores = jnp.where(seen, scores, masked_fill / attn_scale)
        top = jnp.max(scores, axis=0, keepdims=True)
        grown = jnp.exp2((scores - top) * exp2_scale)
        probs = (grown * (1.0 / jnp.sum(grown, axis=0, keepdims=True))).astype(bf16)
        probs_ref[0, n] = probs
        out_ref[:, lanes] = join_heads(contract_first(probs, qkv_ref[2, :, lanes])).astype(bf16)


def attend_pull_kernel(seqs, sizes, qkv_ref, probs_ref, do_ref, normed_ref, out_ref, *refs):
    ncore, ncol, nz, part, piece = sizes
    sum_refs, (sum_ref, held) = refs[:ncore], refs[ncore:]
    at = pl.program_id(0)
    rows = held.shape[2] // (part * HD)

    @pl.when(at < seqs)
    def _():
        place = pl.ds(pl.multiple_of(at * LEN, LEN), LEN)
        for n in range(STEP):
            lanes = slice(n * QUAD, (n + 1) * QUAD)
            queries = split_heads(qkv_ref[0, :, lanes])
            keys = qkv_ref[1, :, lanes]
            pulled = split_heads(do_ref[:, lanes])
            low = probs_ref[0, n]
            probs = low.astype(f32)
            prob_grad = contract_last(qkv_ref[2, :, lanes], pulled)
            inner = jnp.sum(prob_grad * probs, axis=0, keepdims=True)
            score_grad = (probs * (prob_grad - inner)).astype(bf16)
            value_grad = matmul(low, pulled).astype(bf16)
            key_grad = (matmul(score_grad, queries) * attn_scale).astype(bf16)
            query_grad = join_heads(contract_first(score_grad, keys) * attn_scale).astype(bf16)
            for i, value in enumerate((query_grad, key_grad, value_grad)):
                out_ref[i, :, lanes] = value
                held[i, place, lanes] = value

    @pl.when(at >= seqs)
    def _():
        width = normed_ref.shape[1] // ncol
        kind, row = (at - seqs) // rows, (at - seqs) % rows
        size = part * HD
        left = held[kind, :, pl.ds(pl.multiple_of(row * size, size), size)] if rows > 1 else held[kind]
        for c in range(ncol):
            value = contract_first(left, normed_ref[:, c * width : (c + 1) * width]).astype(bf16)
            value = value.reshape(part, ncore, nz, piece, width)
            for core in range(ncore):
                for z in range(nz):
                    sum_refs[core][0, c, z, 0] = value[:, core, z]
        sum_ref[0] = jnp.sum(left.astype(f32), axis=0, keepdims=True)


def out_kernel(layout, parts, o_ref, bias_ref, gain_ref, shift_ref, *refs):
    x, refs = token_tile(parts, refs)
    (middle_ref, a_ref), fetch, read = head_weight(layout, refs)
    fetch()
    middle = x + (matmul(o_ref[...], read(0)) + bias_ref[...])
    middle_ref[...] = middle
    unit, _ = unit_norm(middle)
    a_ref[...] = (unit * gain_ref[...] + shift_ref[...]).astype(bf16)


def pieces_of(dims, refs):
    ncol, nrow, ncore, places = dims
    w_refs, rest = refs[: len(places)], refs[len(places) :]

    def piece(block, col):
        core, within = divmod(block, 2 * nrow)
        row, half = divmod(within, 2)
        lead, second = (row, col) if half else (col, row)
        for ref, (in_core, in_half, first) in zip(w_refs, places):
            if (in_core, in_half) == (core, half) and first <= lead < first + ref.shape[0]:
                return ref[lead - first, second]

    return piece, 2 * ncore * nrow, w_refs[0].shape[2], w_refs[0].shape[3], rest


def up_kernel(dims, a_ref, bias_ref, *refs):
    piece, blocks, step, width, (hid_ref, slope_ref) = pieces_of(dims, refs)
    for b in range(blocks):
        rows = slice(b * step, (b + 1) * step)
        value = bias_ref[:, rows]
        for c in range(dims[0]):
            value = value + contract_last(a_ref[:, c * width : (c + 1) * width], piece(b, c))
        cdf = 0.5 + 0.5 * lax.erf(value * root_half)
        pdf = jnp.exp(-0.5 * value * value) * density
        hid_ref[:, rows] = (value * cdf).astype(bf16)
        slope_ref[:, rows] = (cdf + value * pdf).astype(bf16)


def down_kernel(dims, hid_ref, middle_ref, bias_ref, *refs):
    piece, blocks, step, width, (own_ref, other_ref) = pieces_of(dims, refs)
    for c in range(dims[0]):
        lanes = slice(c * width, (c + 1) * width)
        value = middle_ref[:, lanes] + bias_ref[:, lanes]
        for b in range(blocks):
            value = value + matmul(hid_ref[:, b * step : (b + 1) * step], piece(b, c))
        if c == 0:
            own_ref[...] = value.astype(bf16)
        else:
            other_ref[c - 1] = value.astype(bf16)


def hidden_pull_kernel(dims, g_ref, slope_ref, *refs):
    piece, blocks, step, width, (du_ref, sum_ref) = pieces_of(dims, refs)

    @pl.when(pl.program_id(0) == 0)
    def _():
        sum_ref[...] = jnp.zeros_like(sum_ref)

    for b in range(blocks):
        rows = slice(b * step, (b + 1) * step)
        value = contract_last(g_ref[:, :width], piece(b, 0))
        for c in range(1, dims[0]):
            value = value + contract_last(g_ref[:, c * width : (c + 1) * width], piece(b, c))
        low = (value * slope_ref[:, rows].astype(f32)).astype(bf16)
        du_ref[:, rows] = low
        sum_ref[:, rows] += jnp.sum(low.astype(f32), axis=0, keepdims=True)


def middle_pull_kernel(dims, layout, du_ref, middle_ref, g_ref, gain_ref, *refs):
    piece, blocks, step, width, rest = pieces_of(dims, refs)
    (grad_ref, low_ref, do_ref, sum_ref), fetch, read = head_weight(layout, rest)
    fetch()

    @pl.when(pl.program_id(0) == 0)
    def _():
        sum_ref[...] = jnp.zeros_like(sum_ref)

    parts = []
    for c in range(dims[0]):
        value = matmul(du_ref[:, :step], piece(0, c))
        for b in range(1, blocks):
            value = value + matmul(du_ref[:, b * step : (b + 1) * step], piece(b, c))
        parts.append(value)
    grad = jnp.concatenate(parts, axis=1)
    unit, inverse = unit_norm(middle_ref[...])
    out_grad = g_ref[...].astype(f32)
    total = out_grad + norm_pull(grad, gain_ref[...], unit, inverse)
    grad_ref[...] = total
    low = total.astype(bf16)
    low_ref[...] = low
    do_ref[...] = contract_last(low, read(0)).astype(bf16)
    sum_ref[0:1] += jnp.sum(low.astype(f32), axis=0, keepdims=True)
    sum_ref[1:2] += jnp.sum(grad * unit, axis=0, keepdims=True)
    sum_ref[2:3] += jnp.sum(grad, axis=0, keepdims=True)
    sum_ref[3:4] += jnp.sum(out_grad, axis=0, keepdims=True)


def token_pull_kernel(ncol, layout, parts, near_ref, far_ref, grad_ref, gain_ref, *refs):
    x, refs = token_tile(parts, refs)
    (own_ref, other_ref, sum_ref), fetch, read = head_weight(layout, refs)
    fetch()

    @pl.when(pl.program_id(0) == 0)
    def _():
        sum_ref[...] = jnp.zeros_like(sum_ref)

    grad = None
    for i in range(3):
        weight = read(i)
        middle = weight.shape[0] // 2
        value = matmul(near_ref[i], weight[:middle]) + matmul(far_ref[i], weight[middle:])
        grad = value if grad is None else grad + value
    unit, inverse = unit_norm(x)
    total = grad_ref[...] + norm_pull(grad, gain_ref[...], unit, inverse)
    width = total.shape[1] // ncol
    own_ref[...] = total[:, :width]
    for c in range(1, ncol):
        other_ref[c - 1] = total[:, c * width : (c + 1) * width].astype(bf16)
    sum_ref[0:1] += jnp.sum(grad * unit, axis=0, keepdims=True)
    sum_ref[1:2] += jnp.sum(grad, axis=0, keepdims=True)


def ffn_sent_kernel(ncol, l_ref, r_ref, out_ref):
    width = r_ref.shape[1] // ncol
    left = l_ref[...]
    for c in range(ncol):
        out_ref[0, 0, c] = contract_first(left, r_ref[:, c * width : (c + 1) * width]).astype(bf16)


def ffn_kept_kernel(ncol, nrow, l_ref, r_ref, got_ref, *out_refs):
    by_col, by_row = out_refs[:ncol], out_refs[ncol:]
    width = r_ref.shape[1] // ncol
    left = l_ref[...]
    half, row = pl.program_id(0), pl.program_id(1)
    values = []
    for c in range(ncol):
        value = contract_first(left, r_ref[:, c * width : (c + 1) * width])
        values.append((value + got_ref[0, 0, c].astype(f32)).astype(bf16))

    @pl.when(half == 0)
    def _():
        for c in range(ncol):
            by_col[c][0] = values[c]

    for r in range(nrow):

        @pl.when((half == 1) & (row == r))
        def _(r=r):
            for c in range(ncol):
                by_row[r][c] = values[c]


def head_grad_kernel(sizes, l_ref, r_ref, *refs):
    ncore, ncol, nz, part, piece = sizes
    width = r_ref.shape[1] // ncol
    left = l_ref[0]
    for c in range(ncol):
        value = contract_first(left, r_ref[:, c * width : (c + 1) * width]).astype(bf16)
        value = value.reshape(part, ncore, nz, piece, width)
        for core in range(ncore):
            for z in range(nz):
                refs[core][0, c, z, 0] = value[:, core, z]
    for sum_ref in refs[ncore:]:
        sum_ref[0] = jnp.sum(left.astype(f32), axis=0, keepdims=True)


def sums_kernel(counts, *refs):
    in_refs, out_refs = refs[: sum(counts)], refs[sum(counts) :]
    for n, out_ref in enumerate(out_refs):
        value = in_refs[sum(counts[:n])][...].astype(f32)
        for ref in in_refs[sum(counts[:n]) + 1 : sum(counts[: n + 1])]:
            value = value + ref[...].astype(f32)
        out_ref[...] = value.astype(bf16)


def make_local(nz, ncore, nrow, ncol):
    blocks = ncore * nrow
    sizes = {"z": nz, "core": ncore, "row": nrow, "col": ncol}

    def bits(axis):
        return [1 << k for k in range(sizes[axis].bit_length() - 1)]

    def exchange(values, axis, bit):
        return lax.ppermute(values, axis, [(i, i ^ bit) for i in range(sizes[axis])])

    class Slots:
        def __init__(self):
            self.before, self.now = [], []

        def advance(self):
            self.before, self.now = self.now, []

        def note(self, *values):
            self.now.extend(values)

        def gate(self, *values):
            if not self.before:
                return values
            return lax.optimization_barrier((*values, *self.before))[: len(values)]

        def move(self, values, axis, bit):
            got = exchange(values, axis, bit)
            self.now.append(got)
            return got

        def send(self, values, axis, bit):
            return self.move(self.gate(values)[0], axis, bit)

        def widen(self, parts, axis, lead=True):
            parts = list(self.gate(*parts))
            if lead:
                parts = [joined(parts)[None]]
            for bit in bits(axis):
                values = joined(parts)
                parts = [values, self.move(values, axis, bit)]
            return parts

        def fold(self, held, axis, dim):
            for bit in [bit for bit in reversed(bits(axis)) if bit < held[0][1][dim][1]]:
                got = self.move((yield [half_of(view, dim, 1) for view in held]), axis, bit)
                held = [half_of(view, dim, 0) for view in held] + [view_of(got)]
            return held

        def together(self, *stages):
            running = []
            for job, name in stages:
                stage = getattr(job, name)()
                running.append((job.name + "_" + name, stage, next(stage)))
            while running:
                counts = [len(views) for _, _, views in running]
                arrays = self.gate(*[view[0] for _, _, views in running for view in views])
                spans = [view[1] for _, _, views in running for view in views]
                with jax.named_scope("sums"):
                    values = sums_of(counts, arrays, spans)
                waiting = []
                for (name, stage, _), value in zip(running, values):
                    with jax.named_scope(name):
                        try:
                            waiting.append((name, stage, stage.send(value)))
                        except StopIteration:
                            pass
                running = waiting

    def sums_of(counts, arrays, spans):
        def spec(array, span):
            block = tuple(size for _, size in span) + array.shape[3:]
            index = tuple(start // size for start, size in span) + (0,) * (array.ndim - 3)
            return pl.BlockSpec(block, lambda t: index)

        firsts = [sum(counts[:n]) for n in range(len(counts))]
        shapes = [tuple(size for _, size in spans[n]) + arrays[n].shape[3:] for n in firsts]
        moved = sum(math.prod(size for _, size in span) * math.prod(a.shape[3:]) for a, span in zip(arrays, spans))
        return call(
            functools.partial(sums_kernel, counts),
            (1,),
            [spec(array, span) for array, span in zip(arrays, spans)],
            [summed(shape) for shape in shapes],
            [jax.ShapeDtypeStruct(shape, bf16) for shape in shapes],
            moved,
            3 * moved,
            "sums",
            vmem=16,
        )(*arrays)

    def joined(parts):
        return parts[0] if len(parts) == 1 else jnp.concatenate(parts)

    def view_of(array):
        return (array, tuple((0, n) for n in array.shape[:3]))

    def half_of(view, dim, which):
        array, spans = view
        start, size = spans[dim]
        size //= 2
        return (array, spans[:dim] + ((start + which * size, size),) + spans[dim + 1 :])

    def total(held):
        value = None
        for array, spans in held:
            part = array[tuple(slice(start, start + size) for start, size in spans)].astype(f32)
            value = part if value is None else value + part
        return value

    class Gather:
        def __init__(self, name, slots, shard):
            self.name, self.slots, self.low = name, slots, [shard[None]]

        def z_all(self):
            (values,) = self.slots.gate(*self.low)
            near = nz // 2
            parts = [values] + [self.slots.move(values, "z", k) for k in range(1, nz)]
            self.low, self.high = parts[:near], parts[near:]

        def z_low(self):
            parts = list(self.slots.gate(*self.low))
            for bit in bits("z")[:-1]:
                values = joined(parts)
                parts = [values, self.slots.move(values, "z", bit)]
            self.low = parts

        def z_high(self):
            values = joined(list(self.slots.gate(*self.low)))
            self.low = [values]
            self.high = [self.slots.move(values, "z", bits("z")[-1])]

        def z_high_first(self):
            values = joined(list(self.slots.gate(*self.low)))
            half = values.shape[0] // 2
            self.low = [values[:half], values[half:]]
            self.high = [self.slots.move(self.low[0], "z", bits("z")[-1])]

        def z_high_second(self):
            (values,) = self.slots.gate(self.low[1])
            self.high.append(self.slots.move(values, "z", bits("z")[-1]))

        def x_low(self):
            self.low_row = self.slots.widen(self.low, "row")

        def y_high(self):
            self.high_col = self.slots.widen(self.high, "col")

        def y_low(self):
            self.low_all = self.slots.widen(self.low_row, "col")

        def x_high(self):
            self.high_all = self.slots.widen(self.high_col, "row")

        def y(self):
            self.all_col = self.slots.widen(self.low + self.high, "col")

        def x(self):
            self.all_row = self.slots.widen(self.all_col, "row")

        def core_near(self):
            self.near = [[self.slots.move(p[0], "core", k) for k in range(1, ncore)] for p in (self.low_all, self.high_all)]

        def core(self):
            if hasattr(self, "all_row"):
                lists = [(2, self.all_row)]
            else:
                lists = [(0, self.low_all), (1, self.high_all)]
            self.places, self.pieces = [], []
            for half, parts in lists:
                parts = self.slots.gate(*parts)
                for k in range(ncore):
                    first = 0
                    for n, values in enumerate(parts):
                        self.places.append((k, half, first))
                        if k and n == 0 and hasattr(self, "near"):
                            self.pieces.append(self.near[half][k - 1])
                        else:
                            self.pieces.append(self.slots.move(values, "core", k) if k else values)
                        first += values.shape[0]

    class Scatter:
        def __init__(self, name, slots):
            self.name, self.slots, self.low, self.high = name, slots, [], []

        def halve(self, arrays):
            views = [view_of(array) for array in arrays]
            self.low = self.low + [half_of(view, 2, 0) for view in views]
            self.high = self.high + [half_of(view, 2, 1) for view in views]

        def first_fold(self, parts, axis, dim):
            parts = list(self.slots.gate(*parts))
            held = []
            for bit in reversed(bits(axis)):
                value = parts[bit] if bit == 1 else jnp.concatenate(parts[bit : 2 * bit], axis=dim)
                if held:
                    value = (value.astype(f32) + total([half_of(view, dim, 1) for view in held])).astype(bf16)
                got = self.slots.move(value, axis, bit)
                held = [half_of(view, dim, 0) for view in held] + [view_of(got)]
            return [view_of(parts[0])] + held

        def x_high_first(self, by_row):
            self.high = self.first_fold(by_row, "row", 0)

        def y_low_first(self, by_col):
            self.low = self.first_fold(by_col, "col", 1)

        def x_high(self):
            self.high = yield from self.slots.fold(self.high, "row", 0)

        def y_low(self):
            self.low = yield from self.slots.fold(self.low, "col", 1)

        def y_high(self):
            self.high = yield from self.slots.fold(self.high, "col", 1)

        def x_low(self):
            self.low = yield from self.slots.fold(self.low, "row", 0)

        def z_high(self):
            value = yield self.high
            self.low = self.low + [view_of(self.slots.move(value, "z", nz // 2))]

        def z_low(self):
            held = self.low
            for bit in reversed(bits("z")[:-1]):
                value = yield [half_of(view, 2, 1) for view in held]
                held = [half_of(view, 2, 0) for view in held] + [view_of(self.slots.move(value, "z", bit))]
            self.low = held

        def far_high(self):
            value = yield self.high
            self.got_high = view_of(self.slots.move(value, "row", nrow // 2))

        def far_low(self):
            value = yield self.low
            self.got_low = view_of(self.slots.move(value, "row", nrow // 2))

        def result(self):
            arrays = self.slots.gate(*[view[0] for view in self.low])
            return total([(array, view[1]) for array, view in zip(arrays, self.low)])[0, 0, 0]

    class TokensIn:
        def __init__(self, name, slots, values):
            self.name, self.slots, self.values, self.parts, self.blocks = name, slots, values, [], {}

        def slices(self, which):
            (values,) = self.slots.gate(self.values)
            rows = values.shape[0] // ncol
            here = lax.axis_index("col")
            size = rows // 2
            starts = [(here ^ k) * rows + which * size for k in range(ncol)]
            self.blocks[which] = [lax.dynamic_slice_in_dim(values, start, size, 0) for start in starts]
            self.slots.note(*self.blocks[which])

        def step(self, which):
            own, *sent = self.blocks[which]
            sent = self.slots.gate(*sent)
            self.parts.append([own] + [self.slots.move(block, "col", k + 1) for k, block in enumerate(sent)])

        def first(self):
            self.step(0)

        def second(self):
            self.step(1)

        def end(self):
            count = len(self.parts[0])
            flat = self.slots.gate(*[part for parts in self.parts for part in parts])
            rows = [jnp.concatenate(flat[i : i + count], axis=1) for i in range(0, len(flat), count)]
            return jnp.concatenate(rows)

        def operands(self):
            size = self.parts[0][0].shape[0]
            if size % LEN:
                values = self.end()
                return [values], [pl.BlockSpec((LEN, values.shape[1]), lambda t: (t, 0))]
            half = size // LEN
            values = list(self.slots.gate(*[part for parts in self.parts for part in parts]))
            shape = (LEN, values[0].shape[1])
            near = pl.BlockSpec(shape, lambda t: (jnp.minimum(t, half - 1), 0))
            far = pl.BlockSpec(shape, lambda t: (jnp.maximum(t - half, 0), 0))
            return values, [near] * ncol + [far] * ncol

    def do(job, *stages):
        for stage in stages:
            with jax.named_scope(job.name + "_" + stage):
                getattr(job, stage)()

    class TokensOut:
        def __init__(self, name, slots, own, other):
            self.name, self.slots, self.own, self.other = name, slots, own, other

        @staticmethod
        def space(slots, rows, width, dtype):
            zeros = lax.optimization_barrier(jnp.zeros((rows * ncol, width), dtype))
            slots.note(zeros)
            return zeros

        def send(self):
            self.blocks = [self.slots.send(self.other[k - 1], "col", k) for k in range(1, ncol)]

        def end(self, result):
            rows = self.own.shape[0]
            here = lax.axis_index("col")
            first, *rest = self.slots.gate(self.own, *self.blocks)
            result = lax.dynamic_update_slice_in_dim(result, first, here * rows, 0)
            for k, block in enumerate(rest):
                result = lax.dynamic_update_slice_in_dim(
                    result, block.astype(self.own.dtype), (here ^ (k + 1)) * rows, 0
                )
            return result

    def local(
        tokens,
        key_mask,
        first_gain,
        first_shift,
        qkv_weight,
        qkv_bias,
        out_weight,
        out_bias,
        second_gain,
        second_shift,
        up_weight,
        up_bias,
        down_weight,
        down_bias,
        cotangent,
    ):
        count = tokens.shape[0] // ncol
        seqs = count // LEN
        part, piece, width = out_weight.shape
        heads = part * nrow
        flat = heads * HD
        hidden_part = up_weight.shape[0]
        step = nz * hidden_part
        dim = width * ncol
        hidden = step * blocks
        pairs = heads // 2
        moved = count * dim

        def tile(shape, index=None):
            return pl.BlockSpec(shape, index or (lambda t: (t,) + (0,) * (len(shape) - 1)))

        slots = Slots()
        q = Gather("qkv", slots, qkv_weight.reshape(3 * part, piece, width).astype(bf16))
        o = Gather("out", slots, out_weight.astype(bf16))
        u = Gather("up", slots, up_weight.astype(bf16))
        d = Gather("down", slots, down_weight.astype(bf16))
        tok = TokensIn("tokens", slots, tokens)
        cot = TokensIn("cotangent", slots, cotangent)
        vectors = jnp.stack([first_gain, first_shift, second_gain, second_shift, out_bias, down_bias])

        small = [jnp.concatenate([qkv_bias.reshape(-1), up_bias]).astype(bf16)[None]]
        features = jnp.concatenate([vectors.reshape(-1), key_mask.reshape(-1).astype(f32)])
        tok.slices(0)
        do(q, "z_all")
        do(tok, "first")
        features = slots.widen([features], "col")
        slots.advance()
        spaces = [TokensOut.space(slots, count, width, dtype) for dtype in (bf16, f32)]
        do(q, "x_low", "y_high")
        do(o, "z_low")
        do(u, "z_low")
        small = slots.widen(small, "z", False)
        small = slots.widen(small, "row")
        tok.slices(1)
        slots.advance()
        do(q, "y_low", "x_high")
        do(o, "z_high")
        do(u, "z_high")
        do(tok, "second")
        small = slots.widen(small, "core")
        slots.advance()
        do(q, "core")
        do(o, "y")
        do(d, "z_low")
        cot.slices(0)
        small_all = joined(list(slots.gate(*small))).astype(f32)
        qkv_count = qkv_bias.size
        qkv_offset = small_all[..., :qkv_count].reshape(ncore, nrow, nz, 2, part, piece)
        qkv_offset = jnp.transpose(qkv_offset, (3, 1, 4, 0, 2, 5)).reshape(2, flat)
        up_offset = small_all[..., qkv_count:].reshape(1, hidden)
        features = joined(list(slots.gate(*features)))
        vectors, nearby = features[:, : vectors.size], features[:, vectors.size :]
        vectors = jnp.transpose(vectors.reshape(ncol, 6, width), (1, 0, 2)).reshape(6, dim)
        slots.note(vectors, qkv_offset, up_offset)
        slots.advance()
        inputs, input_specs = tok.operands()
        parts = len(inputs)
        gain_one, shift_one, gain_two, shift_two, out_offset, down_offset = [vectors[i : i + 1] for i in range(6)]

        here = lax.axis_index("col")
        nearby = nearby.reshape((ncol,) + key_mask.shape)
        masks = jnp.zeros_like(nearby)
        for k in range(ncol):
            masks = lax.dynamic_update_slice_in_dim(masks, nearby[k : k + 1], here ^ k, 0)
        masks = masks.reshape(-1, key_mask.shape[1])
        first_seq = (lax.axis_index("row") * ncol + here) * seqs
        masks = lax.dynamic_slice_in_dim(masks, first_seq, seqs, 0)
        visible = jnp.concatenate([jnp.ones((seqs, BUF), f32), masks], axis=1)

        def head_operands(w, kinds):
            half = nz // 2
            places = []
            for k, r, c, z in itertools.product(range(ncore), range(nrow), range(ncol), range(nz)):
                for n, ((in_core, in_half, first), values) in enumerate(zip(w.places, w.pieces)):
                    lead, second, inner = (c, r, z) if in_half == 0 else (r, c, z - half * (in_half == 1))
                    held = in_half == 2 or in_half == z // half
                    if held and in_core == k and first <= lead < first + values.shape[0]:
                        index = (lead - first, second, inner)
                        places.append((n, index, r * part, (k * nz + z) * piece, c * width))
            if piece % 8 == 0:
                specs = [pl.BlockSpec(memory_space=pl.ANY)] * len(w.pieces)
                scratch = [pltpu.VMEM((kinds, heads, HD, dim), bf16), pltpu.SemaphoreType.DMA((kinds,))]
                return w.pieces, specs, scratch, (tuple(places), kinds, part)
            matrix = jnp.zeros((kinds, heads, HD, dim), bf16)
            for n, index, head, row, lane in places:
                block = w.pieces[n][index][: kinds * part].reshape(kinds, part, piece, width)
                matrix = lax.dynamic_update_slice(matrix, block, (0, head, row, lane))
            return [matrix.reshape(kinds, flat, dim)], [whole((kinds, flat, dim))], [], None

        qkv_ops, qkv_specs, qkv_scratch, qkv_layout = head_operands(q, 3)

        tokens_spec = tile((LEN, dim))
        hidden_spec = tile((LEN, hidden))
        half_step = step // 2
        vector_spec = whole((1, dim))
        three = pl.BlockSpec((3, LEN, flat), lambda t: (0, t, 0))
        own_spec = tile((LEN, width))
        other_spec = pl.BlockSpec((ncol - 1, LEN, width), lambda t: (0, t, 0))

        def out_of(*shape, dtype=bf16):
            return jax.ShapeDtypeStruct(shape, dtype)

        def ffn_operands(w):
            operands = [p.reshape(p.shape[0], p.shape[1], half_step, width) for p in w.pieces]
            return operands, [whole(p.shape) for p in operands], (ncol, nrow, ncore, tuple(w.places))

        do(u, "x_low", "y_high")
        do(o, "x")
        do(d, "z_high")
        do(cot, "first")
        normed, qkv = call(
            functools.partial(qkv_kernel, qkv_layout, parts),
            (seqs,),
            [vector_spec, vector_spec, whole((2, flat))] + input_specs + qkv_specs,
            [tokens_spec, three],
            [out_of(count, dim), out_of(3, count, flat)],
            6 * moved * flat,
            6 * flat * dim + 10 * moved,
            "qkv",
            scratch=qkv_scratch,
        )(gain_one, shift_one, qkv_offset, *inputs, *qkv_ops)
        slots.note(qkv)
        slots.advance()

        do(u, "y_low", "x_high", "core_near")
        do(o, "core")
        quads = flat // QUAD
        step_lanes = STEP * QUAD
        queries = HELD * LEN
        attended, probs = call(
            attend_kernel,
            (seqs, quads // STEP),
            [
                pl.BlockSpec((3, LEN, step_lanes), lambda s, p: (0, s, p)),
                pl.BlockSpec((1, LEN, 1), lambda s, p: (s, 0, 0)),
            ],
            [
                pl.BlockSpec((LEN, step_lanes), lambda s, p: (s, p)),
                pl.BlockSpec((1, STEP, LEN, queries), lambda s, p: (s, p, 0, 0)),
            ],
            [out_of(count, flat), out_of(seqs, quads, LEN, queries)],
            16 * count * LEN * flat,
            8 * moved + 2 * seqs * quads * LEN * queries,
            "attend",
        )(slots.gate(qkv)[0], visible[:, :, None])
        slots.note(attended)
        slots.advance()

        do(u, "core")
        do(d, "x_low", "y_high")
        out_ops, out_specs, out_scratch, out_layout = head_operands(o, 1)
        middle, normed_two = call(
            functools.partial(out_kernel, out_layout, parts),
            (seqs,),
            [tile((LEN, flat)), vector_spec, vector_spec, vector_spec] + input_specs + out_specs,
            [tokens_spec, tokens_spec],
            [out_of(count, dim, dtype=f32), out_of(count, dim)],
            2 * moved * flat,
            2 * flat * dim + 10 * moved,
            "out",
            scratch=out_scratch,
        )(slots.gate(attended)[0], out_offset, gain_two, shift_two, *inputs, *out_ops)
        slots.note(normed_two)
        slots.advance()

        do(d, "y_low", "x_high", "core_near")
        cot.slices(1)
        up_ops, up_specs, up_dims = ffn_operands(u)
        hid, slope = call(
            functools.partial(up_kernel, up_dims),
            (seqs,),
            [tokens_spec, whole((1, hidden))] + up_specs,
            [hidden_spec, hidden_spec],
            [out_of(count, hidden), out_of(count, hidden)],
            8 * moved * hidden,
            2 * hidden * dim + 4 * count * hidden,
            "up",
        )(slots.gate(normed_two)[0], up_offset, *up_ops)
        slots.note(hid)
        slots.advance()

        def ffn_sent(left, right, name):
            return call(
                functools.partial(ffn_sent_kernel, ncol),
                (2, nrow),
                [
                    pl.BlockSpec((count, half_step), lambda h, r: (0, (nrow + r) * 2 + h)),
                    whole((count, dim)),
                ],
                pl.BlockSpec((1, 1, ncol, half_step, width), lambda h, r: (h, r, 0, 0, 0)),
                out_of(2, nrow, ncol, half_step, width),
                2 * moved * hidden // ncore,
                2 * (hidden * dim + count * hidden) // ncore + 2 * moved,
                name,
            )(slots.gate(left)[0], right)

        def ffn_kept(left, right, got, name):
            by_col = pl.BlockSpec((1, half_step, width), lambda h, r: (jnp.where(h == 0, r, nrow - 1), 0, 0))
            out = call(
                functools.partial(ffn_kept_kernel, ncol, nrow),
                (2, nrow),
                [
                    pl.BlockSpec((count, half_step), lambda h, r: (0, r * 2 + h)),
                    whole((count, dim)),
                    pl.BlockSpec((1, 1, ncol, half_step, width), lambda h, r: (h, r, 0, 0, 0)),
                ],
                [by_col] * ncol + [summed((ncol, half_step, width))] * nrow,
                [out_of(nrow, half_step, width)] * ncol + [out_of(ncol, half_step, width)] * nrow,
                2 * moved * hidden // ncore,
                3 * (hidden * dim + count * hidden) // ncore + 2 * moved,
                name,
            )(left, right, got)
            shape = (nz // 2, hidden_part, width)
            slots.note(out[0])
            low = [values.reshape((nrow, 1) + shape) for values in out[:ncol]]
            return low, [values.reshape((1, ncol) + shape) for values in out[ncol:]]

        def head_grad(left, right, first, name, sums=False):
            kinds, _, lanes = left.shape
            rows = lanes // (part * HD)
            out = call(
                functools.partial(head_grad_kernel, (ncore, ncol, nz, part, piece)),
                (kinds, rows),
                [
                    pl.BlockSpec((1, count, part * HD), lambda i, r: (i, 0, r)),
                    whole((count, dim)),
                ],
                [pl.BlockSpec((1, ncol, nz, 1, part, piece, width), lambda i, r: (r, 0, 0, i, 0, 0, 0))] * ncore
                + [pl.BlockSpec((1, 1, part * HD), lambda i, r: (i, 0, r))] * sums,
                [out_of(rows, ncol, nz, kinds, part, piece, width)] * ncore
                + [out_of(kinds, 1, lanes, dtype=f32)] * sums,
                2 * moved * lanes * kinds,
                2 * kinds * (lanes * dim + count * lanes) + 2 * moved,
                name,
            )(left, right)
            slots.note(out[0])
            return out[:ncore], out[ncore:]

        def core_fold(name, sums, gated=True):
            with jax.named_scope(name + "_core"):
                sent = slots.gate(*sums[1:]) if gated else sums[1:]
                return [sums[0]] + [slots.move(values, "core", k + 1) for k, values in enumerate(sent)]

        def pull(first, rows):
            lanes = rows * part * HD
            which = first // rows
            kinds = 3

            def seq(t):
                return jnp.minimum(t, seqs - 1)

            def kind_row(t):
                step_after = jnp.maximum(t - seqs, 0)
                return step_after // rows, step_after % rows

            def sums_at(t):
                kind, row = kind_row(t)
                return (row, 0, 0, kind, 0, 0, 0)

            def own_at(t):
                kind, row = kind_row(t)
                return (kind, 0, row)

            out = call(
                functools.partial(attend_pull_kernel, seqs, (ncore, ncol, nz, part, piece)),
                (seqs + kinds * rows,),
                [
                    pl.BlockSpec((kinds, LEN, lanes), lambda t: (0, seq(t), which)),
                    pl.BlockSpec((1, STEP, LEN, queries), lambda t: (seq(t), which, 0, 0)),
                    pl.BlockSpec((LEN, lanes), lambda t: (seq(t), which)),
                    whole((count, dim)),
                ],
                [pl.BlockSpec((kinds, LEN, lanes), lambda t: (0, seq(t), 0))]
                + [pl.BlockSpec((1, ncol, nz, 1, part, piece, width), sums_at)] * ncore
                + [pl.BlockSpec((1, 1, part * HD), own_at)],
                [out_of(kinds, count, lanes)]
                + [out_of(rows, ncol, nz, kinds, part, piece, width)] * ncore
                + [out_of(kinds, 1, lanes, dtype=f32)],
                30 * count * LEN * lanes + 2 * moved * lanes * kinds,
                14 * moved * rows // nrow,
                "attend_pull",
                scratch=[pltpu.VMEM((kinds, count, lanes), bf16)],
            )(qkv, probs, slots.gate(attended_grad)[0], normed)
            slots.note(out[0])
            return out[0], out[1 : 1 + ncore], out[1 + ncore]

        do(d, "core")
        do(cot, "second")
        down_ops, down_specs, down_dims = ffn_operands(d)
        own, other = call(
            functools.partial(down_kernel, down_dims),
            (seqs,),
            [hidden_spec, tokens_spec, vector_spec] + down_specs,
            [own_spec, other_spec],
            [out_of(count, width), out_of(ncol - 1, count, width)],
            2 * moved * hidden,
            2 * hidden * dim + 2 * count * hidden + 6 * moved,
            "down",
        )(hid, middle, down_offset, *down_ops)
        slots.note(own)
        slots.advance()

        dg, ug, og, qg = [Scatter(name, slots) for name in ("down_grad", "up_grad", "out_grad", "qkv_grad")]
        activations = TokensOut("activations", slots, own, other)
        do(activations, "send")
        grad_low = cot.end()
        sent = ffn_sent(hid, grad_low, "down_grad")
        (got,) = core_fold("down_grad", [sent, sent], False)[1:]
        upward_grad, up_bias_sum = call(
            functools.partial(hidden_pull_kernel, down_dims),
            (seqs,),
            [tokens_spec, hidden_spec] + down_specs,
            [hidden_spec, summed((1, hidden))],
            [out_of(count, hidden), out_of(1, hidden, dtype=f32)],
            2 * moved * hidden,
            2 * hidden * dim + 4 * count * hidden,
            "hidden_pull",
        )(slots.gate(grad_low)[0], slope, *down_ops)
        slots.note(upward_grad)
        down_low, down_high = ffn_kept(hid, grad_low, got, "down_grad")
        slots.advance()

        with jax.named_scope("down_grad_first"):
            dg.x_high_first(down_high)
            dg.y_low_first(down_low)
        sent = ffn_sent(upward_grad, normed_two, "up_grad")
        (got,) = core_fold("up_grad", [sent, sent], False)[1:]
        middle_grad, branch_low, attended_grad, sums_two = call(
            functools.partial(middle_pull_kernel, up_dims, out_layout),
            (seqs,),
            [hidden_spec, tokens_spec, tokens_spec, vector_spec] + up_specs + out_specs,
            [tokens_spec, tokens_spec, tile((LEN, flat)), summed((4, dim))],
            [
                out_of(count, dim, dtype=f32),
                out_of(count, dim),
                out_of(count, flat),
                out_of(4, dim, dtype=f32),
            ],
            2 * moved * (hidden + flat),
            2 * hidden * dim + 2 * count * hidden + 14 * moved,
            "middle_pull",
            scratch=out_scratch,
        )(slots.gate(upward_grad)[0], middle, grad_low, gain_two, *up_ops, *out_ops)
        slots.note(attended_grad)
        activations = activations.end(spaces[0])
        slots.note(activations)
        slots.advance()

        slots.together((dg, "y_high"), (dg, "x_low"))
        out_sums, _ = head_grad(slots.gate(attended)[0][None], branch_low, 0, "out_grad")
        up_low, up_high = ffn_kept(slots.gate(upward_grad)[0], normed_two, got, "up_grad")
        slots.advance()

        with jax.named_scope("up_grad_first"):
            ug.x_high_first(up_high)
            ug.y_low_first(up_low)
        slots.together((dg, "z_high"))
        out_held = core_fold("out_grad", out_sums)
        far, far_sums, far_own = pull(nrow // 2, nrow // 2)
        slots.note(*far_sums)
        slots.advance()

        far_held = core_fold("qkv_grad_far", far_sums)
        slots.together((ug, "y_high"), (ug, "x_low"))
        slots.advance()

        far_low = Scatter("qkv_grad_far", slots)
        far_low.halve(far_held)
        og.halve(out_held)
        slots.together(
            (far_low, "far_high"), (far_low, "y_low"), (ug, "z_high"), (og, "x_high"), (og, "y_low")
        )
        near, near_sums, near_own = pull(0, nrow // 2)
        slots.note(*near_sums)
        slots.advance()

        near_held = core_fold("qkv_grad_near", near_sums)
        slots.together((far_low, "far_low"), (og, "y_high"), (og, "x_low"), (dg, "z_low"))
        slots.advance()

        qg.halve(near_held)
        qg.high = qg.high + [far_low.got_high]
        if nrow > 2:
            slots.together((qg, "x_high"))
        slots.together((qg, "y_high"), (qg, "y_low"), (og, "z_high"), (ug, "z_low"))
        down_grad = dg.result()
        own_grad, other_grad, sums_one = call(
            functools.partial(token_pull_kernel, ncol, qkv_layout, parts),
            (seqs,),
            [pl.BlockSpec((3, LEN, flat // 2), lambda t: (0, t, 0))] * 2
            + [tokens_spec, vector_spec]
            + input_specs
            + qkv_specs,
            [own_spec, other_spec, summed((2, dim))],
            [
                out_of(count, width, dtype=f32),
                out_of(ncol - 1, count, width),
                out_of(2, dim, dtype=f32),
            ],
            6 * moved * flat,
            6 * flat * dim + 14 * moved,
            "token_pull",
            scratch=qkv_scratch,
        )(slots.gate(near)[0], far, middle_grad, gain_one, *inputs, *qkv_ops)
        slots.note(own_grad)
        slots.advance()

        bias_sum = jnp.concatenate([near_own, far_own], axis=2)[::2].reshape(2, nrow, part, ncore, nz, piece)
        bias_sum = jnp.transpose(bias_sum, (3, 1, 4, 0, 2, 5)).reshape(ncore, nrow, nz, qkv_count)
        bias_sum = jnp.concatenate([bias_sum, up_bias_sum.reshape(ncore, nrow, nz, hidden_part)], axis=-1)
        sums = jnp.concatenate([sums_one, sums_two])
        size = sums.shape[0] * width
        flat_bias = bias_sum.reshape(-1)
        packs = [jnp.concatenate([sums[:, :width].reshape(-1), flat_bias])]

        def small_sums():
            (pack,) = slots.gate(packs[0])
            for k in range(1, ncol):
                far_part = sums[:, k * width : (k + 1) * width].reshape(-1)
                pack = pack + slots.send(jnp.concatenate([far_part, flat_bias]), "col", k)
            for axis in ("core", "row", "z"):
                for bit in reversed(bits(axis)):
                    rest = pack[size:]
                    half = rest.size // 2
                    got = slots.move(jnp.concatenate([pack[:size], rest[half:]]), axis, bit)
                    pack = pack[: size + half] + got
            packs[0] = pack

        token_grad = TokensOut("token_grad", slots, own_grad, other_grad)
        do(token_grad, "send")
        qg.low = qg.low + [far_low.got_low]
        if nrow > 2:
            slots.together((qg, "x_low"))
        slots.together((qg, "z_high"), (og, "z_low"))
        with jax.named_scope("small_sums"):
            small_sums()
        up_grad = ug.result()
        slots.note(up_grad)
        slots.advance()

        slots.together((qg, "z_low"))
        token_grad = token_grad.end(spaces[1])
        out_grad, qkv_grad = og.result(), qg.result()

        pack = packs[0]
        sums = pack[:size].reshape(-1, width)
        bias_sum = pack[size:]
        return (
            activations,
            token_grad,
            sums[0],
            sums[1],
            qkv_grad,
            bias_sum[:qkv_count].reshape(qkv_bias.shape),
            out_grad[0],
            sums[2],
            sums[3],
            sums[4],
            up_grad,
            bias_sum[qkv_count:],
            down_grad,
            sums[5],
        )

    return local


def solution(mesh):
    devices = mesh.devices
    nz, ncore = devices.shape[0] // 2, 2
    nrow, ncol = devices.shape[1], devices.shape[2]
    fine = Mesh(devices.reshape(nz, ncore, nrow, ncol), ("z", "core", "row", "col"))
    dp = ("z", "core")
    rows = P(("z", "core", "row"), "col")
    qkv_weight = P(None, "row", dp, "col")
    qkv_bias = P(None, "row", dp)
    out_weight = P("row", dp, "col")
    feature = P("col")
    unit = P(("z", "core", "row"))
    in_specs = (
        rows,
        P(("z", "core", "col"), None),
        feature,
        feature,
        qkv_weight,
        qkv_bias,
        out_weight,
        feature,
        feature,
        feature,
        rows,
        unit,
        rows,
        feature,
        rows,
    )
    out_specs = (
        rows,
        rows,
        feature,
        feature,
        qkv_weight,
        qkv_bias,
        out_weight,
        feature,
        feature,
        feature,
        rows,
        unit,
        rows,
        feature,
    )
    return jax.shard_map(
        make_local(nz, ncore, nrow, ncol),
        mesh=fine,
        in_specs=in_specs,
        out_specs=out_specs,
        check_vma=False,
    )
```

```python
import functools
import itertools
import math

import jax
import jax.numpy as jnp
from jax import lax
from jax.experimental import pallas as pl
from jax.experimental.pallas import tpu as pltpu
from jax.sharding import Mesh, PartitionSpec as P

HD = 64
HELD = 4
QUAD = HELD * HD
STEP = 2
BUF = 64
LEN = 320
masked_fill = -1000000000.0
norm_epsilon = 1e-06
attn_scale = 0.125
exp2_scale = attn_scale * 1.4426950408889634
root_half = 0.7071067811865476
density = 0.3989422804014327
bf16 = jnp.bfloat16
f32 = jnp.float32
MIB = 1 << 20


def contract_last(left, right):
    return lax.dot_general(left, right, (((1,), (1,)), ((), ())), preferred_element_type=f32)


def contract_first(left, right):
    return lax.dot_general(left, right, (((0,), (0,)), ((), ())), preferred_element_type=f32)


def matmul(left, right):
    return lax.dot_general(left, right, (((1,), (0,)), ((), ())), preferred_element_type=f32)


def whole(shape):
    return pl.BlockSpec(shape, lambda *_: (0,) * len(shape), pipeline_mode=pl.Buffered(1))


def summed(shape):
    return pl.BlockSpec(shape, lambda *_: (0,) * len(shape))


def call(kernel, grid, in_specs, out_specs, out_shape, flops, moved, name, vmem=48, scratch=()):
    return pl.pallas_call(
        kernel,
        grid=grid,
        in_specs=in_specs,
        out_specs=out_specs,
        out_shape=out_shape,
        scratch_shapes=scratch,
        name=name,
        compiler_params=pltpu.CompilerParams(vmem_limit_bytes=vmem * MIB),
        cost_estimate=pl.CostEstimate(flops=flops, bytes_accessed=moved, transcendentals=0),
    )


def unit_norm(values):
    center = jnp.mean(values, axis=1, keepdims=True)
    centered = values - center
    spread = jnp.mean(centered * centered, axis=1, keepdims=True)
    inverse = lax.rsqrt(spread + norm_epsilon)
    return centered * inverse, inverse


def norm_pull(grad, gain, unit, inverse):
    scaled = grad * gain
    total = jnp.mean(scaled, axis=1, keepdims=True)
    paired = jnp.mean(scaled * unit, axis=1, keepdims=True)
    return inverse * (scaled - total - unit * paired)


def head_weight(layout, refs):
    if layout is None:
        return refs[1:], lambda: None, lambda i: refs[0][i]
    places, kinds, part = layout
    held, sem = refs[-2:]
    operands = 1 + max(place[0] for place in places)

    def copies(kind):
        for operand, index, head, row, lane in places:
            source = refs[operand].at[index + (pl.ds(kind * part, part),)]
            _, piece, width = source.shape
            target = held.at[kind, pl.ds(head, part), pl.ds(row, piece), pl.ds(lane, width)]
            yield pltpu.make_async_copy(source, target, sem.at[kind])

    def fetch():
        @pl.when(pl.program_id(0) == 0)
        def _():
            for kind in range(kinds):
                for copy in copies(kind):
                    copy.start()

    def read(kind):
        @pl.when(pl.program_id(0) == 0)
        def _():
            for copy in copies(kind):
                copy.wait()

        return held[kind].reshape(held.shape[1] * held.shape[2], held.shape[3])

    return refs[operands:-2], fetch, read


def token_tile(parts, refs):
    if parts == 1:
        return refs[0][...].astype(f32), refs[1:]
    half = parts // 2
    near = jnp.concatenate([ref[...] for ref in refs[:half]], axis=1).astype(f32)
    far = jnp.concatenate([ref[...] for ref in refs[half:parts]], axis=1).astype(f32)
    return jnp.where(pl.program_id(0) < pl.num_programs(0) // 2, near, far), refs[parts:]


def qkv_kernel(layout, parts, gain_ref, shift_ref, bias_ref, *refs):
    x, refs = token_tile(parts, refs)
    (a_ref, out_ref), fetch, read = head_weight(layout, refs)
    fetch()
    unit, _ = unit_norm(x)
    a = (unit * gain_ref[...] + shift_ref[...]).astype(bf16)
    a_ref[...] = a
    for i in range(3):
        value = contract_last(a, read(i))
        if i != 1:
            value = value + bias_ref[i // 2 : i // 2 + 1]
        out_ref[i] = value.astype(bf16)


def split_heads(held):
    head = lax.broadcasted_iota(jnp.int32, held.shape, 1) // HD
    zero = jnp.zeros_like(held)
    return jnp.concatenate([jnp.where(head == h, held, zero) for h in range(HELD)], axis=0)


def join_heads(all_heads):
    rows = all_heads.shape[0] // HELD
    head = lax.broadcasted_iota(jnp.int32, (rows, all_heads.shape[1]), 1) // HD
    value = all_heads[:rows]
    for h in range(1, HELD):
        value = jnp.where(head == h, all_heads[h * rows : (h + 1) * rows], value)
    return value


def attend_kernel(qkv_ref, mask_ref, out_ref, probs_ref):
    seen = mask_ref[0] > 0
    for n in range(STEP):
        lanes = slice(n * QUAD, (n + 1) * QUAD)
        scores = contract_last(qkv_ref[1, :, lanes], split_heads(qkv_ref[0, :, lanes]))
        scores = jnp.where(seen, scores, masked_fill / attn_scale)
        top = jnp.max(scores, axis=0, keepdims=True)
        grown = jnp.exp2((scores - top) * exp2_scale)
        probs = (grown * (1.0 / jnp.sum(grown, axis=0, keepdims=True))).astype(bf16)
        probs_ref[0, n] = probs
        out_ref[:, lanes] = join_heads(contract_first(probs, qkv_ref[2, :, lanes])).astype(bf16)


def attend_pull_kernel(seqs, sizes, qkv_ref, probs_ref, do_ref, normed_ref, out_ref, *refs):
    ncore, ncol, nz, part, piece = sizes
    sum_refs, (sum_ref, held) = refs[:ncore], refs[ncore:]
    at = pl.program_id(0)
    rows = held.shape[2] // (part * HD)

    @pl.when(at < seqs)
    def _():
        place = pl.ds(pl.multiple_of(at * LEN, LEN), LEN)
        for n in range(STEP):
            lanes = slice(n * QUAD, (n + 1) * QUAD)
            queries = split_heads(qkv_ref[0, :, lanes])
            keys = qkv_ref[1, :, lanes]
            pulled = split_heads(do_ref[:, lanes])
            low = probs_ref[0, n]
            probs = low.astype(f32)
            prob_grad = contract_last(qkv_ref[2, :, lanes], pulled)
            inner = jnp.sum(prob_grad * probs, axis=0, keepdims=True)
            score_grad = (probs * (prob_grad - inner)).astype(bf16)
            value_grad = matmul(low, pulled).astype(bf16)
            key_grad = (matmul(score_grad, queries) * attn_scale).astype(bf16)
            query_grad = join_heads(contract_first(score_grad, keys) * attn_scale).astype(bf16)
            for i, value in enumerate((query_grad, key_grad, value_grad)):
                out_ref[i, :, lanes] = value
                held[i, place, lanes] = value

    @pl.when(at >= seqs)
    def _():
        width = normed_ref.shape[1] // ncol
        kind, row = (at - seqs) // rows, (at - seqs) % rows
        size = part * HD
        left = held[kind, :, pl.ds(pl.multiple_of(row * size, size), size)] if rows > 1 else held[kind]
        for c in range(ncol):
            value = contract_first(left, normed_ref[:, c * width : (c + 1) * width]).astype(bf16)
            value = value.reshape(part, ncore, nz, piece, width)
            for core in range(ncore):
                for z in range(nz):
                    sum_refs[core][0, c, z, 0] = value[:, core, z]
        sum_ref[0] = jnp.sum(left.astype(f32), axis=0, keepdims=True)


def out_kernel(layout, parts, o_ref, bias_ref, gain_ref, shift_ref, *refs):
    x, refs = token_tile(parts, refs)
    (middle_ref, a_ref), fetch, read = head_weight(layout, refs)
    fetch()
    middle = x + (matmul(o_ref[...], read(0)) + bias_ref[...])
    middle_ref[...] = middle
    unit, _ = unit_norm(middle)
    a_ref[...] = (unit * gain_ref[...] + shift_ref[...]).astype(bf16)


def pieces_of(dims, refs):
    ncol, nrow, ncore, places = dims
    w_refs, rest = refs[: len(places)], refs[len(places) :]

    def piece(block, col):
        core, within = divmod(block, 2 * nrow)
        row, half = divmod(within, 2)
        lead, second = (row, col) if half else (col, row)
        for ref, (in_core, in_half, first) in zip(w_refs, places):
            if (in_core, in_half) == (core, half) and first <= lead < first + ref.shape[0]:
                return ref[lead - first, second]

    return piece, 2 * ncore * nrow, w_refs[0].shape[2], w_refs[0].shape[3], rest


def up_kernel(dims, a_ref, bias_ref, *refs):
    piece, blocks, step, width, (hid_ref, slope_ref) = pieces_of(dims, refs)
    for b in range(blocks):
        rows = slice(b * step, (b + 1) * step)
        value = bias_ref[:, rows]
        for c in range(dims[0]):
            value = value + contract_last(a_ref[:, c * width : (c + 1) * width], piece(b, c))
        cdf = 0.5 + 0.5 * lax.erf(value * root_half)
        pdf = jnp.exp(-0.5 * value * value) * density
        hid_ref[:, rows] = (value * cdf).astype(bf16)
        slope_ref[:, rows] = (cdf + value * pdf).astype(bf16)


def down_kernel(dims, hid_ref, middle_ref, bias_ref, *refs):
    piece, blocks, step, width, (own_ref, other_ref) = pieces_of(dims, refs)
    for c in range(dims[0]):
        lanes = slice(c * width, (c + 1) * width)
        value = middle_ref[:, lanes] + bias_ref[:, lanes]
        for b in range(blocks):
            value = value + matmul(hid_ref[:, b * step : (b + 1) * step], piece(b, c))
        if c == 0:
            own_ref[...] = value.astype(bf16)
        else:
            other_ref[c - 1] = value.astype(bf16)


def hidden_pull_kernel(dims, g_ref, slope_ref, *refs):
    piece, blocks, step, width, (du_ref, sum_ref) = pieces_of(dims, refs)

    @pl.when(pl.program_id(0) == 0)
    def _():
        sum_ref[...] = jnp.zeros_like(sum_ref)

    for b in range(blocks):
        rows = slice(b * step, (b + 1) * step)
        value = contract_last(g_ref[:, :width], piece(b, 0))
        for c in range(1, dims[0]):
            value = value + contract_last(g_ref[:, c * width : (c + 1) * width], piece(b, c))
        low = (value * slope_ref[:, rows].astype(f32)).astype(bf16)
        du_ref[:, rows] = low
        sum_ref[:, rows] += jnp.sum(low.astype(f32), axis=0, keepdims=True)


def middle_pull_kernel(dims, layout, du_ref, middle_ref, g_ref, gain_ref, *refs):
    piece, blocks, step, width, rest = pieces_of(dims, refs)
    (grad_ref, low_ref, do_ref, sum_ref), fetch, read = head_weight(layout, rest)
    fetch()

    @pl.when(pl.program_id(0) == 0)
    def _():
        sum_ref[...] = jnp.zeros_like(sum_ref)

    parts = []
    for c in range(dims[0]):
        value = matmul(du_ref[:, :step], piece(0, c))
        for b in range(1, blocks):
            value = value + matmul(du_ref[:, b * step : (b + 1) * step], piece(b, c))
        parts.append(value)
    grad = jnp.concatenate(parts, axis=1)
    unit, inverse = unit_norm(middle_ref[...])
    out_grad = g_ref[...].astype(f32)
    total = out_grad + norm_pull(grad, gain_ref[...], unit, inverse)
    grad_ref[...] = total
    low = total.astype(bf16)
    low_ref[...] = low
    do_ref[...] = contract_last(low, read(0)).astype(bf16)
    sum_ref[0:1] += jnp.sum(low.astype(f32), axis=0, keepdims=True)
    sum_ref[1:2] += jnp.sum(grad * unit, axis=0, keepdims=True)
    sum_ref[2:3] += jnp.sum(grad, axis=0, keepdims=True)
    sum_ref[3:4] += jnp.sum(out_grad, axis=0, keepdims=True)


def token_pull_kernel(ncol, layout, parts, near_ref, far_ref, grad_ref, gain_ref, *refs):
    x, refs = token_tile(parts, refs)
    (own_ref, other_ref, sum_ref), fetch, read = head_weight(layout, refs)
    fetch()

    @pl.when(pl.program_id(0) == 0)
    def _():
        sum_ref[...] = jnp.zeros_like(sum_ref)

    grad = None
    for i in range(3):
        weight = read(i)
        middle = weight.shape[0] // 2
        value = matmul(near_ref[i], weight[:middle]) + matmul(far_ref[i], weight[middle:])
        grad = value if grad is None else grad + value
    unit, inverse = unit_norm(x)
    total = grad_ref[...] + norm_pull(grad, gain_ref[...], unit, inverse)
    width = total.shape[1] // ncol
    own_ref[...] = total[:, :width]
    for c in range(1, ncol):
        other_ref[c - 1] = total[:, c * width : (c + 1) * width].astype(bf16)
    sum_ref[0:1] += jnp.sum(grad * unit, axis=0, keepdims=True)
    sum_ref[1:2] += jnp.sum(grad, axis=0, keepdims=True)


def ffn_sent_kernel(ncol, l_ref, r_ref, out_ref):
    width = r_ref.shape[1] // ncol
    left = l_ref[...]
    for c in range(ncol):
        out_ref[0, 0, c] = contract_first(left, r_ref[:, c * width : (c + 1) * width]).astype(bf16)


def ffn_kept_kernel(ncol, nrow, l_ref, r_ref, got_ref, *out_refs):
    by_col, by_row = out_refs[:ncol], out_refs[ncol:]
    width = r_ref.shape[1] // ncol
    left = l_ref[...]
    half, row = pl.program_id(0), pl.program_id(1)
    values = []
    for c in range(ncol):
        value = contract_first(left, r_ref[:, c * width : (c + 1) * width])
        values.append((value + got_ref[0, 0, c].astype(f32)).astype(bf16))

    @pl.when(half == 0)
    def _():
        for c in range(ncol):
            by_col[c][0] = values[c]

    for r in range(nrow):

        @pl.when((half == 1) & (row == r))
        def _(r=r):
            for c in range(ncol):
                by_row[r][c] = values[c]


def head_grad_kernel(sizes, l_ref, r_ref, *refs):
    ncore, ncol, nz, part, piece = sizes
    width = r_ref.shape[1] // ncol
    left = l_ref[0]
    for c in range(ncol):
        value = contract_first(left, r_ref[:, c * width : (c + 1) * width]).astype(bf16)
        value = value.reshape(part, ncore, nz, piece, width)
        for core in range(ncore):
            for z in range(nz):
                refs[core][0, c, z, 0] = value[:, core, z]
    for sum_ref in refs[ncore:]:
        sum_ref[0] = jnp.sum(left.astype(f32), axis=0, keepdims=True)


def sums_kernel(counts, *refs):
    in_refs, out_refs = refs[: sum(counts)], refs[sum(counts) :]
    for n, out_ref in enumerate(out_refs):
        value = in_refs[sum(counts[:n])][...].astype(f32)
        for ref in in_refs[sum(counts[:n]) + 1 : sum(counts[: n + 1])]:
            value = value + ref[...].astype(f32)
        out_ref[...] = value.astype(bf16)


def make_local(nz, ncore, nrow, ncol):
    blocks = ncore * nrow
    sizes = {"z": nz, "core": ncore, "row": nrow, "col": ncol}

    def bits(axis):
        return [1 << k for k in range(sizes[axis].bit_length() - 1)]

    def exchange(values, axis, bit):
        return lax.ppermute(values, axis, [(i, i ^ bit) for i in range(sizes[axis])])

    class Slots:
        def __init__(self):
            self.before, self.now = [], []

        def advance(self):
            self.before, self.now = self.now, []

        def note(self, *values):
            self.now.extend(values)

        def gate(self, *values):
            if not self.before:
                return values
            return lax.optimization_barrier((*values, *self.before))[: len(values)]

        def move(self, values, axis, bit):
            got = exchange(values, axis, bit)
            self.now.append(got)
            return got

        def send(self, values, axis, bit):
            return self.move(self.gate(values)[0], axis, bit)

        def widen(self, parts, axis, lead=True):
            parts = list(self.gate(*parts))
            if lead:
                parts = [joined(parts)[None]]
            for bit in bits(axis):
                values = joined(parts)
                parts = [values, self.move(values, axis, bit)]
            return parts

        def fold(self, held, axis, dim):
            for bit in [bit for bit in reversed(bits(axis)) if bit < held[0][1][dim][1]]:
                got = self.move((yield [half_of(view, dim, 1) for view in held]), axis, bit)
                held = [half_of(view, dim, 0) for view in held] + [view_of(got)]
            return held

        def together(self, *stages):
            running = []
            for job, name in stages:
                stage = getattr(job, name)()
                running.append((job.name + "_" + name, stage, next(stage)))
            while running:
                counts = [len(views) for _, _, views in running]
                arrays = self.gate(*[view[0] for _, _, views in running for view in views])
                spans = [view[1] for _, _, views in running for view in views]
                with jax.named_scope("sums"):
                    values = sums_of(counts, arrays, spans)
                waiting = []
                for (name, stage, _), value in zip(running, values):
                    with jax.named_scope(name):
                        try:
                            waiting.append((name, stage, stage.send(value)))
                        except StopIteration:
                            pass
                running = waiting

    def sums_of(counts, arrays, spans):
        def spec(array, span):
            block = tuple(size for _, size in span) + array.shape[3:]
            index = tuple(start // size for start, size in span) + (0,) * (array.ndim - 3)
            return pl.BlockSpec(block, lambda t: index)

        firsts = [sum(counts[:n]) for n in range(len(counts))]
        shapes = [tuple(size for _, size in spans[n]) + arrays[n].shape[3:] for n in firsts]
        moved = sum(math.prod(size for _, size in span) * math.prod(a.shape[3:]) for a, span in zip(arrays, spans))
        return call(
            functools.partial(sums_kernel, counts),
            (1,),
            [spec(array, span) for array, span in zip(arrays, spans)],
            [summed(shape) for shape in shapes],
            [jax.ShapeDtypeStruct(shape, bf16) for shape in shapes],
            moved,
            3 * moved,
            "sums",
            vmem=16,
        )(*arrays)

    def joined(parts):
        return parts[0] if len(parts) == 1 else jnp.concatenate(parts)

    def view_of(array):
        return (array, tuple((0, n) for n in array.shape[:3]))

    def half_of(view, dim, which):
        array, spans = view
        start, size = spans[dim]
        size //= 2
        return (array, spans[:dim] + ((start + which * size, size),) + spans[dim + 1 :])

    def total(held):
        value = None
        for array, spans in held:
            part = array[tuple(slice(start, start + size) for start, size in spans)].astype(f32)
            value = part if value is None else value + part
        return value

    class Gather:
        def __init__(self, name, slots, shard):
            self.name, self.slots, self.low = name, slots, [shard[None]]

        def z_all(self):
            (values,) = self.slots.gate(*self.low)
            near = nz // 2
            parts = [values] + [self.slots.move(values, "z", k) for k in range(1, nz)]
            self.low, self.high = parts[:near], parts[near:]

        def z_low(self):
            parts = list(self.slots.gate(*self.low))
            for bit in bits("z")[:-1]:
                values = joined(parts)
                parts = [values, self.slots.move(values, "z", bit)]
            self.low = parts

        def z_high(self):
            values = joined(list(self.slots.gate(*self.low)))
            self.low = [values]
            self.high = [self.slots.move(values, "z", bits("z")[-1])]

        def z_high_first(self):
            values = joined(list(self.slots.gate(*self.low)))
            half = values.shape[0] // 2
            self.low = [values[:half], values[half:]]
            self.high = [self.slots.move(self.low[0], "z", bits("z")[-1])]

        def z_high_second(self):
            (values,) = self.slots.gate(self.low[1])
            self.high.append(self.slots.move(values, "z", bits("z")[-1]))

        def x_low(self):
            self.low_row = self.slots.widen(self.low, "row")

        def y_high(self):
            self.high_col = self.slots.widen(self.high, "col")

        def y_low(self):
            self.low_all = self.slots.widen(self.low_row, "col")

        def x_high(self):
            self.high_all = self.slots.widen(self.high_col, "row")

        def y(self):
            self.all_col = self.slots.widen(self.low + self.high, "col")

        def x(self):
            self.all_row = self.slots.widen(self.all_col, "row")

        def core_near(self):
            self.near = [[self.slots.move(p[0], "core", k) for k in range(1, ncore)] for p in (self.low_all, self.high_all)]

        def core(self):
            if hasattr(self, "all_row"):
                lists = [(2, self.all_row)]
            else:
                lists = [(0, self.low_all), (1, self.high_all)]
            self.places, self.pieces = [], []
            for half, parts in lists:
                parts = self.slots.gate(*parts)
                for k in range(ncore):
                    first = 0
                    for n, values in enumerate(parts):
                        self.places.append((k, half, first))
                        if k and n == 0 and hasattr(self, "near"):
                            self.pieces.append(self.near[half][k - 1])
                        else:
                            self.pieces.append(self.slots.move(values, "core", k) if k else values)
                        first += values.shape[0]

    class Scatter:
        def __init__(self, name, slots):
            self.name, self.slots, self.low, self.high = name, slots, [], []

        def halve(self, arrays):
            views = [view_of(array) for array in arrays]
            self.low = self.low + [half_of(view, 2, 0) for view in views]
            self.high = self.high + [half_of(view, 2, 1) for view in views]

        def first_fold(self, parts, axis, dim):
            parts = list(self.slots.gate(*parts))
            held = []
            for bit in reversed(bits(axis)):
                value = parts[bit] if bit == 1 else jnp.concatenate(parts[bit : 2 * bit], axis=dim)
                if held:
                    value = (value.astype(f32) + total([half_of(view, dim, 1) for view in held])).astype(bf16)
                got = self.slots.move(value, axis, bit)
                held = [half_of(view, dim, 0) for view in held] + [view_of(got)]
            return [view_of(parts[0])] + held

        def x_high_first(self, by_row):
            self.high = self.first_fold(by_row, "row", 0)

        def y_low_first(self, by_col):
            self.low = self.first_fold(by_col, "col", 1)

        def x_high(self):
            self.high = yield from self.slots.fold(self.high, "row", 0)

        def y_low(self):
            self.low = yield from self.slots.fold(self.low, "col", 1)

        def y_high(self):
            self.high = yield from self.slots.fold(self.high, "col", 1)

        def x_low(self):
            self.low = yield from self.slots.fold(self.low, "row", 0)

        def z_high(self):
            value = yield self.high
            self.low = self.low + [view_of(self.slots.move(value, "z", nz // 2))]

        def z_low(self):
            held = self.low
            for bit in reversed(bits("z")[:-1]):
                value = yield [half_of(view, 2, 1) for view in held]
                held = [half_of(view, 2, 0) for view in held] + [view_of(self.slots.move(value, "z", bit))]
            self.low = held

        def far_high(self):
            value = yield self.high
            self.got_high = view_of(self.slots.move(value, "row", nrow // 2))

        def far_low(self):
            value = yield self.low
            self.got_low = view_of(self.slots.move(value, "row", nrow // 2))

        def result(self):
            arrays = self.slots.gate(*[view[0] for view in self.low])
            return total([(array, view[1]) for array, view in zip(arrays, self.low)])[0, 0, 0]

    class TokensIn:
        def __init__(self, name, slots, values):
            self.name, self.slots, self.values, self.parts, self.blocks = name, slots, values, [], {}

        def slices(self, which):
            (values,) = self.slots.gate(self.values)
            rows = values.shape[0] // ncol
            here = lax.axis_index("col")
            size = rows // 2
            starts = [(here ^ k) * rows + which * size for k in range(ncol)]
            self.blocks[which] = [lax.dynamic_slice_in_dim(values, start, size, 0) for start in starts]
            self.slots.note(*self.blocks[which])

        def step(self, which):
            own, *sent = self.blocks[which]
            sent = self.slots.gate(*sent)
            self.parts.append([own] + [self.slots.move(block, "col", k + 1) for k, block in enumerate(sent)])

        def first(self):
            self.step(0)

        def second(self):
            self.step(1)

        def end(self):
            count = len(self.parts[0])
            flat = self.slots.gate(*[part for parts in self.parts for part in parts])
            rows = [jnp.concatenate(flat[i : i + count], axis=1) for i in range(0, len(flat), count)]
            return jnp.concatenate(rows)

        def operands(self):
            size = self.parts[0][0].shape[0]
            if size % LEN:
                values = self.end()
                return [values], [pl.BlockSpec((LEN, values.shape[1]), lambda t: (t, 0))]
            half = size // LEN
            values = list(self.slots.gate(*[part for parts in self.parts for part in parts]))
            shape = (LEN, values[0].shape[1])
            near = pl.BlockSpec(shape, lambda t: (jnp.minimum(t, half - 1), 0))
            far = pl.BlockSpec(shape, lambda t: (jnp.maximum(t - half, 0), 0))
            return values, [near] * ncol + [far] * ncol

    def do(job, *stages):
        for stage in stages:
            with jax.named_scope(job.name + "_" + stage):
                getattr(job, stage)()

    class TokensOut:
        def __init__(self, name, slots, own, other):
            self.name, self.slots, self.own, self.other = name, slots, own, other

        @staticmethod
        def space(slots, rows, width, dtype):
            zeros = lax.optimization_barrier(jnp.zeros((rows * ncol, width), dtype))
            slots.note(zeros)
            return zeros

        def send(self):
            self.blocks = [self.slots.send(self.other[k - 1], "col", k) for k in range(1, ncol)]

        def end(self, result):
            rows = self.own.shape[0]
            here = lax.axis_index("col")
            first, *rest = self.slots.gate(self.own, *self.blocks)
            result = lax.dynamic_update_slice_in_dim(result, first, here * rows, 0)
            for k, block in enumerate(rest):
                result = lax.dynamic_update_slice_in_dim(
                    result, block.astype(self.own.dtype), (here ^ (k + 1)) * rows, 0
                )
            return result

    def local(
        tokens,
        key_mask,
        first_gain,
        first_shift,
        qkv_weight,
        qkv_bias,
        out_weight,
        out_bias,
        second_gain,
        second_shift,
        up_weight,
        up_bias,
        down_weight,
        down_bias,
        cotangent,
    ):
        count = tokens.shape[0] // ncol
        seqs = count // LEN
        part, piece, width = out_weight.shape
        heads = part * nrow
        flat = heads * HD
        hidden_part = up_weight.shape[0]
        step = nz * hidden_part
        dim = width * ncol
        hidden = step * blocks
        pairs = heads // 2
        moved = count * dim

        def tile(shape, index=None):
            return pl.BlockSpec(shape, index or (lambda t: (t,) + (0,) * (len(shape) - 1)))

        slots = Slots()
        q = Gather("qkv", slots, qkv_weight.reshape(3 * part, piece, width).astype(bf16))
        o = Gather("out", slots, out_weight.astype(bf16))
        u = Gather("up", slots, up_weight.astype(bf16))
        d = Gather("down", slots, down_weight.astype(bf16))
        tok = TokensIn("tokens", slots, tokens)
        cot = TokensIn("cotangent", slots, cotangent)
        vectors = jnp.stack([first_gain, first_shift, second_gain, second_shift, out_bias, down_bias])

        small = [jnp.concatenate([qkv_bias.reshape(-1), up_bias]).astype(bf16)[None]]
        features = jnp.concatenate([vectors.reshape(-1), key_mask.reshape(-1).astype(f32)])
        tok.slices(0)
        do(q, "z_all")
        do(tok, "first")
        features = slots.widen([features], "col")
        slots.advance()
        spaces = [TokensOut.space(slots, count, width, dtype) for dtype in (bf16, f32)]
        do(q, "x_low", "y_high")
        do(o, "z_low")
        do(u, "z_low")
        small = slots.widen(small, "z", False)
        small = slots.widen(small, "row")
        tok.slices(1)
        slots.advance()
        do(q, "y_low", "x_high")
        do(o, "z_high")
        do(u, "z_high")
        do(tok, "second")
        small = slots.widen(small, "core")
        slots.advance()
        do(q, "core")
        do(o, "y")
        do(d, "z_low")
        cot.slices(0)
        small_all = joined(list(slots.gate(*small))).astype(f32)
        qkv_count = qkv_bias.size
        qkv_offset = small_all[..., :qkv_count].reshape(ncore, nrow, nz, 2, part, piece)
        qkv_offset = jnp.transpose(qkv_offset, (3, 1, 4, 0, 2, 5)).reshape(2, flat)
        up_offset = small_all[..., qkv_count:].reshape(1, hidden)
        features = joined(list(slots.gate(*features)))
        vectors, nearby = features[:, : vectors.size], features[:, vectors.size :]
        vectors = jnp.transpose(vectors.reshape(ncol, 6, width), (1, 0, 2)).reshape(6, dim)
        slots.note(vectors, qkv_offset, up_offset)
        slots.advance()
        inputs, input_specs = tok.operands()
        parts = len(inputs)
        gain_one, shift_one, gain_two, shift_two, out_offset, down_offset = [vectors[i : i + 1] for i in range(6)]

        here = lax.axis_index("col")
        nearby = nearby.reshape((ncol,) + key_mask.shape)
        masks = jnp.zeros_like(nearby)
        for k in range(ncol):
            masks = lax.dynamic_update_slice_in_dim(masks, nearby[k : k + 1], here ^ k, 0)
        masks = masks.reshape(-1, key_mask.shape[1])
        first_seq = (lax.axis_index("row") * ncol + here) * seqs
        masks = lax.dynamic_slice_in_dim(masks, first_seq, seqs, 0)
        visible = jnp.concatenate([jnp.ones((seqs, BUF), f32), masks], axis=1)

        def head_operands(w, kinds):
            half = nz // 2
            places = []
            for k, r, c, z in itertools.product(range(ncore), range(nrow), range(ncol), range(nz)):
                for n, ((in_core, in_half, first), values) in enumerate(zip(w.places, w.pieces)):
                    lead, second, inner = (c, r, z) if in_half == 0 else (r, c, z - half * (in_half == 1))
                    held = in_half == 2 or in_half == z // half
                    if held and in_core == k and first <= lead < first + values.shape[0]:
                        index = (lead - first, second, inner)
                        places.append((n, index, r * part, (k * nz + z) * piece, c * width))
            if piece % 8 == 0:
                specs = [pl.BlockSpec(memory_space=pl.ANY)] * len(w.pieces)
                scratch = [pltpu.VMEM((kinds, heads, HD, dim), bf16), pltpu.SemaphoreType.DMA((kinds,))]
                return w.pieces, specs, scratch, (tuple(places), kinds, part)
            matrix = jnp.zeros((kinds, heads, HD, dim), bf16)
            for n, index, head, row, lane in places:
                block = w.pieces[n][index][: kinds * part].reshape(kinds, part, piece, width)
                matrix = lax.dynamic_update_slice(matrix, block, (0, head, row, lane))
            return [matrix.reshape(kinds, flat, dim)], [whole((kinds, flat, dim))], [], None

        qkv_ops, qkv_specs, qkv_scratch, qkv_layout = head_operands(q, 3)

        tokens_spec = tile((LEN, dim))
        hidden_spec = tile((LEN, hidden))
        half_step = step // 2
        vector_spec = whole((1, dim))
        three = pl.BlockSpec((3, LEN, flat), lambda t: (0, t, 0))
        own_spec = tile((LEN, width))
        other_spec = pl.BlockSpec((ncol - 1, LEN, width), lambda t: (0, t, 0))

        def out_of(*shape, dtype=bf16):
            return jax.ShapeDtypeStruct(shape, dtype)

        def ffn_operands(w):
            operands = [p.reshape(p.shape[0], p.shape[1], half_step, width) for p in w.pieces]
            return operands, [whole(p.shape) for p in operands], (ncol, nrow, ncore, tuple(w.places))

        do(u, "x_low", "y_high")
        do(o, "x")
        do(d, "z_high")
        do(cot, "first")
        normed, qkv = call(
            functools.partial(qkv_kernel, qkv_layout, parts),
            (seqs,),
            [vector_spec, vector_spec, whole((2, flat))] + input_specs + qkv_specs,
            [tokens_spec, three],
            [out_of(count, dim), out_of(3, count, flat)],
            6 * moved * flat,
            6 * flat * dim + 10 * moved,
            "qkv",
            scratch=qkv_scratch,
        )(gain_one, shift_one, qkv_offset, *inputs, *qkv_ops)
        slots.note(qkv)
        slots.advance()

        do(u, "y_low", "x_high", "core_near")
        do(o, "core")
        quads = flat // QUAD
        step_lanes = STEP * QUAD
        queries = HELD * LEN
        attended, probs = call(
            attend_kernel,
            (seqs, quads // STEP),
            [
                pl.BlockSpec((3, LEN, step_lanes), lambda s, p: (0, s, p)),
                pl.BlockSpec((1, LEN, 1), lambda s, p: (s, 0, 0)),
            ],
            [
                pl.BlockSpec((LEN, step_lanes), lambda s, p: (s, p)),
                pl.BlockSpec((1, STEP, LEN, queries), lambda s, p: (s, p, 0, 0)),
            ],
            [out_of(count, flat), out_of(seqs, quads, LEN, queries)],
            16 * count * LEN * flat,
            8 * moved + 2 * seqs * quads * LEN * queries,
            "attend",
        )(slots.gate(qkv)[0], visible[:, :, None])
        slots.note(attended)
        slots.advance()

        do(u, "core")
        do(d, "x_low", "y_high")
        out_ops, out_specs, out_scratch, out_layout = head_operands(o, 1)
        middle, normed_two = call(
            functools.partial(out_kernel, out_layout, parts),
            (seqs,),
            [tile((LEN, flat)), vector_spec, vector_spec, vector_spec] + input_specs + out_specs,
            [tokens_spec, tokens_spec],
            [out_of(count, dim, dtype=f32), out_of(count, dim)],
            2 * moved * flat,
            2 * flat * dim + 10 * moved,
            "out",
            scratch=out_scratch,
        )(slots.gate(attended)[0], out_offset, gain_two, shift_two, *inputs, *out_ops)
        slots.note(normed_two)
        slots.advance()

        do(d, "y_low", "x_high", "core_near")
        cot.slices(1)
        up_ops, up_specs, up_dims = ffn_operands(u)
        hid, slope = call(
            functools.partial(up_kernel, up_dims),
            (seqs,),
            [tokens_spec, whole((1, hidden))] + up_specs,
            [hidden_spec, hidden_spec],
            [out_of(count, hidden), out_of(count, hidden)],
            8 * moved * hidden,
            2 * hidden * dim + 4 * count * hidden,
            "up",
        )(slots.gate(normed_two)[0], up_offset, *up_ops)
        slots.note(hid)
        slots.advance()

        def ffn_sent(left, right, name):
            return call(
                functools.partial(ffn_sent_kernel, ncol),
                (2, nrow),
                [
                    pl.BlockSpec((count, half_step), lambda h, r: (0, (nrow + r) * 2 + h)),
                    whole((count, dim)),
                ],
                pl.BlockSpec((1, 1, ncol, half_step, width), lambda h, r: (h, r, 0, 0, 0)),
                out_of(2, nrow, ncol, half_step, width),
                2 * moved * hidden // ncore,
                2 * (hidden * dim + count * hidden) // ncore + 2 * moved,
                name,
            )(slots.gate(left)[0], right)

        def ffn_kept(left, right, got, name):
            by_col = pl.BlockSpec((1, half_step, width), lambda h, r: (jnp.where(h == 0, r, nrow - 1), 0, 0))
            out = call(
                functools.partial(ffn_kept_kernel, ncol, nrow),
                (2, nrow),
                [
                    pl.BlockSpec((count, half_step), lambda h, r: (0, r * 2 + h)),
                    whole((count, dim)),
                    pl.BlockSpec((1, 1, ncol, half_step, width), lambda h, r: (h, r, 0, 0, 0)),
                ],
                [by_col] * ncol + [summed((ncol, half_step, width))] * nrow,
                [out_of(nrow, half_step, width)] * ncol + [out_of(ncol, half_step, width)] * nrow,
                2 * moved * hidden // ncore,
                3 * (hidden * dim + count * hidden) // ncore + 2 * moved,
                name,
            )(left, right, got)
            shape = (nz // 2, hidden_part, width)
            slots.note(out[0])
            low = [values.reshape((nrow, 1) + shape) for values in out[:ncol]]
            return low, [values.reshape((1, ncol) + shape) for values in out[ncol:]]

        def head_grad(left, right, first, name, sums=False):
            kinds, _, lanes = left.shape
            rows = lanes // (part * HD)
            out = call(
                functools.partial(head_grad_kernel, (ncore, ncol, nz, part, piece)),
                (kinds, rows),
                [
                    pl.BlockSpec((1, count, part * HD), lambda i, r: (i, 0, r)),
                    whole((count, dim)),
                ],
                [pl.BlockSpec((1, ncol, nz, 1, part, piece, width), lambda i, r: (r, 0, 0, i, 0, 0, 0))] * ncore
                + [pl.BlockSpec((1, 1, part * HD), lambda i, r: (i, 0, r))] * sums,
                [out_of(rows, ncol, nz, kinds, part, piece, width)] * ncore
                + [out_of(kinds, 1, lanes, dtype=f32)] * sums,
                2 * moved * lanes * kinds,
                2 * kinds * (lanes * dim + count * lanes) + 2 * moved,
                name,
            )(left, right)
            slots.note(out[0])
            return out[:ncore], out[ncore:]

        def core_fold(name, sums, gated=True):
            with jax.named_scope(name + "_core"):
                sent = slots.gate(*sums[1:]) if gated else sums[1:]
                return [sums[0]] + [slots.move(values, "core", k + 1) for k, values in enumerate(sent)]

        def pull(first, rows):
            lanes = rows * part * HD
            which = first // rows
            kinds = 3

            def seq(t):
                return jnp.minimum(t, seqs - 1)

            def kind_row(t):
                step_after = jnp.maximum(t - seqs, 0)
                return step_after // rows, step_after % rows

            def sums_at(t):
                kind, row = kind_row(t)
                return (row, 0, 0, kind, 0, 0, 0)

            def own_at(t):
                kind, row = kind_row(t)
                return (kind, 0, row)

            out = call(
                functools.partial(attend_pull_kernel, seqs, (ncore, ncol, nz, part, piece)),
                (seqs + kinds * rows,),
                [
                    pl.BlockSpec((kinds, LEN, lanes), lambda t: (0, seq(t), which)),
                    pl.BlockSpec((1, STEP, LEN, queries), lambda t: (seq(t), which, 0, 0)),
                    pl.BlockSpec((LEN, lanes), lambda t: (seq(t), which)),
                    whole((count, dim)),
                ],
                [pl.BlockSpec((kinds, LEN, lanes), lambda t: (0, seq(t), 0))]
                + [pl.BlockSpec((1, ncol, nz, 1, part, piece, width), sums_at)] * ncore
                + [pl.BlockSpec((1, 1, part * HD), own_at)],
                [out_of(kinds, count, lanes)]
                + [out_of(rows, ncol, nz, kinds, part, piece, width)] * ncore
                + [out_of(kinds, 1, lanes, dtype=f32)],
                30 * count * LEN * lanes + 2 * moved * lanes * kinds,
                14 * moved * rows // nrow,
                "attend_pull",
                scratch=[pltpu.VMEM((kinds, count, lanes), bf16)],
            )(qkv, probs, slots.gate(attended_grad)[0], normed)
            slots.note(out[0])
            return out[0], out[1 : 1 + ncore], out[1 + ncore]

        do(d, "core")
        do(cot, "second")
        down_ops, down_specs, down_dims = ffn_operands(d)
        own, other = call(
            functools.partial(down_kernel, down_dims),
            (seqs,),
            [hidden_spec, tokens_spec, vector_spec] + down_specs,
            [own_spec, other_spec],
            [out_of(count, width), out_of(ncol - 1, count, width)],
            2 * moved * hidden,
            2 * hidden * dim + 2 * count * hidden + 6 * moved,
            "down",
        )(hid, middle, down_offset, *down_ops)
        slots.note(own)
        slots.advance()

        dg, ug, og, qg = [Scatter(name, slots) for name in ("down_grad", "up_grad", "out_grad", "qkv_grad")]
        activations = TokensOut("activations", slots, own, other)
        do(activations, "send")
        grad_low = cot.end()
        sent = ffn_sent(hid, grad_low, "down_grad")
        (got,) = core_fold("down_grad", [sent, sent], False)[1:]
        upward_grad, up_bias_sum = call(
            functools.partial(hidden_pull_kernel, down_dims),
            (seqs,),
            [tokens_spec, hidden_spec] + down_specs,
            [hidden_spec, summed((1, hidden))],
            [out_of(count, hidden), out_of(1, hidden, dtype=f32)],
            2 * moved * hidden,
            2 * hidden * dim + 4 * count * hidden,
            "hidden_pull",
        )(slots.gate(grad_low)[0], slope, *down_ops)
        slots.note(upward_grad)
        down_low, down_high = ffn_kept(hid, grad_low, got, "down_grad")
        slots.advance()

        with jax.named_scope("down_grad_first"):
            dg.x_high_first(down_high)
            dg.y_low_first(down_low)
        sent = ffn_sent(upward_grad, normed_two, "up_grad")
        (got,) = core_fold("up_grad", [sent, sent], False)[1:]
        middle_grad, branch_low, attended_grad, sums_two = call(
            functools.partial(middle_pull_kernel, up_dims, out_layout),
            (seqs,),
            [hidden_spec, tokens_spec, tokens_spec, vector_spec] + up_specs + out_specs,
            [tokens_spec, tokens_spec, tile((LEN, flat)), summed((4, dim))],
            [
                out_of(count, dim, dtype=f32),
                out_of(count, dim),
                out_of(count, flat),
                out_of(4, dim, dtype=f32),
            ],
            2 * moved * (hidden + flat),
            2 * hidden * dim + 2 * count * hidden + 14 * moved,
            "middle_pull",
            scratch=out_scratch,
        )(slots.gate(upward_grad)[0], middle, grad_low, gain_two, *up_ops, *out_ops)
        slots.note(attended_grad)
        slots.advance()

        slots.together((dg, "y_high"), (dg, "x_low"))
        out_sums, _ = head_grad(slots.gate(attended)[0][None], branch_low, 0, "out_grad")
        up_low, up_high = ffn_kept(slots.gate(upward_grad)[0], normed_two, got, "up_grad")
        slots.advance()

        with jax.named_scope("up_grad_first"):
            ug.x_high_first(up_high)
            ug.y_low_first(up_low)
        slots.together((dg, "z_high"))
        out_held = core_fold("out_grad", out_sums)
        far, far_sums, far_own = pull(nrow // 2, nrow // 2)
        slots.note(*far_sums)
        slots.advance()

        far_held = core_fold("qkv_grad_far", far_sums)
        activations = activations.end(spaces[0])
        slots.note(activations)
        slots.together((ug, "y_high"), (ug, "x_low"))
        slots.advance()

        far_low = Scatter("qkv_grad_far", slots)
        far_low.halve(far_held)
        og.halve(out_held)
        slots.together(
            (far_low, "far_high"), (far_low, "y_low"), (ug, "z_high"), (og, "x_high"), (og, "y_low")
        )
        near, near_sums, near_own = pull(0, nrow // 2)
        slots.note(*near_sums)
        slots.advance()

        near_held = core_fold("qkv_grad_near", near_sums)
        slots.together((far_low, "far_low"), (og, "y_high"), (og, "x_low"), (dg, "z_low"))
        slots.advance()

        qg.halve(near_held)
        qg.high = qg.high + [far_low.got_high]
        if nrow > 2:
            slots.together((qg, "x_high"))
        slots.together((qg, "y_high"), (qg, "y_low"), (og, "z_high"), (ug, "z_low"))
        down_grad = dg.result()
        own_grad, other_grad, sums_one = call(
            functools.partial(token_pull_kernel, ncol, qkv_layout, parts),
            (seqs,),
            [pl.BlockSpec((3, LEN, flat // 2), lambda t: (0, t, 0))] * 2
            + [tokens_spec, vector_spec]
            + input_specs
            + qkv_specs,
            [own_spec, other_spec, summed((2, dim))],
            [
                out_of(count, width, dtype=f32),
                out_of(ncol - 1, count, width),
                out_of(2, dim, dtype=f32),
            ],
            6 * moved * flat,
            6 * flat * dim + 14 * moved,
            "token_pull",
            scratch=qkv_scratch,
        )(slots.gate(near)[0], far, middle_grad, gain_one, *inputs, *qkv_ops)
        slots.note(own_grad)
        slots.advance()

        bias_sum = jnp.concatenate([near_own, far_own], axis=2)[::2].reshape(2, nrow, part, ncore, nz, piece)
        bias_sum = jnp.transpose(bias_sum, (3, 1, 4, 0, 2, 5)).reshape(ncore, nrow, nz, qkv_count)
        bias_sum = jnp.concatenate([bias_sum, up_bias_sum.reshape(ncore, nrow, nz, hidden_part)], axis=-1)
        sums = jnp.concatenate([sums_one, sums_two])
        size = sums.shape[0] * width
        flat_bias = bias_sum.reshape(-1)
        packs = [jnp.concatenate([sums[:, :width].reshape(-1), flat_bias])]

        def small_sums():
            (pack,) = slots.gate(packs[0])
            for k in range(1, ncol):
                far_part = sums[:, k * width : (k + 1) * width].reshape(-1)
                pack = pack + slots.send(jnp.concatenate([far_part, flat_bias]), "col", k)
            for axis in ("core", "row", "z"):
                for bit in reversed(bits(axis)):
                    rest = pack[size:]
                    half = rest.size // 2
                    got = slots.move(jnp.concatenate([pack[:size], rest[half:]]), axis, bit)
                    pack = pack[: size + half] + got
            packs[0] = pack

        token_grad = TokensOut("token_grad", slots, own_grad, other_grad)
        do(token_grad, "send")
        qg.low = qg.low + [far_low.got_low]
        if nrow > 2:
            slots.together((qg, "x_low"))
        slots.together((qg, "z_high"), (og, "z_low"))
        with jax.named_scope("small_sums"):
            small_sums()
        up_grad = ug.result()
        slots.note(up_grad)
        slots.advance()

        slots.together((qg, "z_low"))
        token_grad = token_grad.end(spaces[1])
        out_grad, qkv_grad = og.result(), qg.result()

        pack = packs[0]
        sums = pack[:size].reshape(-1, width)
        bias_sum = pack[size:]
        return (
            activations,
            token_grad,
            sums[0],
            sums[1],
            qkv_grad,
            bias_sum[:qkv_count].reshape(qkv_bias.shape),
            out_grad[0],
            sums[2],
            sums[3],
            sums[4],
            up_grad,
            bias_sum[qkv_count:],
            down_grad,
            sums[5],
        )

    return local


def solution(mesh):
    devices = mesh.devices
    nz, ncore = devices.shape[0] // 2, 2
    nrow, ncol = devices.shape[1], devices.shape[2]
    fine = Mesh(devices.reshape(nz, ncore, nrow, ncol), ("z", "core", "row", "col"))
    dp = ("z", "core")
    rows = P(("z", "core", "row"), "col")
    qkv_weight = P(None, "row", dp, "col")
    qkv_bias = P(None, "row", dp)
    out_weight = P("row", dp, "col")
    feature = P("col")
    unit = P(("z", "core", "row"))
    in_specs = (
        rows,
        P(("z", "core", "col"), None),
        feature,
        feature,
        qkv_weight,
        qkv_bias,
        out_weight,
        feature,
        feature,
        feature,
        rows,
        unit,
        rows,
        feature,
        rows,
    )
    out_specs = (
        rows,
        rows,
        feature,
        feature,
        qkv_weight,
        qkv_bias,
        out_weight,
        feature,
        feature,
        feature,
        rows,
        unit,
        rows,
        feature,
    )
    return jax.shard_map(
        make_local(nz, ncore, nrow, ncol),
        mesh=fine,
        in_specs=in_specs,
        out_specs=out_specs,
        check_vma=False,
    )
```

```python
import functools
import itertools
import math

import jax
import jax.numpy as jnp
from jax import lax
from jax.experimental import pallas as pl
from jax.experimental.pallas import tpu as pltpu
from jax.sharding import Mesh, PartitionSpec as P

HD = 64
HELD = 4
QUAD = HELD * HD
STEP = 2
BUF = 64
LEN = 320
masked_fill = -1000000000.0
norm_epsilon = 1e-06
attn_scale = 0.125
exp2_scale = attn_scale * 1.4426950408889634
root_half = 0.7071067811865476
density = 0.3989422804014327
bf16 = jnp.bfloat16
f32 = jnp.float32
MIB = 1 << 20


def contract_last(left, right):
    return lax.dot_general(left, right, (((1,), (1,)), ((), ())), preferred_element_type=f32)


def contract_first(left, right):
    return lax.dot_general(left, right, (((0,), (0,)), ((), ())), preferred_element_type=f32)


def matmul(left, right):
    return lax.dot_general(left, right, (((1,), (0,)), ((), ())), preferred_element_type=f32)


def whole(shape):
    return pl.BlockSpec(shape, lambda *_: (0,) * len(shape), pipeline_mode=pl.Buffered(1))


def summed(shape):
    return pl.BlockSpec(shape, lambda *_: (0,) * len(shape))


def call(kernel, grid, in_specs, out_specs, out_shape, flops, moved, name, vmem=48, scratch=()):
    return pl.pallas_call(
        kernel,
        grid=grid,
        in_specs=in_specs,
        out_specs=out_specs,
        out_shape=out_shape,
        scratch_shapes=scratch,
        name=name,
        compiler_params=pltpu.CompilerParams(vmem_limit_bytes=vmem * MIB),
        cost_estimate=pl.CostEstimate(flops=flops, bytes_accessed=moved, transcendentals=0),
    )


def unit_norm(values):
    center = jnp.mean(values, axis=1, keepdims=True)
    centered = values - center
    spread = jnp.mean(centered * centered, axis=1, keepdims=True)
    inverse = lax.rsqrt(spread + norm_epsilon)
    return centered * inverse, inverse


def norm_pull(grad, gain, unit, inverse):
    scaled = grad * gain
    total = jnp.mean(scaled, axis=1, keepdims=True)
    paired = jnp.mean(scaled * unit, axis=1, keepdims=True)
    return inverse * (scaled - total - unit * paired)


def head_weight(layout, refs):
    if layout is None:
        return refs[1:], lambda: None, lambda i: refs[0][i]
    places, kinds, part = layout
    held, sem = refs[-2:]
    operands = 1 + max(place[0] for place in places)

    def copies(kind):
        for operand, index, head, row, lane in places:
            source = refs[operand].at[index + (pl.ds(kind * part, part),)]
            _, piece, width = source.shape
            target = held.at[kind, pl.ds(head, part), pl.ds(row, piece), pl.ds(lane, width)]
            yield pltpu.make_async_copy(source, target, sem.at[kind])

    def fetch():
        @pl.when(pl.program_id(0) == 0)
        def _():
            for kind in range(kinds):
                for copy in copies(kind):
                    copy.start()

    def read(kind):
        @pl.when(pl.program_id(0) == 0)
        def _():
            for copy in copies(kind):
                copy.wait()

        return held[kind].reshape(held.shape[1] * held.shape[2], held.shape[3])

    return refs[operands:-2], fetch, read


def token_tile(parts, refs):
    if parts == 1:
        return refs[0][...].astype(f32), refs[1:]
    half = parts // 2
    near = jnp.concatenate([ref[...] for ref in refs[:half]], axis=1).astype(f32)
    far = jnp.concatenate([ref[...] for ref in refs[half:parts]], axis=1).astype(f32)
    return jnp.where(pl.program_id(0) < pl.num_programs(0) // 2, near, far), refs[parts:]


def qkv_kernel(layout, parts, gain_ref, shift_ref, bias_ref, *refs):
    x, refs = token_tile(parts, refs)
    (a_ref, out_ref), fetch, read = head_weight(layout, refs)
    fetch()
    unit, _ = unit_norm(x)
    a = (unit * gain_ref[...] + shift_ref[...]).astype(bf16)
    a_ref[...] = a
    for i in range(3):
        value = contract_last(a, read(i))
        if i != 1:
            value = value + bias_ref[i // 2 : i // 2 + 1]
        out_ref[i] = value.astype(bf16)


def split_heads(held):
    head = lax.broadcasted_iota(jnp.int32, held.shape, 1) // HD
    zero = jnp.zeros_like(held)
    return jnp.concatenate([jnp.where(head == h, held, zero) for h in range(HELD)], axis=0)


def join_heads(all_heads):
    rows = all_heads.shape[0] // HELD
    head = lax.broadcasted_iota(jnp.int32, (rows, all_heads.shape[1]), 1) // HD
    value = all_heads[:rows]
    for h in range(1, HELD):
        value = jnp.where(head == h, all_heads[h * rows : (h + 1) * rows], value)
    return value


def attend_kernel(qkv_ref, mask_ref, out_ref, probs_ref):
    seen = mask_ref[0] > 0
    for n in range(STEP):
        lanes = slice(n * QUAD, (n + 1) * QUAD)
        scores = contract_last(qkv_ref[1, :, lanes], split_heads(qkv_ref[0, :, lanes]))
        scores = jnp.where(seen, scores, masked_fill / attn_scale)
        top = jnp.max(scores, axis=0, keepdims=True)
        grown = jnp.exp2((scores - top) * exp2_scale)
        probs = (grown * (1.0 / jnp.sum(grown, axis=0, keepdims=True))).astype(bf16)
        probs_ref[0, n] = probs
        out_ref[:, lanes] = join_heads(contract_first(probs, qkv_ref[2, :, lanes])).astype(bf16)


def attend_pull_kernel(seqs, sizes, qkv_ref, probs_ref, do_ref, normed_ref, out_ref, *refs):
    ncore, ncol, nz, part, piece = sizes
    sum_refs, (sum_ref, held) = refs[:ncore], refs[ncore:]
    at = pl.program_id(0)
    rows = held.shape[2] // (part * HD)

    @pl.when(at < seqs)
    def _():
        place = pl.ds(pl.multiple_of(at * LEN, LEN), LEN)
        for n in range(STEP):
            lanes = slice(n * QUAD, (n + 1) * QUAD)
            queries = split_heads(qkv_ref[0, :, lanes])
            keys = qkv_ref[1, :, lanes]
            pulled = split_heads(do_ref[:, lanes])
            low = probs_ref[0, n]
            probs = low.astype(f32)
            prob_grad = contract_last(qkv_ref[2, :, lanes], pulled)
            inner = jnp.sum(prob_grad * probs, axis=0, keepdims=True)
            score_grad = (probs * (prob_grad - inner)).astype(bf16)
            value_grad = matmul(low, pulled).astype(bf16)
            key_grad = (matmul(score_grad, queries) * attn_scale).astype(bf16)
            query_grad = join_heads(contract_first(score_grad, keys) * attn_scale).astype(bf16)
            for i, value in enumerate((query_grad, key_grad, value_grad)):
                out_ref[i, :, lanes] = value
                held[i, place, lanes] = value

    @pl.when(at >= seqs)
    def _():
        width = normed_ref.shape[1] // ncol
        kind, row = (at - seqs) // rows, (at - seqs) % rows
        size = part * HD
        left = held[kind, :, pl.ds(pl.multiple_of(row * size, size), size)] if rows > 1 else held[kind]
        for c in range(ncol):
            value = contract_first(left, normed_ref[:, c * width : (c + 1) * width]).astype(bf16)
            value = value.reshape(part, ncore, nz, piece, width)
            for core in range(ncore):
                for z in range(nz):
                    sum_refs[core][0, c, z, 0] = value[:, core, z]
        sum_ref[0] = jnp.sum(left.astype(f32), axis=0, keepdims=True)


def out_kernel(layout, parts, o_ref, bias_ref, gain_ref, shift_ref, *refs):
    x, refs = token_tile(parts, refs)
    (middle_ref, a_ref), fetch, read = head_weight(layout, refs)
    fetch()
    middle = x + (matmul(o_ref[...], read(0)) + bias_ref[...])
    middle_ref[...] = middle
    unit, _ = unit_norm(middle)
    a_ref[...] = (unit * gain_ref[...] + shift_ref[...]).astype(bf16)


def pieces_of(dims, refs):
    ncol, nrow, ncore, places = dims
    w_refs, rest = refs[: len(places)], refs[len(places) :]

    def piece(block, col):
        core, within = divmod(block, 2 * nrow)
        row, half = divmod(within, 2)
        lead, second = (row, col) if half else (col, row)
        for ref, (in_core, in_half, first) in zip(w_refs, places):
            if (in_core, in_half) == (core, half) and first <= lead < first + ref.shape[0]:
                return ref[lead - first, second]

    return piece, 2 * ncore * nrow, w_refs[0].shape[2], w_refs[0].shape[3], rest


def up_kernel(dims, a_ref, bias_ref, *refs):
    piece, blocks, step, width, (hid_ref, slope_ref) = pieces_of(dims, refs)
    for b in range(blocks):
        rows = slice(b * step, (b + 1) * step)
        value = bias_ref[:, rows]
        for c in range(dims[0]):
            value = value + contract_last(a_ref[:, c * width : (c + 1) * width], piece(b, c))
        cdf = 0.5 + 0.5 * lax.erf(value * root_half)
        pdf = jnp.exp(-0.5 * value * value) * density
        hid_ref[:, rows] = (value * cdf).astype(bf16)
        slope_ref[:, rows] = (cdf + value * pdf).astype(bf16)


def down_kernel(dims, hid_ref, middle_ref, bias_ref, *refs):
    piece, blocks, step, width, (own_ref, other_ref) = pieces_of(dims, refs)
    for c in range(dims[0]):
        lanes = slice(c * width, (c + 1) * width)
        value = middle_ref[:, lanes] + bias_ref[:, lanes]
        for b in range(blocks):
            value = value + matmul(hid_ref[:, b * step : (b + 1) * step], piece(b, c))
        if c == 0:
            own_ref[...] = value.astype(bf16)
        else:
            other_ref[c - 1] = value.astype(bf16)


def hidden_pull_kernel(dims, g_ref, slope_ref, *refs):
    piece, blocks, step, width, (du_ref, sum_ref) = pieces_of(dims, refs)

    @pl.when(pl.program_id(0) == 0)
    def _():
        sum_ref[...] = jnp.zeros_like(sum_ref)

    for b in range(blocks):
        rows = slice(b * step, (b + 1) * step)
        value = contract_last(g_ref[:, :width], piece(b, 0))
        for c in range(1, dims[0]):
            value = value + contract_last(g_ref[:, c * width : (c + 1) * width], piece(b, c))
        low = (value * slope_ref[:, rows].astype(f32)).astype(bf16)
        du_ref[:, rows] = low
        sum_ref[:, rows] += jnp.sum(low.astype(f32), axis=0, keepdims=True)


def middle_pull_kernel(dims, layout, du_ref, middle_ref, g_ref, gain_ref, *refs):
    piece, blocks, step, width, rest = pieces_of(dims, refs)
    (grad_ref, low_ref, do_ref, sum_ref), fetch, read = head_weight(layout, rest)
    fetch()

    @pl.when(pl.program_id(0) == 0)
    def _():
        sum_ref[...] = jnp.zeros_like(sum_ref)

    parts = []
    for c in range(dims[0]):
        value = matmul(du_ref[:, :step], piece(0, c))
        for b in range(1, blocks):
            value = value + matmul(du_ref[:, b * step : (b + 1) * step], piece(b, c))
        parts.append(value)
    grad = jnp.concatenate(parts, axis=1)
    unit, inverse = unit_norm(middle_ref[...])
    out_grad = g_ref[...].astype(f32)
    total = out_grad + norm_pull(grad, gain_ref[...], unit, inverse)
    grad_ref[...] = total
    low = total.astype(bf16)
    low_ref[...] = low
    do_ref[...] = contract_last(low, read(0)).astype(bf16)
    sum_ref[0:1] += jnp.sum(low.astype(f32), axis=0, keepdims=True)
    sum_ref[1:2] += jnp.sum(grad * unit, axis=0, keepdims=True)
    sum_ref[2:3] += jnp.sum(grad, axis=0, keepdims=True)
    sum_ref[3:4] += jnp.sum(out_grad, axis=0, keepdims=True)


def token_pull_kernel(ncol, layout, parts, near_ref, far_ref, grad_ref, gain_ref, *refs):
    x, refs = token_tile(parts, refs)
    (own_ref, other_ref, sum_ref), fetch, read = head_weight(layout, refs)
    fetch()

    @pl.when(pl.program_id(0) == 0)
    def _():
        sum_ref[...] = jnp.zeros_like(sum_ref)

    grad = None
    for i in range(3):
        weight = read(i)
        middle = weight.shape[0] // 2
        value = matmul(near_ref[i], weight[:middle]) + matmul(far_ref[i], weight[middle:])
        grad = value if grad is None else grad + value
    unit, inverse = unit_norm(x)
    total = grad_ref[...] + norm_pull(grad, gain_ref[...], unit, inverse)
    width = total.shape[1] // ncol
    own_ref[...] = total[:, :width]
    for c in range(1, ncol):
        other_ref[c - 1] = total[:, c * width : (c + 1) * width].astype(bf16)
    sum_ref[0:1] += jnp.sum(grad * unit, axis=0, keepdims=True)
    sum_ref[1:2] += jnp.sum(grad, axis=0, keepdims=True)


def ffn_sent_kernel(ncol, l_ref, r_ref, out_ref):
    width = r_ref.shape[1] // ncol
    left = l_ref[...]
    for c in range(ncol):
        out_ref[0, 0, c] = contract_first(left, r_ref[:, c * width : (c + 1) * width]).astype(bf16)


def ffn_kept_kernel(ncol, nrow, l_ref, r_ref, got_ref, *out_refs):
    by_col, by_row = out_refs[:ncol], out_refs[ncol:]
    width = r_ref.shape[1] // ncol
    left = l_ref[...]
    half, row = pl.program_id(0), pl.program_id(1)
    values = []
    for c in range(ncol):
        value = contract_first(left, r_ref[:, c * width : (c + 1) * width])
        values.append((value + got_ref[0, 0, c].astype(f32)).astype(bf16))

    @pl.when(half == 0)
    def _():
        for c in range(ncol):
            by_col[c][0] = values[c]

    for r in range(nrow):

        @pl.when((half == 1) & (row == r))
        def _(r=r):
            for c in range(ncol):
                by_row[r][c] = values[c]


def head_grad_kernel(sizes, l_ref, r_ref, *refs):
    ncore, ncol, nz, part, piece = sizes
    width = r_ref.shape[1] // ncol
    left = l_ref[0]
    for c in range(ncol):
        value = contract_first(left, r_ref[:, c * width : (c + 1) * width]).astype(bf16)
        value = value.reshape(part, ncore, nz, piece, width)
        for core in range(ncore):
            for z in range(nz):
                refs[core][0, c, z, 0] = value[:, core, z]
    for sum_ref in refs[ncore:]:
        sum_ref[0] = jnp.sum(left.astype(f32), axis=0, keepdims=True)


def sums_kernel(counts, *refs):
    in_refs, out_refs = refs[: sum(counts)], refs[sum(counts) :]
    for n, out_ref in enumerate(out_refs):
        value = in_refs[sum(counts[:n])][...].astype(f32)
        for ref in in_refs[sum(counts[:n]) + 1 : sum(counts[: n + 1])]:
            value = value + ref[...].astype(f32)
        out_ref[...] = value.astype(bf16)


def make_local(nz, ncore, nrow, ncol):
    blocks = ncore * nrow
    sizes = {"z": nz, "core": ncore, "row": nrow, "col": ncol}

    def bits(axis):
        return [1 << k for k in range(sizes[axis].bit_length() - 1)]

    def exchange(values, axis, bit):
        return lax.ppermute(values, axis, [(i, i ^ bit) for i in range(sizes[axis])])

    class Slots:
        def __init__(self):
            self.before, self.now = [], []

        def advance(self):
            self.before, self.now = self.now, []

        def note(self, *values):
            self.now.extend(values)

        def gate(self, *values):
            if not self.before:
                return values
            return lax.optimization_barrier((*values, *self.before))[: len(values)]

        def move(self, values, axis, bit):
            got = exchange(values, axis, bit)
            self.now.append(got)
            return got

        def send(self, values, axis, bit):
            return self.move(self.gate(values)[0], axis, bit)

        def widen(self, parts, axis, lead=True):
            parts = list(self.gate(*parts))
            if lead:
                parts = [joined(parts)[None]]
            for bit in bits(axis):
                values = joined(parts)
                parts = [values, self.move(values, axis, bit)]
            return parts

        def fold(self, held, axis, dim):
            for bit in [bit for bit in reversed(bits(axis)) if bit < held[0][1][dim][1]]:
                got = self.move((yield [half_of(view, dim, 1) for view in held]), axis, bit)
                held = [half_of(view, dim, 0) for view in held] + [view_of(got)]
            return held

        def together(self, *stages):
            running = []
            for job, name in stages:
                stage = getattr(job, name)()
                running.append((job.name + "_" + name, stage, next(stage)))
            while running:
                counts = [len(views) for _, _, views in running]
                arrays = self.gate(*[view[0] for _, _, views in running for view in views])
                spans = [view[1] for _, _, views in running for view in views]
                with jax.named_scope("sums"):
                    values = sums_of(counts, arrays, spans)
                waiting = []
                for (name, stage, _), value in zip(running, values):
                    with jax.named_scope(name):
                        try:
                            waiting.append((name, stage, stage.send(value)))
                        except StopIteration:
                            pass
                running = waiting

    def sums_of(counts, arrays, spans):
        def spec(array, span):
            block = tuple(size for _, size in span) + array.shape[3:]
            index = tuple(start // size for start, size in span) + (0,) * (array.ndim - 3)
            return pl.BlockSpec(block, lambda t: index)

        firsts = [sum(counts[:n]) for n in range(len(counts))]
        shapes = [tuple(size for _, size in spans[n]) + arrays[n].shape[3:] for n in firsts]
        moved = sum(math.prod(size for _, size in span) * math.prod(a.shape[3:]) for a, span in zip(arrays, spans))
        return call(
            functools.partial(sums_kernel, counts),
            (1,),
            [spec(array, span) for array, span in zip(arrays, spans)],
            [summed(shape) for shape in shapes],
            [jax.ShapeDtypeStruct(shape, bf16) for shape in shapes],
            moved,
            3 * moved,
            "sums",
            vmem=16,
        )(*arrays)

    def joined(parts):
        return parts[0] if len(parts) == 1 else jnp.concatenate(parts)

    def view_of(array):
        return (array, tuple((0, n) for n in array.shape[:3]))

    def half_of(view, dim, which):
        array, spans = view
        start, size = spans[dim]
        size //= 2
        return (array, spans[:dim] + ((start + which * size, size),) + spans[dim + 1 :])

    def total(held):
        value = None
        for array, spans in held:
            part = array[tuple(slice(start, start + size) for start, size in spans)].astype(f32)
            value = part if value is None else value + part
        return value

    class Gather:
        def __init__(self, name, slots, shard):
            self.name, self.slots, self.low = name, slots, [shard[None]]

        def z_all(self):
            (values,) = self.slots.gate(*self.low)
            near = nz // 2
            parts = [values] + [self.slots.move(values, "z", k) for k in range(1, nz)]
            self.low, self.high = parts[:near], parts[near:]

        def z_low(self):
            parts = list(self.slots.gate(*self.low))
            for bit in bits("z")[:-1]:
                values = joined(parts)
                parts = [values, self.slots.move(values, "z", bit)]
            self.low = parts

        def z_high(self):
            values = joined(list(self.slots.gate(*self.low)))
            self.low = [values]
            self.high = [self.slots.move(values, "z", bits("z")[-1])]

        def z_high_first(self):
            values = joined(list(self.slots.gate(*self.low)))
            half = values.shape[0] // 2
            self.low = [values[:half], values[half:]]
            self.high = [self.slots.move(self.low[0], "z", bits("z")[-1])]

        def z_high_second(self):
            (values,) = self.slots.gate(self.low[1])
            self.high.append(self.slots.move(values, "z", bits("z")[-1]))

        def x_low(self):
            self.low_row = self.slots.widen(self.low, "row")

        def y_high(self):
            self.high_col = self.slots.widen(self.high, "col")

        def y_low(self):
            self.low_all = self.slots.widen(self.low_row, "col")

        def x_high(self):
            self.high_all = self.slots.widen(self.high_col, "row")

        def y(self):
            self.all_col = self.slots.widen(self.low + self.high, "col")

        def x(self):
            self.all_row = self.slots.widen(self.all_col, "row")

        def core_near(self):
            self.near = [[self.slots.move(p[0], "core", k) for k in range(1, ncore)] for p in (self.low_all, self.high_all)]

        def core(self):
            if hasattr(self, "all_row"):
                lists = [(2, self.all_row)]
            else:
                lists = [(0, self.low_all), (1, self.high_all)]
            self.places, self.pieces = [], []
            for half, parts in lists:
                parts = self.slots.gate(*parts)
                for k in range(ncore):
                    first = 0
                    for n, values in enumerate(parts):
                        self.places.append((k, half, first))
                        if k and n == 0 and hasattr(self, "near"):
                            self.pieces.append(self.near[half][k - 1])
                        else:
                            self.pieces.append(self.slots.move(values, "core", k) if k else values)
                        first += values.shape[0]

    class Scatter:
        def __init__(self, name, slots):
            self.name, self.slots, self.low, self.high = name, slots, [], []

        def halve(self, arrays):
            views = [view_of(array) for array in arrays]
            self.low = self.low + [half_of(view, 2, 0) for view in views]
            self.high = self.high + [half_of(view, 2, 1) for view in views]

        def first_fold(self, parts, axis, dim):
            parts = list(self.slots.gate(*parts))
            held = []
            for bit in reversed(bits(axis)):
                value = parts[bit] if bit == 1 else jnp.concatenate(parts[bit : 2 * bit], axis=dim)
                if held:
                    value = (value.astype(f32) + total([half_of(view, dim, 1) for view in held])).astype(bf16)
                got = self.slots.move(value, axis, bit)
                held = [half_of(view, dim, 0) for view in held] + [view_of(got)]
            return [view_of(parts[0])] + held

        def x_high_first(self, by_row):
            self.high = self.first_fold(by_row, "row", 0)

        def y_low_first(self, by_col):
            self.low = self.first_fold(by_col, "col", 1)

        def x_high(self):
            self.high = yield from self.slots.fold(self.high, "row", 0)

        def y_low(self):
            self.low = yield from self.slots.fold(self.low, "col", 1)

        def y_high(self):
            self.high = yield from self.slots.fold(self.high, "col", 1)

        def x_low(self):
            self.low = yield from self.slots.fold(self.low, "row", 0)

        def z_high(self):
            value = yield self.high
            self.low = self.low + [view_of(self.slots.move(value, "z", nz // 2))]

        def z_low(self):
            held = self.low
            for bit in reversed(bits("z")[:-1]):
                value = yield [half_of(view, 2, 1) for view in held]
                held = [half_of(view, 2, 0) for view in held] + [view_of(self.slots.move(value, "z", bit))]
            self.low = held

        def far_high(self):
            value = yield self.high
            self.got_high = view_of(self.slots.move(value, "row", nrow // 2))

        def far_low(self):
            value = yield self.low
            self.got_low = view_of(self.slots.move(value, "row", nrow // 2))

        def result(self):
            arrays = self.slots.gate(*[view[0] for view in self.low])
            return total([(array, view[1]) for array, view in zip(arrays, self.low)])[0, 0, 0]

    class TokensIn:
        def __init__(self, name, slots, values):
            self.name, self.slots, self.values, self.parts, self.blocks = name, slots, values, [], {}

        def slices(self, which):
            (values,) = self.slots.gate(self.values)
            rows = values.shape[0] // ncol
            here = lax.axis_index("col")
            size = rows // 2
            starts = [(here ^ k) * rows + which * size for k in range(ncol)]
            self.blocks[which] = [lax.dynamic_slice_in_dim(values, start, size, 0) for start in starts]
            self.slots.note(*self.blocks[which])

        def step(self, which):
            own, *sent = self.blocks[which]
            sent = self.slots.gate(*sent)
            self.parts.append([own] + [self.slots.move(block, "col", k + 1) for k, block in enumerate(sent)])

        def first(self):
            self.step(0)

        def second(self):
            self.step(1)

        def end(self):
            count = len(self.parts[0])
            flat = self.slots.gate(*[part for parts in self.parts for part in parts])
            rows = [jnp.concatenate(flat[i : i + count], axis=1) for i in range(0, len(flat), count)]
            return jnp.concatenate(rows)

        def operands(self):
            size = self.parts[0][0].shape[0]
            if size % LEN:
                values = self.end()
                return [values], [pl.BlockSpec((LEN, values.shape[1]), lambda t: (t, 0))]
            half = size // LEN
            values = list(self.slots.gate(*[part for parts in self.parts for part in parts]))
            shape = (LEN, values[0].shape[1])
            near = pl.BlockSpec(shape, lambda t: (jnp.minimum(t, half - 1), 0))
            far = pl.BlockSpec(shape, lambda t: (jnp.maximum(t - half, 0), 0))
            return values, [near] * ncol + [far] * ncol

    def do(job, *stages):
        for stage in stages:
            with jax.named_scope(job.name + "_" + stage):
                getattr(job, stage)()

    class TokensOut:
        def __init__(self, name, slots, own, other):
            self.name, self.slots, self.own, self.other = name, slots, own, other

        @staticmethod
        def space(slots, rows, width, dtype):
            zeros = lax.optimization_barrier(jnp.zeros((rows * ncol, width), dtype))
            slots.note(zeros)
            return zeros

        def send(self):
            self.blocks = [self.slots.send(self.other[k - 1], "col", k) for k in range(1, ncol)]

        def end(self, result):
            rows = self.own.shape[0]
            here = lax.axis_index("col")
            first, *rest = self.slots.gate(self.own, *self.blocks)
            result = lax.dynamic_update_slice_in_dim(result, first, here * rows, 0)
            for k, block in enumerate(rest):
                result = lax.dynamic_update_slice_in_dim(
                    result, block.astype(self.own.dtype), (here ^ (k + 1)) * rows, 0
                )
            return result

    def local(
        tokens,
        key_mask,
        first_gain,
        first_shift,
        qkv_weight,
        qkv_bias,
        out_weight,
        out_bias,
        second_gain,
        second_shift,
        up_weight,
        up_bias,
        down_weight,
        down_bias,
        cotangent,
    ):
        count = tokens.shape[0] // ncol
        seqs = count // LEN
        part, piece, width = out_weight.shape
        heads = part * nrow
        flat = heads * HD
        hidden_part = up_weight.shape[0]
        step = nz * hidden_part
        dim = width * ncol
        hidden = step * blocks
        pairs = heads // 2
        moved = count * dim

        def tile(shape, index=None):
            return pl.BlockSpec(shape, index or (lambda t: (t,) + (0,) * (len(shape) - 1)))

        slots = Slots()
        q = Gather("qkv", slots, qkv_weight.reshape(3 * part, piece, width).astype(bf16))
        o = Gather("out", slots, out_weight.astype(bf16))
        u = Gather("up", slots, up_weight.astype(bf16))
        d = Gather("down", slots, down_weight.astype(bf16))
        tok = TokensIn("tokens", slots, tokens)
        cot = TokensIn("cotangent", slots, cotangent)
        vectors = jnp.stack([first_gain, first_shift, second_gain, second_shift, out_bias, down_bias])

        small = [jnp.concatenate([qkv_bias.reshape(-1), up_bias]).astype(bf16)[None]]
        features = jnp.concatenate([vectors.reshape(-1), key_mask.reshape(-1).astype(f32)])
        tok.slices(0)
        do(q, "z_all")
        do(tok, "first")
        features = slots.widen([features], "col")
        slots.advance()
        spaces = [TokensOut.space(slots, count, width, dtype) for dtype in (bf16, f32)]
        do(q, "x_low", "y_high")
        do(o, "z_low")
        do(u, "z_low")
        small = slots.widen(small, "z", False)
        small = slots.widen(small, "row")
        tok.slices(1)
        slots.advance()
        do(q, "y_low", "x_high")
        do(o, "z_high")
        do(u, "z_high")
        do(tok, "second")
        small = slots.widen(small, "core")
        slots.advance()
        do(d, "z_low")
        do(q, "core")
        do(o, "y")
        cot.slices(0)
        small_all = joined(list(slots.gate(*small))).astype(f32)
        qkv_count = qkv_bias.size
        qkv_offset = small_all[..., :qkv_count].reshape(ncore, nrow, nz, 2, part, piece)
        qkv_offset = jnp.transpose(qkv_offset, (3, 1, 4, 0, 2, 5)).reshape(2, flat)
        up_offset = small_all[..., qkv_count:].reshape(1, hidden)
        features = joined(list(slots.gate(*features)))
        vectors, nearby = features[:, : vectors.size], features[:, vectors.size :]
        vectors = jnp.transpose(vectors.reshape(ncol, 6, width), (1, 0, 2)).reshape(6, dim)
        slots.note(vectors, qkv_offset, up_offset)
        slots.advance()
        inputs, input_specs = tok.operands()
        parts = len(inputs)
        gain_one, shift_one, gain_two, shift_two, out_offset, down_offset = [vectors[i : i + 1] for i in range(6)]

        here = lax.axis_index("col")
        nearby = nearby.reshape((ncol,) + key_mask.shape)
        masks = jnp.zeros_like(nearby)
        for k in range(ncol):
            masks = lax.dynamic_update_slice_in_dim(masks, nearby[k : k + 1], here ^ k, 0)
        masks = masks.reshape(-1, key_mask.shape[1])
        first_seq = (lax.axis_index("row") * ncol + here) * seqs
        masks = lax.dynamic_slice_in_dim(masks, first_seq, seqs, 0)
        visible = jnp.concatenate([jnp.ones((seqs, BUF), f32), masks], axis=1)

        def head_operands(w, kinds):
            half = nz // 2
            places = []
            for k, r, c, z in itertools.product(range(ncore), range(nrow), range(ncol), range(nz)):
                for n, ((in_core, in_half, first), values) in enumerate(zip(w.places, w.pieces)):
                    lead, second, inner = (c, r, z) if in_half == 0 else (r, c, z - half * (in_half == 1))
                    held = in_half == 2 or in_half == z // half
                    if held and in_core == k and first <= lead < first + values.shape[0]:
                        index = (lead - first, second, inner)
                        places.append((n, index, r * part, (k * nz + z) * piece, c * width))
            if piece % 8 == 0:
                specs = [pl.BlockSpec(memory_space=pl.ANY)] * len(w.pieces)
                scratch = [pltpu.VMEM((kinds, heads, HD, dim), bf16), pltpu.SemaphoreType.DMA((kinds,))]
                return w.pieces, specs, scratch, (tuple(places), kinds, part)
            matrix = jnp.zeros((kinds, heads, HD, dim), bf16)
            for n, index, head, row, lane in places:
                block = w.pieces[n][index][: kinds * part].reshape(kinds, part, piece, width)
                matrix = lax.dynamic_update_slice(matrix, block, (0, head, row, lane))
            return [matrix.reshape(kinds, flat, dim)], [whole((kinds, flat, dim))], [], None

        qkv_ops, qkv_specs, qkv_scratch, qkv_layout = head_operands(q, 3)

        tokens_spec = tile((LEN, dim))
        hidden_spec = tile((LEN, hidden))
        half_step = step // 2
        vector_spec = whole((1, dim))
        three = pl.BlockSpec((3, LEN, flat), lambda t: (0, t, 0))
        own_spec = tile((LEN, width))
        other_spec = pl.BlockSpec((ncol - 1, LEN, width), lambda t: (0, t, 0))

        def out_of(*shape, dtype=bf16):
            return jax.ShapeDtypeStruct(shape, dtype)

        def ffn_operands(w):
            operands = [p.reshape(p.shape[0], p.shape[1], half_step, width) for p in w.pieces]
            return operands, [whole(p.shape) for p in operands], (ncol, nrow, ncore, tuple(w.places))

        do(u, "y_high")
        do(o, "x")
        do(d, "z_high")
        do(cot, "first")
        do(u, "x_low")
        normed, qkv = call(
            functools.partial(qkv_kernel, qkv_layout, parts),
            (seqs,),
            [vector_spec, vector_spec, whole((2, flat))] + input_specs + qkv_specs,
            [tokens_spec, three],
            [out_of(count, dim), out_of(3, count, flat)],
            6 * moved * flat,
            6 * flat * dim + 10 * moved,
            "qkv",
            scratch=qkv_scratch,
        )(gain_one, shift_one, qkv_offset, *inputs, *qkv_ops)
        slots.note(qkv)
        slots.advance()

        do(o, "core")
        do(u, "x_high", "y_low", "core_near")
        quads = flat // QUAD
        step_lanes = STEP * QUAD
        queries = HELD * LEN
        attended, probs = call(
            attend_kernel,
            (seqs, quads // STEP),
            [
                pl.BlockSpec((3, LEN, step_lanes), lambda s, p: (0, s, p)),
                pl.BlockSpec((1, LEN, 1), lambda s, p: (s, 0, 0)),
            ],
            [
                pl.BlockSpec((LEN, step_lanes), lambda s, p: (s, p)),
                pl.BlockSpec((1, STEP, LEN, queries), lambda s, p: (s, p, 0, 0)),
            ],
            [out_of(count, flat), out_of(seqs, quads, LEN, queries)],
            16 * count * LEN * flat,
            8 * moved + 2 * seqs * quads * LEN * queries,
            "attend",
        )(slots.gate(qkv)[0], visible[:, :, None])
        slots.note(attended)
        slots.advance()

        do(u, "core")
        do(d, "x_low", "y_high")
        out_ops, out_specs, out_scratch, out_layout = head_operands(o, 1)
        middle, normed_two = call(
            functools.partial(out_kernel, out_layout, parts),
            (seqs,),
            [tile((LEN, flat)), vector_spec, vector_spec, vector_spec] + input_specs + out_specs,
            [tokens_spec, tokens_spec],
            [out_of(count, dim, dtype=f32), out_of(count, dim)],
            2 * moved * flat,
            2 * flat * dim + 10 * moved,
            "out",
            scratch=out_scratch,
        )(slots.gate(attended)[0], out_offset, gain_two, shift_two, *inputs, *out_ops)
        slots.note(normed_two)
        slots.advance()

        do(d, "y_low", "x_high", "core_near")
        cot.slices(1)
        up_ops, up_specs, up_dims = ffn_operands(u)
        hid, slope = call(
            functools.partial(up_kernel, up_dims),
            (seqs,),
            [tokens_spec, whole((1, hidden))] + up_specs,
            [hidden_spec, hidden_spec],
            [out_of(count, hidden), out_of(count, hidden)],
            8 * moved * hidden,
            2 * hidden * dim + 4 * count * hidden,
            "up",
        )(slots.gate(normed_two)[0], up_offset, *up_ops)
        slots.note(hid)
        slots.advance()

        def ffn_sent(left, right, name):
            return call(
                functools.partial(ffn_sent_kernel, ncol),
                (2, nrow),
                [
                    pl.BlockSpec((count, half_step), lambda h, r: (0, (nrow + r) * 2 + h)),
                    whole((count, dim)),
                ],
                pl.BlockSpec((1, 1, ncol, half_step, width), lambda h, r: (h, r, 0, 0, 0)),
                out_of(2, nrow, ncol, half_step, width),
                2 * moved * hidden // ncore,
                2 * (hidden * dim + count * hidden) // ncore + 2 * moved,
                name,
            )(slots.gate(left)[0], right)

        def ffn_kept(left, right, got, name):
            by_col = pl.BlockSpec((1, half_step, width), lambda h, r: (jnp.where(h == 0, r, nrow - 1), 0, 0))
            out = call(
                functools.partial(ffn_kept_kernel, ncol, nrow),
                (2, nrow),
                [
                    pl.BlockSpec((count, half_step), lambda h, r: (0, r * 2 + h)),
                    whole((count, dim)),
                    pl.BlockSpec((1, 1, ncol, half_step, width), lambda h, r: (h, r, 0, 0, 0)),
                ],
                [by_col] * ncol + [summed((ncol, half_step, width))] * nrow,
                [out_of(nrow, half_step, width)] * ncol + [out_of(ncol, half_step, width)] * nrow,
                2 * moved * hidden // ncore,
                3 * (hidden * dim + count * hidden) // ncore + 2 * moved,
                name,
            )(left, right, got)
            shape = (nz // 2, hidden_part, width)
            slots.note(out[0])
            low = [values.reshape((nrow, 1) + shape) for values in out[:ncol]]
            return low, [values.reshape((1, ncol) + shape) for values in out[ncol:]]

        def head_grad(left, right, first, name, sums=False):
            kinds, _, lanes = left.shape
            rows = lanes // (part * HD)
            out = call(
                functools.partial(head_grad_kernel, (ncore, ncol, nz, part, piece)),
                (kinds, rows),
                [
                    pl.BlockSpec((1, count, part * HD), lambda i, r: (i, 0, r)),
                    whole((count, dim)),
                ],
                [pl.BlockSpec((1, ncol, nz, 1, part, piece, width), lambda i, r: (r, 0, 0, i, 0, 0, 0))] * ncore
                + [pl.BlockSpec((1, 1, part * HD), lambda i, r: (i, 0, r))] * sums,
                [out_of(rows, ncol, nz, kinds, part, piece, width)] * ncore
                + [out_of(kinds, 1, lanes, dtype=f32)] * sums,
                2 * moved * lanes * kinds,
                2 * kinds * (lanes * dim + count * lanes) + 2 * moved,
                name,
            )(left, right)
            slots.note(out[0])
            return out[:ncore], out[ncore:]

        def core_fold(name, sums, gated=True):
            with jax.named_scope(name + "_core"):
                sent = slots.gate(*sums[1:]) if gated else sums[1:]
                return [sums[0]] + [slots.move(values, "core", k + 1) for k, values in enumerate(sent)]

        def pull(first, rows):
            lanes = rows * part * HD
            which = first // rows
            kinds = 3

            def seq(t):
                return jnp.minimum(t, seqs - 1)

            def kind_row(t):
                step_after = jnp.maximum(t - seqs, 0)
                return step_after // rows, step_after % rows

            def sums_at(t):
                kind, row = kind_row(t)
                return (row, 0, 0, kind, 0, 0, 0)

            def own_at(t):
                kind, row = kind_row(t)
                return (kind, 0, row)

            out = call(
                functools.partial(attend_pull_kernel, seqs, (ncore, ncol, nz, part, piece)),
                (seqs + kinds * rows,),
                [
                    pl.BlockSpec((kinds, LEN, lanes), lambda t: (0, seq(t), which)),
                    pl.BlockSpec((1, STEP, LEN, queries), lambda t: (seq(t), which, 0, 0)),
                    pl.BlockSpec((LEN, lanes), lambda t: (seq(t), which)),
                    whole((count, dim)),
                ],
                [pl.BlockSpec((kinds, LEN, lanes), lambda t: (0, seq(t), 0))]
                + [pl.BlockSpec((1, ncol, nz, 1, part, piece, width), sums_at)] * ncore
                + [pl.BlockSpec((1, 1, part * HD), own_at)],
                [out_of(kinds, count, lanes)]
                + [out_of(rows, ncol, nz, kinds, part, piece, width)] * ncore
                + [out_of(kinds, 1, lanes, dtype=f32)],
                30 * count * LEN * lanes + 2 * moved * lanes * kinds,
                14 * moved * rows // nrow,
                "attend_pull",
                scratch=[pltpu.VMEM((kinds, count, lanes), bf16)],
            )(qkv, probs, slots.gate(attended_grad)[0], normed)
            slots.note(out[0])
            return out[0], out[1 : 1 + ncore], out[1 + ncore]

        do(d, "core")
        do(cot, "second")
        down_ops, down_specs, down_dims = ffn_operands(d)
        own, other = call(
            functools.partial(down_kernel, down_dims),
            (seqs,),
            [hidden_spec, tokens_spec, vector_spec] + down_specs,
            [own_spec, other_spec],
            [out_of(count, width), out_of(ncol - 1, count, width)],
            2 * moved * hidden,
            2 * hidden * dim + 2 * count * hidden + 6 * moved,
            "down",
        )(hid, middle, down_offset, *down_ops)
        slots.note(own)
        slots.advance()

        dg, ug, og, qg = [Scatter(name, slots) for name in ("down_grad", "up_grad", "out_grad", "qkv_grad")]
        activations = TokensOut("activations", slots, own, other)
        do(activations, "send")
        grad_low = cot.end()
        sent = ffn_sent(hid, grad_low, "down_grad")
        (got,) = core_fold("down_grad", [sent, sent], False)[1:]
        upward_grad, up_bias_sum = call(
            functools.partial(hidden_pull_kernel, down_dims),
            (seqs,),
            [tokens_spec, hidden_spec] + down_specs,
            [hidden_spec, summed((1, hidden))],
            [out_of(count, hidden), out_of(1, hidden, dtype=f32)],
            2 * moved * hidden,
            2 * hidden * dim + 4 * count * hidden,
            "hidden_pull",
        )(slots.gate(grad_low)[0], slope, *down_ops)
        slots.note(upward_grad)
        down_low, down_high = ffn_kept(hid, grad_low, got, "down_grad")
        slots.advance()

        with jax.named_scope("down_grad_first"):
            dg.x_high_first(down_high)
            dg.y_low_first(down_low)
        sent = ffn_sent(upward_grad, normed_two, "up_grad")
        (got,) = core_fold("up_grad", [sent, sent], False)[1:]
        middle_grad, branch_low, attended_grad, sums_two = call(
            functools.partial(middle_pull_kernel, up_dims, out_layout),
            (seqs,),
            [hidden_spec, tokens_spec, tokens_spec, vector_spec] + up_specs + out_specs,
            [tokens_spec, tokens_spec, tile((LEN, flat)), summed((4, dim))],
            [
                out_of(count, dim, dtype=f32),
                out_of(count, dim),
                out_of(count, flat),
                out_of(4, dim, dtype=f32),
            ],
            2 * moved * (hidden + flat),
            2 * hidden * dim + 2 * count * hidden + 14 * moved,
            "middle_pull",
            scratch=out_scratch,
        )(slots.gate(upward_grad)[0], middle, grad_low, gain_two, *up_ops, *out_ops)
        slots.note(attended_grad)
        slots.advance()

        slots.together((dg, "y_high"), (dg, "x_low"))
        out_sums, _ = head_grad(slots.gate(attended)[0][None], branch_low, 0, "out_grad")
        up_low, up_high = ffn_kept(slots.gate(upward_grad)[0], normed_two, got, "up_grad")
        slots.advance()

        with jax.named_scope("up_grad_first"):
            ug.x_high_first(up_high)
            ug.y_low_first(up_low)
        slots.together((dg, "z_high"))
        out_held = core_fold("out_grad", out_sums)
        far, far_sums, far_own = pull(nrow // 2, nrow // 2)
        slots.note(*far_sums)
        slots.advance()

        far_held = core_fold("qkv_grad_far", far_sums)
        activations = activations.end(spaces[0])
        slots.note(activations)
        slots.together((ug, "y_high"), (ug, "x_low"))
        slots.advance()

        far_low = Scatter("qkv_grad_far", slots)
        far_low.halve(far_held)
        og.halve(out_held)
        slots.together(
            (far_low, "far_high"), (far_low, "y_low"), (ug, "z_high"), (og, "x_high"), (og, "y_low")
        )
        near, near_sums, near_own = pull(0, nrow // 2)
        slots.note(*near_sums)
        slots.advance()

        near_held = core_fold("qkv_grad_near", near_sums)
        slots.together((far_low, "far_low"), (og, "y_high"), (og, "x_low"), (dg, "z_low"))
        slots.advance()

        qg.halve(near_held)
        qg.high = qg.high + [far_low.got_high]
        if nrow > 2:
            slots.together((qg, "x_high"))
        slots.together((qg, "y_high"), (qg, "y_low"), (og, "z_high"), (ug, "z_low"))
        down_grad = dg.result()
        own_grad, other_grad, sums_one = call(
            functools.partial(token_pull_kernel, ncol, qkv_layout, parts),
            (seqs,),
            [pl.BlockSpec((3, LEN, flat // 2), lambda t: (0, t, 0))] * 2
            + [tokens_spec, vector_spec]
            + input_specs
            + qkv_specs,
            [own_spec, other_spec, summed((2, dim))],
            [
                out_of(count, width, dtype=f32),
                out_of(ncol - 1, count, width),
                out_of(2, dim, dtype=f32),
            ],
            6 * moved * flat,
            6 * flat * dim + 14 * moved,
            "token_pull",
            scratch=qkv_scratch,
        )(slots.gate(near)[0], far, middle_grad, gain_one, *inputs, *qkv_ops)
        slots.note(own_grad)
        slots.advance()

        bias_sum = jnp.concatenate([near_own, far_own], axis=2)[::2].reshape(2, nrow, part, ncore, nz, piece)
        bias_sum = jnp.transpose(bias_sum, (3, 1, 4, 0, 2, 5)).reshape(ncore, nrow, nz, qkv_count)
        bias_sum = jnp.concatenate([bias_sum, up_bias_sum.reshape(ncore, nrow, nz, hidden_part)], axis=-1)
        sums = jnp.concatenate([sums_one, sums_two])
        size = sums.shape[0] * width
        flat_bias = bias_sum.reshape(-1)
        packs = [jnp.concatenate([sums[:, :width].reshape(-1), flat_bias])]

        def small_sums():
            (pack,) = slots.gate(packs[0])
            for k in range(1, ncol):
                far_part = sums[:, k * width : (k + 1) * width].reshape(-1)
                pack = pack + slots.send(jnp.concatenate([far_part, flat_bias]), "col", k)
            for axis in ("core", "row", "z"):
                for bit in reversed(bits(axis)):
                    rest = pack[size:]
                    half = rest.size // 2
                    got = slots.move(jnp.concatenate([pack[:size], rest[half:]]), axis, bit)
                    pack = pack[: size + half] + got
            packs[0] = pack

        token_grad = TokensOut("token_grad", slots, own_grad, other_grad)
        with jax.named_scope("small_sums"):
            small_sums()
        qg.low = qg.low + [far_low.got_low]
        if nrow > 2:
            slots.together((qg, "x_low"))
        slots.together((qg, "z_high"), (og, "z_low"))
        do(token_grad, "send")
        up_grad = ug.result()
        slots.note(up_grad)
        slots.advance()

        slots.together((qg, "z_low"))
        token_grad = token_grad.end(spaces[1])
        out_grad, qkv_grad = og.result(), qg.result()

        pack = packs[0]
        sums = pack[:size].reshape(-1, width)
        bias_sum = pack[size:]
        return (
            activations,
            token_grad,
            sums[0],
            sums[1],
            qkv_grad,
            bias_sum[:qkv_count].reshape(qkv_bias.shape),
            out_grad[0],
            sums[2],
            sums[3],
            sums[4],
            up_grad,
            bias_sum[qkv_count:],
            down_grad,
            sums[5],
        )

    return local


def solution(mesh):
    devices = mesh.devices
    nz, ncore = devices.shape[0] // 2, 2
    nrow, ncol = devices.shape[1], devices.shape[2]
    fine = Mesh(devices.reshape(nz, ncore, nrow, ncol), ("z", "core", "row", "col"))
    dp = ("z", "core")
    rows = P(("z", "core", "row"), "col")
    qkv_weight = P(None, "row", dp, "col")
    qkv_bias = P(None, "row", dp)
    out_weight = P("row", dp, "col")
    feature = P("col")
    unit = P(("z", "core", "row"))
    in_specs = (
        rows,
        P(("z", "core", "col"), None),
        feature,
        feature,
        qkv_weight,
        qkv_bias,
        out_weight,
        feature,
        feature,
        feature,
        rows,
        unit,
        rows,
        feature,
        rows,
    )
    out_specs = (
        rows,
        rows,
        feature,
        feature,
        qkv_weight,
        qkv_bias,
        out_weight,
        feature,
        feature,
        feature,
        rows,
        unit,
        rows,
        feature,
    )
    return jax.shard_map(
        make_local(nz, ncore, nrow, ncol),
        mesh=fine,
        in_specs=in_specs,
        out_specs=out_specs,
        check_vma=False,
    )
```
